32 devices in a mesh: dp: 16 (over z, x, core), band: 2 (over y).
Axes of the slice: x: 2, y: 2, z: 4, core: 2. Of those that a mesh axis runs over, the one named last changes fastest.
Arguments:
- block_input: bfloat16 [16, 5, 32, 16, 1024], P('dp', None, 'band'), may hold values from -6 to 6
- modulation: float32 [16, 6, 1024], P('dp'), may hold values from -2 to 2
- band_live: int32 [16, 2], P('dp'), may hold values 0 or 1
- w_query: bfloat16 [1024, 1024], replicated, may hold values from -0.25 to 0.25
- w_key: bfloat16 [1024, 1024], replicated, may hold values from -0.25 to 0.25
- w_value: bfloat16 [1024, 1024], replicated, may hold values from -0.1875 to 0.1875
- w_out: bfloat16 [1024, 1024], replicated, may hold values from -0.5 to 0.5
- w_up: bfloat16 [1024, 4096], replicated, may hold values from -0.1875 to 0.1875
- w_down: bfloat16 [4096, 1024], replicated, may hold values from -0.09375 to 0.09375
- cotangent: bfloat16 [16, 5, 32, 16, 1024], P('dp', None, 'band'), may hold values from -6 to 6
Outputs:
- block_output: bfloat16 [16, 5, 32, 16, 1024], P('dp', None, 'band')
- grad_input: bfloat16 [16, 5, 32, 16, 1024], P('dp', None, 'band')
- grad_modulation: float32 [16, 6, 1024], P('dp')
- grad_w_query: float32 [1048576], P('dp')
- grad_w_key: float32 [1048576], P('dp')
- grad_w_value: float32 [1048576], P('dp')
- grad_w_out: float32 [1048576], P('dp')
- grad_w_up: float32 [4194304], P('dp')
- grad_w_down: float32 [4194304], P('dp')
The draws below stay inside these ranges and needn't reach their ends.
Inputs may be any that keep to these rules, and one draw needn't show every extreme that they name: band_live[c, b] is 1 where band b of clip c holds latent rows and 0 where that band slot is empty; an empty band's tokens pass the block unchanged.
All inputs are finite; a program needn't handle non-finite values.
Results may differ from the reference program's by a relative error of at most 0.015.
The reference program's roundings to bfloat16 on the way count: a program that leaves them out, or rounds other values in their place, can miss the bound.
Values may be sent and summed in bfloat16 or wider, within the bound.
A program may use at most 384 MiB of HBM per device.

```python
import jax
import jax.numpy as jnp
from jax import lax

D = 1024
HEADS = 16
FF = 4096
HEAD_DIM = 64
FRAMES = 5
BAND_ROWS = 16
COLS = 16
HEIGHT = 32
CLIPS = 16
N_BAND = 2


def set_ends(values, key, low, largest):
    place = [jax.random.randint(jax.random.fold_in(key, axis), (), 0, length) for axis, length in enumerate(values.shape)]
    longest = values.shape.index(max(values.shape))
    beside = place[:longest] + [(place[longest] + 1) % values.shape[longest]] + place[longest + 1:]
    return values.at[tuple(place)].set(low).at[tuple(beside)].set(largest)


def block_levels(stream_key, shape, split, low, high):
    def one(axis_at, parts):
        steps = jax.random.uniform(jax.random.fold_in(jax.random.fold_in(stream_key, 6), axis_at), (parts,), jnp.float32, low / len(split), high / len(split))
        return jnp.repeat(jnp.exp(steps), shape[axis_at] // parts).reshape((-1,) + (1,) * (len(shape) - axis_at - 1))

    gain = one(*split[0])
    for cut in split[1:]:
        gain = gain * one(*cut)
    return gain


def noise(stream_key, shape, width, bound, shards=(), kind=jnp.bfloat16):
    values = jax.random.normal(stream_key, shape, jnp.float32) * width
    if len(shards) > 0:
        values = block_levels(stream_key, shape, shards, -0.22, 0.18) * values
    return jnp.clip(values, min=-bound, max=bound).astype(kind)


def setup_inputs(seed: int = 0) -> dict:
    arg_keys = jax.random.split(jax.random.key(seed), 11)
    block_input = noise(arg_keys[0], (CLIPS, FRAMES, HEIGHT, COLS, D), 1.0, 6.0, ((0, 16), (2, 2)))
    modulation = noise(arg_keys[1], (CLIPS, 6, D), 0.5, 2.0, ((0, 16),), jnp.float32)
    band_live = set_ends((jax.random.randint(arg_keys[2], (CLIPS, N_BAND), 0, 4) < 3).astype(jnp.int32), jax.random.fold_in(arg_keys[2], 1), 0, 1)
    w_query = noise(arg_keys[3], (D, D), (D // 2) ** -0.5, 0.25)
    w_key = noise(arg_keys[4], (D, D), (D // 2) ** -0.5, 0.25)
    w_value = noise(arg_keys[5], (D, D), D ** -0.5, 0.1875)
    w_out = noise(arg_keys[6], (D, D), (D // 8) ** -0.5, 0.5)
    w_up = noise(arg_keys[7], (D, FF), D ** -0.5, 0.1875)
    w_down = noise(arg_keys[8], (FF, D), FF ** -0.5, 0.09375)
    cotangent = noise(arg_keys[9], (CLIPS, FRAMES, HEIGHT, COLS, D), 1.0, 6.0, ((0, 16), (2, 2)))
    return dict(block_input=block_input, modulation=modulation, band_live=band_live, w_query=w_query, w_key=w_key, w_value=w_value, w_out=w_out, w_up=w_up, w_down=w_down, cotangent=cotangent)


@jax.custom_vjp
def low(v):
    return lax.optimization_barrier(v.astype(jnp.bfloat16)).astype(jnp.float32)

@jax.custom_vjp
def low_back(v):
    return v

def low_keep(v):
    return (low(v), None)

def low_pass(kept, grad):
    return (grad,)

def back_keep(v):
    return (v, None)

def back_low(kept, grad):
    return (low(grad),)
low.defvjp(low_keep, low_pass)
low_back.defvjp(back_keep, back_low)
epsilon = 1e-06
masked_score = -1e+30
highest = lax.Precision.HIGHEST

def layer_norm(values):
    centred = values - lax.optimization_barrier(jnp.mean(values, axis=-1, keepdims=True))
    spread = lax.optimization_barrier(jnp.mean(centred * centred, axis=-1, keepdims=True))
    return centred * lax.rsqrt(spread + epsilon)

def product(left, right):
    return jnp.dot(left, right, precision=highest)

def to_windows(field_in):
    frame_count, row_count, col_count, model_width = field_in.shape
    blocks = field_in.reshape(frame_count, row_count // 8, 8, col_count // 8, 8, model_width)
    blocks = blocks.transpose(1, 3, 0, 2, 4, 5)
    return blocks.reshape(row_count // 8 * (col_count // 8), frame_count * 64, model_width)

def from_windows(windows, frame_count, row_count, col_count):
    model_width = windows.shape[-1]
    blocks = windows.reshape(row_count // 8, col_count // 8, frame_count, 8, 8, model_width)
    blocks = blocks.transpose(2, 0, 3, 1, 4, 5)
    return blocks.reshape(frame_count, row_count, col_count, model_width)

def clip_forward(inputs, modulation, live_rows, w_query, w_key, w_value, w_out, w_up, w_down):
    frame_count, row_count, col_count, model_width = inputs.shape
    flat_in = inputs.reshape(-1, model_width)
    live_field = jnp.broadcast_to(live_rows[None, :, None], (frame_count, row_count, col_count))
    live_gate = live_field.reshape(-1, 1).astype(jnp.float32)
    normed = low(layer_norm(flat_in) * (1.0 + modulation[1]) + modulation[0])
    query_rows = low(low_back(product(normed, w_query)))
    key_rows = low(low_back(product(normed, w_key)))
    value_rows = low(low_back(product(normed, w_value)))
    padding = ((0, 0), (4, 4), (0, 0), (0, 0))

    def windowed(flat_rows):
        field_in = jnp.pad(flat_rows.reshape(frame_count, row_count, col_count, model_width), padding)
        windows = to_windows(field_in)
        return windows.reshape(windows.shape[0], windows.shape[1], HEADS, HEAD_DIM)
    win_query = windowed(query_rows)
    win_key = windowed(key_rows)
    win_value = windowed(value_rows)
    in_grid = jnp.pad(jnp.ones((row_count,), jnp.bool_), 4)
    live_pad = jnp.pad(live_rows, 4)

    def row_windows(row_flags):
        field_in = jnp.broadcast_to(row_flags[None, :, None, None], (frame_count, row_count + 8, col_count, 1))
        return to_windows(field_in)[:, :, 0]
    grid_win = row_windows(in_grid)
    live_win = row_windows(live_pad)
    allowed = grid_win[:, None, :] & (live_win[:, None, :] | jnp.logical_not(live_win[:, :, None]))
    scores = jnp.einsum('wqhd,wkhd->whqk', win_query, win_key, precision=highest) * HEAD_DIM ** (-0.5)
    scores = low_back(scores)
    scores = jnp.where(allowed[:, None], scores, masked_score)
    attention = low(jax.nn.softmax(scores, axis=-1))
    blended = jnp.einsum('whqk,wkhd->wqhd', attention, win_value, precision=highest)
    blended = blended.reshape(blended.shape[0], blended.shape[1], model_width)
    attended = from_windows(blended, frame_count, row_count + 8, col_count)[:, 4:4 + row_count]
    attended = low(low_back(attended.reshape(-1, model_width)))
    attn_out = low_back(product(attended, w_out))
    middle = flat_in + live_gate * modulation[2] * attn_out
    normed_mid = low(layer_norm(middle) * (1.0 + modulation[4]) + modulation[3])
    pre_act = low_back(product(normed_mid, w_up))
    hidden = low(jax.nn.gelu(pre_act))
    mlp_out = low_back(product(hidden, w_down))
    result = middle + live_gate * modulation[5] * mlp_out
    return result.reshape(frame_count, row_count, col_count, model_width)

def reference(block_input, modulation, band_live, w_query, w_key, w_value, w_out, w_up, w_down, cotangent):
    matrices = (w_query.astype(jnp.float32), w_key.astype(jnp.float32), w_value.astype(jnp.float32), w_out.astype(jnp.float32), w_up.astype(jnp.float32), w_down.astype(jnp.float32))
    live_bands = band_live == 1

    def one_clip(grad_sums, pieces):
        clip_in, clip_mod, clip_live, clip_cot = pieces
        live_rows = jnp.repeat(clip_live, BAND_ROWS)

        def forward(inputs, modulation_in, m_query, m_key, m_value, m_out, m_up, m_down):
            return clip_forward(inputs, modulation_in, live_rows, m_query, m_key, m_value, m_out, m_up, m_down)
        result, pullback = jax.vjp(forward, clip_in.astype(jnp.float32), clip_mod, matrices[0], matrices[1], matrices[2], matrices[3], matrices[4], matrices[5])
        gradients = pullback(clip_cot.astype(jnp.float32))
        grad_sums = tuple((running + added for running, added in zip(grad_sums, gradients[2:])))
        return (grad_sums, (result.astype(jnp.bfloat16), gradients[0].astype(jnp.bfloat16), gradients[1]))
    zero_sums = tuple((jnp.zeros(matrix.shape, jnp.float32) for matrix in matrices))
    grad_sums, (outputs, input_grads, mod_grads) = lax.scan(one_clip, zero_sums, (block_input, modulation, live_bands, cotangent))
    return (outputs, input_grads, mod_grads, grad_sums[0].reshape(-1), grad_sums[1].reshape(-1), grad_sums[2].reshape(-1), grad_sums[3].reshape(-1), grad_sums[4].reshape(-1), grad_sums[5].reshape(-1))
```

```python
import functools

import jax
import jax.numpy as jnp
from jax import lax
from jax.experimental import pallas as pl
from jax.experimental.pallas import tpu as pltpu
from jax.sharding import PartitionSpec as P

HEADS = 16
HEAD_DIM = 64
EPS = 1e-06
MASKED = -1e30
LOG2E = 1.4426950408889634
F32 = jnp.float32
BF16 = jnp.bfloat16
ANY = pl.BlockSpec(memory_space=pl.ANY)
VMEM_LIMIT = 60 * 1024 * 1024

MID_SPOTS = ((1, 0), (2, 0), (1, 1), (2, 1))


def group_spot(band, s):
    lone = 3 * band
    paired = 3 - 3 * band
    if s < 2:
        return lone, s
    if s < 6:
        return MID_SPOTS[s - 2]
    return paired, s - 6


def params(**kw):
    return pltpu.CompilerParams(vmem_limit_bytes=VMEM_LIMIT, **kw)


def dot(a, b, ca=1, cb=0):
    return lax.dot_general(a, b, (((ca,), (cb,)), ((), ())), preferred_element_type=F32)


def whole(shape):
    return pl.BlockSpec(shape, lambda *_: (0,) * len(shape), pipeline_mode=pl.Buffered(1))


def norm_stats(v):
    c = v - jnp.mean(v, axis=-1, keepdims=True)
    r = lax.rsqrt(jnp.mean(c * c, axis=-1, keepdims=True) + EPS)
    return c * r, r


def spot_copy(hbm, vmem, band, s, sem, out=False):
    g, j = group_spot(band, s)
    there = hbm.at[0, :, pl.ds(g * 4, 4), pl.ds(j * 8, 8), :]
    if out:
        return pltpu.make_async_copy(vmem.at[s], there, sem.at[s])
    return pltpu.make_async_copy(there, vmem.at[s], sem.at[s])


def pre_kernel(n_group, from_spots, x_hbm, mod_ref, *refs):
    n_mat = (len(refs) - 5) // 2 if from_spots else (len(refs) - 3) // 2
    w_refs = refs[:n_mat]
    outs = refs[n_mat:]
    if from_spots:
        xw_ref, normed_ref = outs[:2]
        o_refs = outs[2 : 2 + n_mat]
    else:
        o_refs = outs[:n_mat]
    stage, sem, nsc = outs[-3:] if not from_spots else outs[-3:]
    rows = nsc.shape[0] // n_group

    @pl.when(pl.program_id(0) == 0)
    def _():
        band = lax.axis_index("band")
        if from_spots:
            copies = [spot_copy(x_hbm, stage, band, s, sem) for s in range(n_group)]
        else:
            copies = [
                pltpu.make_async_copy(x_hbm.at[:, :, pl.ds(8 * s, 8), :], stage.at[s], sem.at[s])
                for s in range(n_group)
            ]
        for c in copies:
            c.start()
        for s in range(n_group):
            copies[s].wait()
            x = stage[s].astype(F32).reshape(rows, stage.shape[-1])
            n, _ = norm_stats(x)
            part = pl.ds(s * rows, rows)
            nsc[part, :] = (n * (1.0 + mod_ref[1:2, :]) + mod_ref[0:1, :]).astype(BF16)
            if from_spots:
                xw_ref[part, :] = x.astype(BF16)
                normed_ref[part, :] = nsc[part, :]

    for w_ref, o_ref in zip(w_refs, o_refs):
        o_ref[...] = dot(nsc[...], w_ref[...]).astype(BF16)


def pre(x, mod, weights, n_group, from_spots):
    d = x.shape[-1]
    frames = x.shape[1] if from_spots else x.shape[0]
    rows = frames * 32
    t = n_group * rows
    tile = 256
    o_tile = pl.BlockSpec((t, tile), lambda n: (0, n))
    full = pl.BlockSpec((t, d), lambda n: (0, 0))
    act = jax.ShapeDtypeStruct((t, d), BF16)
    k = len(weights)
    head = [act, act] if from_spots else []
    return pl.pallas_call(
        functools.partial(pre_kernel, n_group, from_spots),
        grid=(d // tile,),
        in_specs=[ANY, whole((6, d))] + [pl.BlockSpec((d, tile), lambda n: (0, n))] * k,
        out_specs=[full] * len(head) + [o_tile] * k,
        out_shape=head + [act] * k,
        scratch_shapes=[
            pltpu.VMEM((n_group, frames, 4, 8, d), BF16),
            pltpu.SemaphoreType.DMA((n_group,)),
            pltpu.VMEM((t, d), BF16),
        ],
        compiler_params=params(),
        name="pre" if from_spots else "pre_halo",
        cost_estimate=pl.CostEstimate(
            flops=2 * t * d * d * k, bytes_accessed=2 * (k * d * d + (k + 3) * t * d), transcendentals=0
        ),
    )(x, mod, *weights)


def units(rows):
    r = rows
    out = [((0, r), (0, r), None), ((r, r), (r, r), None)]
    out += [((2 * r, 2 * r), (2 * r, 2 * r), None), ((4 * r, 2 * r), (4 * r, 2 * r), None)]
    out += [((6 * r, r), (6 * r, r), (0, r)), ((7 * r, r), (7 * r, r), (r, r))]
    return out


SCALE2 = HEAD_DIM**-0.5 * LOG2E


def attn_fwd_kernel(ok_ref, q_ref, k_ref, v_ref, kh_ref, vh_ref, o_ref, lse_ref):
    r = q_ref.shape[0] // 8
    halo_ok = ok_ref[0] == 1
    for h in range(2):
        lanes = slice(64 * h, 64 * h + 64)
        for (q0, qn), (k0, kn), halo in units(r):
            q = q_ref[q0 : q0 + qn, lanes]
            k = k_ref[k0 : k0 + kn, lanes]
            v = v_ref[k0 : k0 + kn, lanes]
            s = dot(q, k, 1, 1) * SCALE2
            top = jnp.max(s, axis=-1, keepdims=True)
            if halo is not None:
                kh = kh_ref[halo[0] : halo[0] + halo[1], lanes]
                vh = vh_ref[halo[0] : halo[0] + halo[1], lanes]
                sh = jnp.where(halo_ok, dot(q, kh, 1, 1) * SCALE2, MASKED)
                top = jnp.maximum(top, jnp.max(sh, axis=-1, keepdims=True))
            e = jnp.exp2(s - top)
            total = jnp.sum(e, axis=-1, keepdims=True)
            o = dot(e.astype(BF16), v)
            if halo is not None:
                eh = jnp.exp2(sh - top)
                total = total + jnp.sum(eh, axis=-1, keepdims=True)
                o = o + dot(eh.astype(BF16), vh)
            o_ref[q0 : q0 + qn, lanes] = (o * (1.0 / total)).astype(BF16)
            lse_ref[q0 : q0 + qn, lanes] = jnp.broadcast_to(top + jnp.log2(total), (qn, 64))


def attn_fwd(halo_ok, q, k, v, kh, vh):
    t, d = q.shape
    th = kh.shape[0]
    big = pl.BlockSpec((t, 128), lambda n: (0, n))
    small = pl.BlockSpec((th, 128), lambda n: (0, n))
    pairs = t * t // 8 * 2 * 7 // 8
    return pl.pallas_call(
        attn_fwd_kernel,
        grid=(d // 128,),
        in_specs=[pl.BlockSpec(memory_space=pltpu.SMEM), big, big, big, small, small],
        out_specs=[big, big],
        out_shape=[jax.ShapeDtypeStruct((t, d), BF16), jax.ShapeDtypeStruct((t, d), F32)],
        compiler_params=params(),
        name="attn_fwd",
        cost_estimate=pl.CostEstimate(
            flops=4 * pairs * d * 4, bytes_accessed=12 * t * d, transcendentals=pairs * 16
        ),
    )(halo_ok, q, k, v, kh, vh)


def attn_bwd_kernel(which, ok_ref, q_ref, k_ref, v_ref, do_ref, lse_ref, *refs):
    base = 0
    if which == "paired":
        kh_ref, vh_ref, dq_ref, dk_ref, dv_ref, out_ref = refs
        r = q_ref.shape[0] // 2
        base = 6 * r
        todo = units(r)[4:]
        halo_ok = ok_ref[0] == 1
    else:
        dq_ref, dk_ref, dv_ref = refs
        r = q_ref.shape[0] // 6
        todo = units(r)[:4]
    scale = HEAD_DIM**-0.5
    for h in range(2):
        lanes = slice(64 * h, 64 * h + 64)
        for (q0, qn), (k0, kn), halo in todo:
            qs, ks = slice(q0 - base, q0 - base + qn), slice(k0 - base, k0 - base + kn)
            q, k, v = q_ref[qs, lanes], k_ref[ks, lanes], v_ref[ks, lanes]
            do = do_ref[qs, lanes]
            lse = lse_ref[qs, 64 * h : 64 * h + 1]
            p = jnp.exp2(dot(q, k, 1, 1) * SCALE2 - lse)
            dp = dot(do, v, 1, 1)
            row = jnp.sum(p * dp, axis=-1, keepdims=True)
            if halo is not None:
                hs = slice(halo[0], halo[0] + halo[1])
                kh, vh = kh_ref[hs, lanes], vh_ref[hs, lanes]
                sh = jnp.where(halo_ok, dot(q, kh, 1, 1) * SCALE2, MASKED)
                ph = jnp.exp2(sh - lse)
                dph = dot(do, vh, 1, 1)
                row = row + jnp.sum(ph * dph, axis=-1, keepdims=True)
            ds = (p * (dp - row)).astype(BF16)
            dq = dot(ds, k)
            dk = dot(ds, q, 0, 0) * scale
            dv = dot(p.astype(BF16), do, 0, 0)
            if halo is not None:
                dsh = (ph * (dph - row)).astype(BF16)
                dq = dq + dot(dsh, kh)
                out_ref[0, hs, lanes] = (dot(dsh, q, 0, 0) * scale).astype(BF16)
                out_ref[1, hs, lanes] = dot(ph.astype(BF16), do, 0, 0).astype(BF16)
            dq_ref[qs, lanes] = (dq * scale).astype(dq_ref.dtype)
            dk_ref[ks, lanes] = dk.astype(dk_ref.dtype)
            dv_ref[ks, lanes] = dv.astype(dv_ref.dtype)


def attn_bwd_main(halo_ok, q, k, v, do, lse):
    t, d = q.shape
    part = t // 8 * 6
    big = pl.BlockSpec((part, 128), lambda n: (0, n))
    act = jax.ShapeDtypeStruct((t, d), BF16)
    pairs = t * t // 64 * 10
    return pl.pallas_call(
        functools.partial(attn_bwd_kernel, "main"),
        grid=(d // 128,),
        in_specs=[pl.BlockSpec(memory_space=pltpu.SMEM)] + [big] * 5,
        out_specs=[big] * 3,
        out_shape=[jax.ShapeDtypeStruct((part, d), BF16)] * 3,
        compiler_params=params(),
        name="attn_bwd_main",
        cost_estimate=pl.CostEstimate(
            flops=10 * pairs * d * 4, bytes_accessed=18 * t * d, transcendentals=pairs * 16
        ),
    )(halo_ok, q, k, v, do, lse)


def attn_bwd_paired(halo_ok, q, k, v, do, lse, kh, vh):
    t, d = q.shape
    part = t // 4
    big = pl.BlockSpec((part, 128), lambda n: (3, n))
    small = pl.BlockSpec((part, 128), lambda n: (0, n))
    f32 = jax.ShapeDtypeStruct((part, d), F32)
    pairs = t * t // 64 * 4
    return pl.pallas_call(
        functools.partial(attn_bwd_kernel, "paired"),
        grid=(d // 128,),
        in_specs=[pl.BlockSpec(memory_space=pltpu.SMEM)] + [big] * 5 + [small] * 2,
        out_specs=[small] * 3 + [pl.BlockSpec((2, part, 128), lambda n: (0, 0, n))],
        out_shape=[jax.ShapeDtypeStruct((part, d), BF16), f32, f32, jax.ShapeDtypeStruct((2, part, d), BF16)],
        compiler_params=params(),
        name="attn_bwd_paired",
        cost_estimate=pl.CostEstimate(
            flops=10 * pairs * d * 4, bytes_accessed=12 * t * d, transcendentals=pairs * 16
        ),
    )(halo_ok, q, k, v, do, lse, kh, vh)


def mid_kernel(g_hbm, live_ref, att_ref, w_ref, x_ref, mod_ref, ao_ref, mid_ref, nm_ref, gw_ref, gm_ref, stage, sem):
    step = pl.program_id(0)
    band = lax.axis_index("band")
    live = live_ref[0].astype(F32)
    n_group = stage.shape[0]
    per = n_group // 4
    rows = gw_ref.shape[0] // per

    @pl.when(step == 0)
    def _():
        for s in range(n_group):
            spot_copy(g_hbm, stage, band, s, sem).start()

    attn_out = dot(att_ref[...], w_ref[...])
    middle = x_ref[...].astype(F32) + (live * mod_ref[2:3, :]) * attn_out
    ao_ref[...] = attn_out
    mid_ref[...] = middle
    n, _ = norm_stats(middle)
    nm_ref[...] = (n * (1.0 + mod_ref[4:5, :]) + mod_ref[3:4, :]).astype(BF16)
    for i in range(per):
        s = step * per + i
        pltpu.make_async_copy(g_hbm.at[0, :, pl.ds(0, 4), pl.ds(0, 8), :], stage.at[s], sem.at[s]).wait()
        g = stage[s].astype(F32).reshape(rows, stage.shape[-1])
        part = pl.ds(i * rows, rows)
        gw_ref[part, :] = g.astype(BF16)
        gm_ref[part, :] = ((live * mod_ref[5:6, :]) * g).astype(BF16)


def mid(cot, live, attended, w_out, xw, mod):
    t, d = xw.shape
    frames = cot.shape[1]
    blk = pl.BlockSpec((t // 4, d), lambda m: (m, 0))
    bf, f32 = jax.ShapeDtypeStruct((t, d), BF16), jax.ShapeDtypeStruct((t, d), F32)
    return pl.pallas_call(
        mid_kernel,
        grid=(4,),
        in_specs=[ANY, pl.BlockSpec(memory_space=pltpu.SMEM), blk, whole((d, d)), blk, whole((6, d))],
        out_specs=[blk] * 5,
        out_shape=[f32, f32, bf, bf, bf],
        scratch_shapes=[pltpu.VMEM((8, frames, 4, 8, d), BF16), pltpu.SemaphoreType.DMA((8,))],
        compiler_params=params(),
        name="mid",
        cost_estimate=pl.CostEstimate(flops=2 * t * d * d, bytes_accessed=22 * t * d, transcendentals=0),
    )(cot, live, attended, w_out, xw, mod)


GELU_C = 0.7978845608
GELU_A = 0.044715


def mlp_kernel(nm_ref, gm_ref, wu_ref, wd_ref, mo_ref, h_ref, dwu_ref, dwd_ref, hid, gp):
    first = pl.program_id(0) == 0
    t = nm_ref.shape[0]
    chunk = t // 4

    @pl.when(first)
    def _():
        mo_ref[...] = jnp.zeros_like(mo_ref)
        h_ref[...] = jnp.zeros_like(h_ref)

    def rows(i, _):
        part = pl.ds(pl.multiple_of(i * chunk, chunk), chunk)
        nm, gm = nm_ref[part, :], gm_ref[part, :]
        v = dot(nm, wu_ref[...])
        gh = dot(gm, wd_ref[...], 1, 1)
        v2 = v * v
        th = jnp.tanh(v * (GELU_C + (GELU_C * GELU_A) * v2))
        half = 0.5 * th + 0.5
        hidden = (v * half).astype(BF16)
        slope = half + (0.5 * v) * (1.0 - th * th) * (GELU_C + (3.0 * GELU_C * GELU_A) * v2)
        gpre = (gh * slope).astype(BF16)
        hid[part, :] = hidden
        gp[part, :] = gpre
        mo_ref[part, :] += dot(hidden, wd_ref[...])
        h_ref[part, :] += dot(gpre, wu_ref[...], 1, 1)
        return 0

    lax.fori_loop(0, 4, rows, 0)
    dwd_ref[...] = dot(hid[...], gm_ref[...], 0, 0).astype(BF16)
    dwu_ref[...] = dot(nm_ref[...], gp[...], 0, 0).astype(BF16)


def mlp(nm, gm, w_up, w_down):
    t, d = nm.shape
    ff = w_up.shape[1]
    tile = 512
    f32 = jax.ShapeDtypeStruct((t, d), F32)
    return pl.pallas_call(
        mlp_kernel,
        grid=(ff // tile,),
        in_specs=[
            whole((t, d)),
            whole((t, d)),
            pl.BlockSpec((d, tile), lambda f: (0, f)),
            pl.BlockSpec((tile, d), lambda f: (f, 0)),
        ],
        out_specs=[
            whole((t, d)),
            whole((t, d)),
            pl.BlockSpec((d, tile), lambda f: (0, f)),
            pl.BlockSpec((tile, d), lambda f: (f, 0)),
        ],
        out_shape=[f32, f32, jax.ShapeDtypeStruct((d, ff), BF16), jax.ShapeDtypeStruct((ff, d), BF16)],
        scratch_shapes=[pltpu.VMEM((t, tile), BF16), pltpu.VMEM((t, tile), BF16)],
        compiler_params=params(),
        name="mlp",
        cost_estimate=pl.CostEstimate(flops=12 * t * d * ff, bytes_accessed=8 * d * ff + 12 * t * d, transcendentals=t * ff),
    )(nm, gm, w_up, w_down)


def post_kernel(live_ref, mid_ref, mo_ref, h_ref, g_ref, ao_ref, mod_ref, w_ref, out_hbm, gmid_ref, ga_ref, do_ref, sums_ref, stage, sem):
    step = pl.program_id(0)
    band = lax.axis_index("band")
    live = live_ref[0].astype(F32)
    n_group = stage.shape[0]
    per = n_group // 4
    middle = mid_ref[...]
    g = g_ref[...].astype(F32)
    mo = mo_ref[...]
    h = h_ref[...]
    out = middle + (live * mod_ref[5:6, :]) * mo
    n, r = norm_stats(middle)
    e = h * (1.0 + mod_ref[4:5, :])
    gmid = g + r * (e - jnp.mean(e, axis=-1, keepdims=True) - n * jnp.mean(e * n, axis=-1, keepdims=True))
    gmid_ref[...] = gmid
    ga = ((live * mod_ref[2:3, :]) * gmid).astype(BF16)
    ga_ref[...] = ga
    do_ref[...] = dot(ga, w_ref[...], 1, 1).astype(BF16)

    def col(v):
        return jnp.sum(v, axis=0, keepdims=True)

    sums = jnp.concatenate(
        [col(live * ao_ref[...] * gmid), col(h), col(h * n), col(live * mo * g), jnp.zeros((4, h.shape[1]), F32)], axis=0
    )

    @pl.when(step == 0)
    def _():
        sums_ref[...] = sums

    @pl.when(step > 0)
    def _():
        sums_ref[...] += sums

    rows = h.shape[0] // per
    shape = stage.shape[1:]
    for k in range(4):

        @pl.when(step == k)
        def _():
            for i in range(per):
                s = k * per + i
                stage[s] = out[i * rows : (i + 1) * rows, :].reshape(shape).astype(BF16)
                spot_copy(out_hbm, stage, band, s, sem, out=True).start()

    @pl.when(step == 3)
    def _():
        for s in range(n_group):
            spot_copy(out_hbm, stage, band, s, sem, out=True).wait()


def post(live, middle, mo, h, gw, ao, mod, w_out, like):
    t, d = gw.shape
    frames = like.shape[1]
    blk = pl.BlockSpec((t // 4, d), lambda m: (m, 0))
    bf, f32 = jax.ShapeDtypeStruct((t, d), BF16), jax.ShapeDtypeStruct((t, d), F32)
    return pl.pallas_call(
        post_kernel,
        grid=(4,),
        in_specs=[pl.BlockSpec(memory_space=pltpu.SMEM), blk, blk, blk, blk, blk, whole((6, d)), whole((d, d))],
        out_specs=[ANY, blk, blk, blk, pl.BlockSpec((8, d), lambda m: (0, 0))],
        out_shape=[jax.ShapeDtypeStruct(like.shape, BF16), f32, bf, bf, jax.ShapeDtypeStruct((8, d), F32)],
        scratch_shapes=[pltpu.VMEM((8, frames, 4, 8, d), BF16), pltpu.SemaphoreType.DMA((8,))],
        compiler_params=params(),
        name="post",
        cost_estimate=pl.CostEstimate(flops=2 * t * d * d, bytes_accessed=30 * t * d, transcendentals=0),
    )(live, middle, mo, h, gw, ao, mod, w_out)


def outer_kernel(a_ref, b_ref, o_ref):
    o_ref[...] = dot(a_ref[...], b_ref[...], 0, 0).astype(BF16)


def outer(a, b):
    t, d = a.shape
    tile = 512
    return pl.pallas_call(
        outer_kernel,
        grid=(b.shape[1] // tile,),
        in_specs=[whole((t, d)), pl.BlockSpec((t, tile), lambda n: (0, n))],
        out_specs=pl.BlockSpec((d, tile), lambda n: (0, n)),
        out_shape=jax.ShapeDtypeStruct((d, b.shape[1]), BF16),
        compiler_params=params(),
        name="outer",
        cost_estimate=pl.CostEstimate(flops=2 * t * d * b.shape[1], bytes_accessed=6 * t * d, transcendentals=0),
    )(a, b)


def final_kernel(dq_ref, dk_ref, dv_ref, wq_ref, wk_ref, wv_ref, x_ref, gmid_ref, mod_ref, out_hbm, sums_ref, stage, sem):
    step = pl.program_id(0)
    band = lax.axis_index("band")
    n_group = stage.shape[0]
    per = n_group // 4
    h = dot(dq_ref[...], wq_ref[...], 1, 1) + dot(dk_ref[...], wk_ref[...], 1, 1) + dot(dv_ref[...], wv_ref[...], 1, 1)
    n, r = norm_stats(x_ref[...].astype(F32))
    e = h * (1.0 + mod_ref[1:2, :])
    out = gmid_ref[...] + r * (e - jnp.mean(e, axis=-1, keepdims=True) - n * jnp.mean(e * n, axis=-1, keepdims=True))

    def col(v):
        return jnp.sum(v, axis=0, keepdims=True)

    sums = jnp.concatenate([col(h), col(h * n), jnp.zeros((6, h.shape[1]), F32)], axis=0)

    @pl.when(step == 0)
    def _():
        sums_ref[...] = sums

    @pl.when(step > 0)
    def _():
        sums_ref[...] += sums

    rows = h.shape[0] // per
    shape = stage.shape[1:]
    for k in range(4):

        @pl.when(step == k)
        def _():
            for i in range(per):
                s = k * per + i
                stage[s] = out[i * rows : (i + 1) * rows, :].reshape(shape).astype(BF16)
                spot_copy(out_hbm, stage, band, s, sem, out=True).start()

    @pl.when(step == 3)
    def _():
        for s in range(n_group):
            spot_copy(out_hbm, stage, band, s, sem, out=True).wait()


def final(dq, dk, dv, wq, wk, wv, xw, gmid, mod, like):
    t, d = xw.shape
    frames = like.shape[1]
    blk = pl.BlockSpec((t // 4, d), lambda m: (m, 0))
    return pl.pallas_call(
        final_kernel,
        grid=(4,),
        in_specs=[blk, blk, blk, whole((d, d)), whole((d, d)), whole((d, d)), blk, blk, whole((6, d))],
        out_specs=[ANY, pl.BlockSpec((8, d), lambda m: (0, 0))],
        out_shape=[jax.ShapeDtypeStruct(like.shape, BF16), jax.ShapeDtypeStruct((8, d), F32)],
        scratch_shapes=[pltpu.VMEM((8, frames, 4, 8, d), BF16), pltpu.SemaphoreType.DMA((8,))],
        compiler_params=params(),
        name="final",
        cost_estimate=pl.CostEstimate(flops=6 * t * d * d, bytes_accessed=14 * t * d, transcendentals=0),
    )(dq, dk, dv, wq, wk, wv, xw, gmid, mod)


def band_swap(v):
    return lax.ppermute(v, "band", [(0, 1), (1, 0)])


def reduced(grad):
    share = lax.psum_scatter(grad, "dp", scatter_dimension=0, tiled=True)
    return (share.astype(F32) + band_swap(share).astype(F32)).reshape(-1)


def on_device(
    block_input, modulation, band_live, w_query, w_key, w_value, w_out, w_up, w_down, cotangent
):
    assert lax.axis_size("band") == 2 and block_input.shape[2:4] == (16, 16)
    band = lax.axis_index("band")
    flags = band_live[0]
    live_own = lax.dynamic_index_in_dim(flags, band, keepdims=True)
    live_other = lax.dynamic_index_in_dim(flags, 1 - band, keepdims=True)
    live = (live_own == 1).astype(jnp.int32)
    halo_ok = ((live_other == 1) | (live_own != 1)).astype(jnp.int32)
    mod = modulation[0]

    edge = lax.dynamic_slice_in_dim(block_input[0], 12 - 12 * band, 4, axis=1)
    x_halo = band_swap(edge)
    xw, normed, q, k, v = pre(block_input, mod, (w_query, w_key, w_value), 8, True)
    kh, vh = pre(x_halo, mod, (w_key, w_value), 2, False)
    attended, lse = attn_fwd(halo_ok, q, k, v, kh, vh)
    ao, middle, nm, gw, gm = mid(cotangent, live, attended, w_out, xw, mod)
    mo, h, d_up, d_down = mlp(nm, gm, w_up, w_down)
    g_up, g_down = reduced(d_up), reduced(d_down)
    block_output, gmid, ga, do, sums_m = post(live, middle, mo, h, gw, ao, mod, w_out, block_input)
    g_out = reduced(outer(attended, ga))
    dq2, dk2, dv2, send = attn_bwd_paired(halo_ok, q, k, v, do, lse, kh, vh)
    got = band_swap(send).astype(F32)
    dq1, dk1, dv1 = attn_bwd_main(halo_ok, q, k, v, do, lse)
    dq = jnp.concatenate([dq1, dq2])
    dk = jnp.concatenate([dk1, (dk2 + got[0]).astype(BF16)])
    dv = jnp.concatenate([dv1, (dv2 + got[1]).astype(BF16)])
    g_query, g_key, g_value = (reduced(outer(normed, d)) for d in (dq, dk, dv))
    grad_input, sums_a = final(dq, dk, dv, w_query, w_key, w_value, xw, gmid, mod, block_input)
    mod_part = jnp.concatenate([sums_a[0:2], sums_m[0:4]])
    mod_total = mod_part + band_swap(mod_part)
    return block_output, grad_input, mod_total[None], g_query, g_key, g_value, g_out, g_up, g_down


def solution(mesh):
    return jax.shard_map(
        on_device,
        mesh=mesh,
        in_specs=(
            P("dp", None, "band", None, None),
            P("dp", None, None),
            P("dp", None),
            P(),
            P(),
            P(),
            P(),
            P(),
            P(),
            P("dp", None, "band", None, None),
        ),
        out_specs=(
            P("dp", None, "band", None, None),
            P("dp", None, "band", None, None),
            P("dp", None, None),
            P("dp"),
            P("dp"),
            P("dp"),
            P("dp"),
            P("dp"),
            P("dp"),
        ),
        check_vma=False,
    )
```

```python
import functools

import jax
import jax.numpy as jnp
from jax import lax
from jax.experimental import pallas as pl
from jax.experimental.pallas import tpu as pltpu
from jax.sharding import PartitionSpec as P

HEADS = 16
HEAD_DIM = 64
EPS = 1e-06
MASKED = -1e30
LOG2E = 1.4426950408889634
F32 = jnp.float32
BF16 = jnp.bfloat16
ANY = pl.BlockSpec(memory_space=pl.ANY)
VMEM_LIMIT = 60 * 1024 * 1024

MID_SPOTS = ((1, 0), (2, 0), (1, 1), (2, 1))


def group_spot(band, s):
    lone = 3 * band
    paired = 3 - 3 * band
    if s < 2:
        return lone, s
    if s < 6:
        return MID_SPOTS[s - 2]
    return paired, s - 6


def params(**kw):
    return pltpu.CompilerParams(vmem_limit_bytes=VMEM_LIMIT, **kw)


def dot(a, b, ca=1, cb=0):
    return lax.dot_general(a, b, (((ca,), (cb,)), ((), ())), preferred_element_type=F32)


def whole(shape):
    return pl.BlockSpec(shape, lambda *_: (0,) * len(shape), pipeline_mode=pl.Buffered(1))


def norm_stats(v):
    c = v - jnp.mean(v, axis=-1, keepdims=True)
    r = lax.rsqrt(jnp.mean(c * c, axis=-1, keepdims=True) + EPS)
    return c * r, r


def spot_copy(hbm, vmem, band, s, sem, out=False):
    g, j = group_spot(band, s)
    there = hbm.at[0, :, pl.ds(g * 4, 4), pl.ds(j * 8, 8), :]
    if out:
        return pltpu.make_async_copy(vmem.at[s], there, sem.at[s])
    return pltpu.make_async_copy(there, vmem.at[s], sem.at[s])


def pre_kernel(n_group, from_spots, x_hbm, mod_ref, *refs):
    n_mat = (len(refs) - 5) // 2 if from_spots else (len(refs) - 3) // 2
    w_refs = refs[:n_mat]
    outs = refs[n_mat:]
    if from_spots:
        xw_ref, normed_ref = outs[:2]
        o_refs = outs[2 : 2 + n_mat]
    else:
        o_refs = outs[:n_mat]
    stage, sem, nsc = outs[-3:] if not from_spots else outs[-3:]
    rows = nsc.shape[0] // n_group

    @pl.when(pl.program_id(0) == 0)
    def _():
        band = lax.axis_index("band")
        if from_spots:
            copies = [spot_copy(x_hbm, stage, band, s, sem) for s in range(n_group)]
        else:
            copies = [
                pltpu.make_async_copy(x_hbm.at[:, :, pl.ds(8 * s, 8), :], stage.at[s], sem.at[s])
                for s in range(n_group)
            ]
        for c in copies:
            c.start()
        for s in range(n_group):
            copies[s].wait()
            x = stage[s].astype(F32).reshape(rows, stage.shape[-1])
            n, _ = norm_stats(x)
            part = pl.ds(s * rows, rows)
            nsc[part, :] = (n * (1.0 + mod_ref[1:2, :]) + mod_ref[0:1, :]).astype(BF16)
            if from_spots:
                xw_ref[part, :] = x.astype(BF16)
                normed_ref[part, :] = nsc[part, :]

    for w_ref, o_ref in zip(w_refs, o_refs):
        o_ref[...] = dot(nsc[...], w_ref[...]).astype(BF16)


def pre(x, mod, weights, n_group, from_spots):
    d = x.shape[-1]
    frames = x.shape[1] if from_spots else x.shape[0]
    rows = frames * 32
    t = n_group * rows
    tile = 256
    o_tile = pl.BlockSpec((t, tile), lambda n: (0, n))
    full = pl.BlockSpec((t, d), lambda n: (0, 0))
    act = jax.ShapeDtypeStruct((t, d), BF16)
    k = len(weights)
    head = [act, act] if from_spots else []
    return pl.pallas_call(
        functools.partial(pre_kernel, n_group, from_spots),
        grid=(d // tile,),
        in_specs=[ANY, whole((6, d))] + [pl.BlockSpec((d, tile), lambda n: (0, n))] * k,
        out_specs=[full] * len(head) + [o_tile] * k,
        out_shape=head + [act] * k,
        scratch_shapes=[
            pltpu.VMEM((n_group, frames, 4, 8, d), BF16),
            pltpu.SemaphoreType.DMA((n_group,)),
            pltpu.VMEM((t, d), BF16),
        ],
        compiler_params=params(),
        name="pre" if from_spots else "pre_halo",
        cost_estimate=pl.CostEstimate(
            flops=2 * t * d * d * k, bytes_accessed=2 * (k * d * d + (k + 3) * t * d), transcendentals=0
        ),
    )(x, mod, *weights)


def units(rows):
    r = rows
    out = [((0, r), (0, r), None), ((r, r), (r, r), None)]
    out += [((2 * r, 2 * r), (2 * r, 2 * r), None), ((4 * r, 2 * r), (4 * r, 2 * r), None)]
    out += [((6 * r, r), (6 * r, r), (0, r)), ((7 * r, r), (7 * r, r), (r, r))]
    return out


SCALE2 = HEAD_DIM**-0.5 * LOG2E


def attn_fwd_kernel(ok_ref, q_ref, k_ref, v_ref, kh_ref, vh_ref, o_ref, lse_ref):
    r = q_ref.shape[0] // 8
    halo_ok = ok_ref[0] == 1
    for h in range(2):
        lanes = slice(64 * h, 64 * h + 64)
        for (q0, qn), (k0, kn), halo in units(r):
            q = q_ref[q0 : q0 + qn, lanes]
            k = k_ref[k0 : k0 + kn, lanes]
            v = v_ref[k0 : k0 + kn, lanes]
            s = dot(q, k, 1, 1) * SCALE2
            top = jnp.max(s, axis=-1, keepdims=True)
            if halo is not None:
                kh = kh_ref[halo[0] : halo[0] + halo[1], lanes]
                vh = vh_ref[halo[0] : halo[0] + halo[1], lanes]
                sh = jnp.where(halo_ok, dot(q, kh, 1, 1) * SCALE2, MASKED)
                top = jnp.maximum(top, jnp.max(sh, axis=-1, keepdims=True))
            e = jnp.exp2(s - top)
            total = jnp.sum(e, axis=-1, keepdims=True)
            o = dot(e.astype(BF16), v)
            if halo is not None:
                eh = jnp.exp2(sh - top)
                total = total + jnp.sum(eh, axis=-1, keepdims=True)
                o = o + dot(eh.astype(BF16), vh)
            o_ref[q0 : q0 + qn, lanes] = (o * (1.0 / total)).astype(BF16)
            lse_ref[q0 : q0 + qn, lanes] = jnp.broadcast_to(top + jnp.log2(total), (qn, 64))


def attn_fwd(halo_ok, q, k, v, kh, vh):
    t, d = q.shape
    th = kh.shape[0]
    big = pl.BlockSpec((t, 128), lambda n: (0, n))
    small = pl.BlockSpec((th, 128), lambda n: (0, n))
    pairs = t * t // 8 * 2 * 7 // 8
    return pl.pallas_call(
        attn_fwd_kernel,
        grid=(d // 128,),
        in_specs=[pl.BlockSpec(memory_space=pltpu.SMEM), big, big, big, small, small],
        out_specs=[big, big],
        out_shape=[jax.ShapeDtypeStruct((t, d), BF16), jax.ShapeDtypeStruct((t, d), F32)],
        compiler_params=params(),
        name="attn_fwd",
        cost_estimate=pl.CostEstimate(
            flops=4 * pairs * d * 4, bytes_accessed=12 * t * d, transcendentals=pairs * 16
        ),
    )(halo_ok, q, k, v, kh, vh)


def attn_bwd_kernel(which, ok_ref, q_ref, k_ref, v_ref, do_ref, lse_ref, *refs):
    base = 0
    if which == "paired":
        kh_ref, vh_ref, dq_ref, dk_ref, dv_ref, out_ref = refs
        r = q_ref.shape[0] // 2
        base = 6 * r
        todo = units(r)[4:]
        halo_ok = ok_ref[0] == 1
    else:
        dq_ref, dk_ref, dv_ref = refs
        r = q_ref.shape[0] // 6
        todo = units(r)[:4]
    scale = HEAD_DIM**-0.5
    for h in range(2):
        lanes = slice(64 * h, 64 * h + 64)
        for (q0, qn), (k0, kn), halo in todo:
            qs, ks = slice(q0 - base, q0 - base + qn), slice(k0 - base, k0 - base + kn)
            q, k, v = q_ref[qs, lanes], k_ref[ks, lanes], v_ref[ks, lanes]
            do = do_ref[qs, lanes]
            lse = lse_ref[qs, 64 * h : 64 * h + 1]
            p = jnp.exp2(dot(q, k, 1, 1) * SCALE2 - lse)
            dp = dot(do, v, 1, 1)
            row = jnp.sum(p * dp, axis=-1, keepdims=True)
            if halo is not None:
                hs = slice(halo[0], halo[0] + halo[1])
                kh, vh = kh_ref[hs, lanes], vh_ref[hs, lanes]
                sh = jnp.where(halo_ok, dot(q, kh, 1, 1) * SCALE2, MASKED)
                ph = jnp.exp2(sh - lse)
                dph = dot(do, vh, 1, 1)
                row = row + jnp.sum(ph * dph, axis=-1, keepdims=True)
            ds = (p * (dp - row)).astype(BF16)
            dq = dot(ds, k)
            dk = dot(ds, q, 0, 0) * scale
            dv = dot(p.astype(BF16), do, 0, 0)
            if halo is not None:
                dsh = (ph * (dph - row)).astype(BF16)
                dq = dq + dot(dsh, kh)
                out_ref[0, hs, lanes] = (dot(dsh, q, 0, 0) * scale).astype(BF16)
                out_ref[1, hs, lanes] = dot(ph.astype(BF16), do, 0, 0).astype(BF16)
            dq_ref[qs, lanes] = (dq * scale).astype(dq_ref.dtype)
            dk_ref[ks, lanes] = dk.astype(dk_ref.dtype)
            dv_ref[ks, lanes] = dv.astype(dv_ref.dtype)


def attn_bwd_main(halo_ok, q, k, v, do, lse):
    t, d = q.shape
    part = t // 8 * 6
    big = pl.BlockSpec((part, 128), lambda n: (0, n))
    act = jax.ShapeDtypeStruct((t, d), BF16)
    pairs = t * t // 64 * 10
    return pl.pallas_call(
        functools.partial(attn_bwd_kernel, "main"),
        grid=(d // 128,),
        in_specs=[pl.BlockSpec(memory_space=pltpu.SMEM)] + [big] * 5,
        out_specs=[big] * 3,
        out_shape=[jax.ShapeDtypeStruct((part, d), BF16)] * 3,
        compiler_params=params(),
        name="attn_bwd_main",
        cost_estimate=pl.CostEstimate(
            flops=10 * pairs * d * 4, bytes_accessed=18 * t * d, transcendentals=pairs * 16
        ),
    )(halo_ok, q, k, v, do, lse)


def attn_bwd_paired(halo_ok, q, k, v, do, lse, kh, vh):
    t, d = q.shape
    part = t // 4
    big = pl.BlockSpec((part, 128), lambda n: (3, n))
    small = pl.BlockSpec((part, 128), lambda n: (0, n))
    f32 = jax.ShapeDtypeStruct((part, d), F32)
    pairs = t * t // 64 * 4
    return pl.pallas_call(
        functools.partial(attn_bwd_kernel, "paired"),
        grid=(d // 128,),
        in_specs=[pl.BlockSpec(memory_space=pltpu.SMEM)] + [big] * 5 + [small] * 2,
        out_specs=[small] * 3 + [pl.BlockSpec((2, part, 128), lambda n: (0, 0, n))],
        out_shape=[jax.ShapeDtypeStruct((part, d), BF16), f32, f32, jax.ShapeDtypeStruct((2, part, d), BF16)],
        compiler_params=params(),
        name="attn_bwd_paired",
        cost_estimate=pl.CostEstimate(
            flops=10 * pairs * d * 4, bytes_accessed=12 * t * d, transcendentals=pairs * 16
        ),
    )(halo_ok, q, k, v, do, lse, kh, vh)


def mid_kernel(g_hbm, live_ref, att_ref, w_ref, x_ref, mod_ref, ao_ref, mid_ref, nm_ref, gw_ref, gm_ref, stage, sem):
    step = pl.program_id(0)
    band = lax.axis_index("band")
    live = live_ref[0].astype(F32)
    n_group = stage.shape[0]
    per = n_group // 4
    rows = gw_ref.shape[0] // per

    @pl.when(step == 0)
    def _():
        for s in range(n_group):
            spot_copy(g_hbm, stage, band, s, sem).start()

    attn_out = dot(att_ref[...], w_ref[...])
    middle = x_ref[...].astype(F32) + (live * mod_ref[2:3, :]) * attn_out
    ao_ref[...] = attn_out
    mid_ref[...] = middle
    n, _ = norm_stats(middle)
    nm_ref[...] = (n * (1.0 + mod_ref[4:5, :]) + mod_ref[3:4, :]).astype(BF16)
    for i in range(per):
        s = step * per + i
        pltpu.make_async_copy(g_hbm.at[0, :, pl.ds(0, 4), pl.ds(0, 8), :], stage.at[s], sem.at[s]).wait()
        g = stage[s].astype(F32).reshape(rows, stage.shape[-1])
        part = pl.ds(i * rows, rows)
        gw_ref[part, :] = g.astype(BF16)
        gm_ref[part, :] = ((live * mod_ref[5:6, :]) * g).astype(BF16)


def mid(cot, live, attended, w_out, xw, mod):
    t, d = xw.shape
    frames = cot.shape[1]
    blk = pl.BlockSpec((t // 4, d), lambda m: (m, 0))
    bf, f32 = jax.ShapeDtypeStruct((t, d), BF16), jax.ShapeDtypeStruct((t, d), F32)
    return pl.pallas_call(
        mid_kernel,
        grid=(4,),
        in_specs=[ANY, pl.BlockSpec(memory_space=pltpu.SMEM), blk, whole((d, d)), blk, whole((6, d))],
        out_specs=[blk] * 5,
        out_shape=[f32, f32, bf, bf, bf],
        scratch_shapes=[pltpu.VMEM((8, frames, 4, 8, d), BF16), pltpu.SemaphoreType.DMA((8,))],
        compiler_params=params(),
        name="mid",
        cost_estimate=pl.CostEstimate(flops=2 * t * d * d, bytes_accessed=22 * t * d, transcendentals=0),
    )(cot, live, attended, w_out, xw, mod)


GELU_C = 0.7978845608
GELU_A = 0.044715


def mlp_kernel(nm_ref, gm_ref, wu_ref, wd_ref, mo_ref, h_ref, dwu_ref, dwd_ref, hid, gp):
    first = pl.program_id(0) == 0
    t = nm_ref.shape[0]
    chunk = t // 4

    @pl.when(first)
    def _():
        mo_ref[...] = jnp.zeros_like(mo_ref)
        h_ref[...] = jnp.zeros_like(h_ref)

    def rows(i, _):
        part = pl.ds(pl.multiple_of(i * chunk, chunk), chunk)
        nm, gm = nm_ref[part, :], gm_ref[part, :]
        v = dot(nm, wu_ref[...])
        gh = dot(gm, wd_ref[...], 1, 1)
        v2 = v * v
        th = jnp.tanh(v * (GELU_C + (GELU_C * GELU_A) * v2))
        half = 0.5 * th + 0.5
        hidden = (v * half).astype(BF16)
        slope = half + (0.5 * v) * (1.0 - th * th) * (GELU_C + (3.0 * GELU_C * GELU_A) * v2)
        gpre = (gh * slope).astype(BF16)
        hid[part, :] = hidden
        gp[part, :] = gpre
        mo_ref[part, :] += dot(hidden, wd_ref[...])
        h_ref[part, :] += dot(gpre, wu_ref[...], 1, 1)
        return 0

    lax.fori_loop(0, 4, rows, 0)
    dwd_ref[...] = dot(hid[...], gm_ref[...], 0, 0).astype(BF16)
    dwu_ref[...] = dot(nm_ref[...], gp[...], 0, 0).astype(BF16)


def mlp(nm, gm, w_up, w_down):
    t, d = nm.shape
    ff = w_up.shape[1]
    tile = 512
    f32 = jax.ShapeDtypeStruct((t, d), F32)
    return pl.pallas_call(
        mlp_kernel,
        grid=(ff // tile,),
        in_specs=[
            whole((t, d)),
            whole((t, d)),
            pl.BlockSpec((d, tile), lambda f: (0, f)),
            pl.BlockSpec((tile, d), lambda f: (f, 0)),
        ],
        out_specs=[
            whole((t, d)),
            whole((t, d)),
            pl.BlockSpec((d, tile), lambda f: (0, f)),
            pl.BlockSpec((tile, d), lambda f: (f, 0)),
        ],
        out_shape=[f32, f32, jax.ShapeDtypeStruct((d, ff), BF16), jax.ShapeDtypeStruct((ff, d), BF16)],
        scratch_shapes=[pltpu.VMEM((t, tile), BF16), pltpu.VMEM((t, tile), BF16)],
        compiler_params=params(),
        name="mlp",
        cost_estimate=pl.CostEstimate(flops=12 * t * d * ff, bytes_accessed=8 * d * ff + 12 * t * d, transcendentals=t * ff),
    )(nm, gm, w_up, w_down)


def post_kernel(live_ref, mid_ref, mo_ref, h_ref, g_ref, ao_ref, mod_ref, w_ref, out_hbm, gmid_ref, ga_ref, do_ref, sums_ref, stage, sem):
    step = pl.program_id(0)
    band = lax.axis_index("band")
    live = live_ref[0].astype(F32)
    n_group = stage.shape[0]
    per = n_group // 4
    middle = mid_ref[...]
    g = g_ref[...].astype(F32)
    mo = mo_ref[...]
    h = h_ref[...]
    out = middle + (live * mod_ref[5:6, :]) * mo
    n, r = norm_stats(middle)
    e = h * (1.0 + mod_ref[4:5, :])
    gmid = g + r * (e - jnp.mean(e, axis=-1, keepdims=True) - n * jnp.mean(e * n, axis=-1, keepdims=True))
    gmid_ref[...] = gmid
    ga = ((live * mod_ref[2:3, :]) * gmid).astype(BF16)
    ga_ref[...] = ga
    do_ref[...] = dot(ga, w_ref[...], 1, 1).astype(BF16)

    def col(v):
        return jnp.sum(v, axis=0, keepdims=True)

    sums = jnp.concatenate(
        [col(live * ao_ref[...] * gmid), col(h), col(h * n), col(live * mo * g), jnp.zeros((4, h.shape[1]), F32)], axis=0
    )

    @pl.when(step == 0)
    def _():
        sums_ref[...] = sums

    @pl.when(step > 0)
    def _():
        sums_ref[...] += sums

    rows = h.shape[0] // per
    shape = stage.shape[1:]
    for k in range(4):

        @pl.when(step == k)
        def _():
            for i in range(per):
                s = k * per + i
                stage[s] = out[i * rows : (i + 1) * rows, :].reshape(shape).astype(BF16)
                spot_copy(out_hbm, stage, band, s, sem, out=True).start()

    @pl.when(step == 3)
    def _():
        for s in range(n_group):
            spot_copy(out_hbm, stage, band, s, sem, out=True).wait()


def post(live, middle, mo, h, gw, ao, mod, w_out, like):
    t, d = gw.shape
    frames = like.shape[1]
    blk = pl.BlockSpec((t // 4, d), lambda m: (m, 0))
    bf, f32 = jax.ShapeDtypeStruct((t, d), BF16), jax.ShapeDtypeStruct((t, d), F32)
    return pl.pallas_call(
        post_kernel,
        grid=(4,),
        in_specs=[pl.BlockSpec(memory_space=pltpu.SMEM), blk, blk, blk, blk, blk, whole((6, d)), whole((d, d))],
        out_specs=[ANY, blk, blk, blk, pl.BlockSpec((8, d), lambda m: (0, 0))],
        out_shape=[jax.ShapeDtypeStruct(like.shape, BF16), f32, bf, bf, jax.ShapeDtypeStruct((8, d), F32)],
        scratch_shapes=[pltpu.VMEM((8, frames, 4, 8, d), BF16), pltpu.SemaphoreType.DMA((8,))],
        compiler_params=params(),
        name="post",
        cost_estimate=pl.CostEstimate(flops=2 * t * d * d, bytes_accessed=30 * t * d, transcendentals=0),
    )(live, middle, mo, h, gw, ao, mod, w_out)


def outer_kernel(a_ref, b_ref, o_ref):
    o_ref[...] = dot(a_ref[...], b_ref[...], 0, 0).astype(BF16)


def outer(a, b):
    t, d = a.shape
    tile = 512
    return pl.pallas_call(
        outer_kernel,
        grid=(b.shape[1] // tile,),
        in_specs=[whole((t, d)), pl.BlockSpec((t, tile), lambda n: (0, n))],
        out_specs=pl.BlockSpec((d, tile), lambda n: (0, n)),
        out_shape=jax.ShapeDtypeStruct((d, b.shape[1]), BF16),
        compiler_params=params(),
        name="outer",
        cost_estimate=pl.CostEstimate(flops=2 * t * d * b.shape[1], bytes_accessed=6 * t * d, transcendentals=0),
    )(a, b)


def final_kernel(dq_ref, dk_ref, dv_ref, wq_ref, wk_ref, wv_ref, x_ref, gmid_ref, mod_ref, out_hbm, sums_ref, stage, sem):
    step = pl.program_id(0)
    band = lax.axis_index("band")
    n_group = stage.shape[0]
    per = n_group // 4
    h = dot(dq_ref[...], wq_ref[...], 1, 1) + dot(dk_ref[...], wk_ref[...], 1, 1) + dot(dv_ref[...], wv_ref[...], 1, 1)
    n, r = norm_stats(x_ref[...].astype(F32))
    e = h * (1.0 + mod_ref[1:2, :])
    out = gmid_ref[...] + r * (e - jnp.mean(e, axis=-1, keepdims=True) - n * jnp.mean(e * n, axis=-1, keepdims=True))

    def col(v):
        return jnp.sum(v, axis=0, keepdims=True)

    sums = jnp.concatenate([col(h), col(h * n), jnp.zeros((6, h.shape[1]), F32)], axis=0)

    @pl.when(step == 0)
    def _():
        sums_ref[...] = sums

    @pl.when(step > 0)
    def _():
        sums_ref[...] += sums

    rows = h.shape[0] // per
    shape = stage.shape[1:]
    for k in range(4):

        @pl.when(step == k)
        def _():
            for i in range(per):
                s = k * per + i
                stage[s] = out[i * rows : (i + 1) * rows, :].reshape(shape).astype(BF16)
                spot_copy(out_hbm, stage, band, s, sem, out=True).start()

    @pl.when(step == 3)
    def _():
        for s in range(n_group):
            spot_copy(out_hbm, stage, band, s, sem, out=True).wait()


def final(dq, dk, dv, wq, wk, wv, xw, gmid, mod, like):
    t, d = xw.shape
    frames = like.shape[1]
    blk = pl.BlockSpec((t // 4, d), lambda m: (m, 0))
    return pl.pallas_call(
        final_kernel,
        grid=(4,),
        in_specs=[blk, blk, blk, whole((d, d)), whole((d, d)), whole((d, d)), blk, blk, whole((6, d))],
        out_specs=[ANY, pl.BlockSpec((8, d), lambda m: (0, 0))],
        out_shape=[jax.ShapeDtypeStruct(like.shape, BF16), jax.ShapeDtypeStruct((8, d), F32)],
        scratch_shapes=[pltpu.VMEM((8, frames, 4, 8, d), BF16), pltpu.SemaphoreType.DMA((8,))],
        compiler_params=params(),
        name="final",
        cost_estimate=pl.CostEstimate(flops=6 * t * d * d, bytes_accessed=14 * t * d, transcendentals=0),
    )(dq, dk, dv, wq, wk, wv, xw, gmid, mod)


LANES = 512


class Reduce:
    def __init__(self, dp, total_rows, orders, vmem_source):
        self.bits = list(range(dp.bit_length() - 2, 0, -1))
        self.nz = len(self.bits)
        self.stages = self.nz + 1
        self.depth = self.stages + 4
        self.r = total_rows // dp
        self.orders = orders
        self.vmem_source = vmem_source
        self.dp = dp

    def scratch(self):
        r, nz, k = self.r, self.nz, self.stages
        cube = (2,) * nz
        out = [] if self.vmem_source else [pltpu.VMEM(cube + (r, LANES), BF16)]
        out += [pltpu.VMEM((2,) + cube + (r, LANES), BF16)]
        for _ in range(2):
            for i in range(k):
                block = (2,) * (k - 1 - i) + (r, 128)
                out += [pltpu.VMEM(block, BF16), pltpu.VMEM(block, BF16), pltpu.VMEM((2,) + block, BF16)]
        out += [pltpu.VMEM((2, r, 128), BF16), pltpu.VMEM((2, 2, r, 128), BF16), pltpu.VMEM((r, LANES), F32)]
        out += [pltpu.SemaphoreType.DMA((2 * k + 4,)), pltpu.SemaphoreType.DMA((2 * k + 2, 2))]
        return out

    def bind(self, refs, source, write):
        refs = list(refs)
        self.own = None if self.vmem_source else refs.pop(0)
        self.got_core = refs.pop(0)
        self.send, self.keep, self.got = {}, {}, {}
        for p in range(2):
            for i in range(self.stages):
                self.send[p, i], self.keep[p, i], self.got[p, i] = refs.pop(0), refs.pop(0), refs.pop(0)
        self.fin, self.got_fin, self.ostage, self.ssem, self.rsem = refs
        self.source, self.write = source, write
        self.me, self.band = lax.axis_index("dp"), lax.axis_index("band")

    def place(self, axis):
        return self.band if axis == 0 else lax.rem(self.me // (1 << axis), 2)

    def partner(self, axis):
        if axis == 0:
            return (self.me, 1 - self.band)
        bit = 1 if axis == -1 else 1 << axis
        here = lax.rem(self.me // bit, 2)
        return (self.me + bit - 2 * bit * here, self.band)

    def barrier(self):
        sem = pltpu.get_barrier_semaphore()
        everyone = [-1, 0] + self.bits
        for axis in everyone:
            pl.semaphore_signal(sem, inc=1, device_id=self.partner(axis), device_id_type=pl.DeviceIdType.MESH)
        pl.semaphore_wait(sem, len(everyone))

    def remote(self, src, dst, s, slot, axis):
        return pltpu.make_async_remote_copy(
            src_ref=src,
            dst_ref=dst,
            send_sem=self.ssem.at[s],
            recv_sem=self.rsem.at[s, slot],
            device_id=self.partner(axis),
            device_id_type=pl.DeviceIdType.MESH,
        )

    def core_copy(self, slot, src):
        return self.remote(src, self.got_core.at[slot], 2 * self.stages, slot, -1)

    def part_copy(self, p, i, slot):
        return self.remote(self.send[p, i], self.got[p, i].at[slot], 2 * i + p, slot, self.orders[p][i])

    def fin_copy(self, slot):
        return self.remote(self.fin, self.got_fin.at[slot], 2 * self.stages + 1, slot, 0)

    def pick(self, axes, axis, at):
        return tuple(at if a == axis else slice(None) for a in axes)

    def split_core(self, j, p):
        slot = lax.rem(j, 2)
        first = self.orders[p][0]
        mine = self.place(first)
        for dst, at in ((self.send[p, 0], 1 - mine), (self.keep[p, 0], mine)):
            if first == 0:
                lanes = pl.ds(pl.multiple_of((2 * p + at) * 128, 128), 128)
                idx = (slice(None),) * (self.nz + 1) + (lanes,)
                v = self.own_half(slot, idx) + self.got_core[(slot,) + idx].astype(F32)
                dst[...] = v.astype(BF16)
            else:
                for b in range(2):
                    lanes = slice((2 * p + b) * 128, (2 * p + b + 1) * 128)
                    idx = self.pick(self.bits, first, at) + (slice(None), lanes)
                    v = self.own_half(slot, idx) + self.got_core[(slot,) + idx].astype(F32)
                    dst[(slice(None),) * (self.nz - 1) + (b,)] = v.astype(BF16)

    def own_half(self, slot, idx):
        if self.vmem_source:
            return self.source(slot, idx).astype(F32)
        return self.own[idx].astype(F32)

    def split(self, j, p, i):
        slot = lax.rem(j, 2)
        axes = [a for a in self.bits + [0] if a not in self.orders[p][:i]]
        axis = self.orders[p][i]
        mine = self.place(axis)
        for dst, at in ((self.send[p, i], 1 - mine), (self.keep[p, i], mine)):
            idx = self.pick(axes, axis, at)
            v = self.keep[p, i - 1][idx].astype(F32) + self.got[p, i - 1][(slot,) + idx].astype(F32)
            dst[...] = v.astype(BF16)

    def stage(self, s, j):
        k = self.stages
        slot = lax.rem(j, 2)
        if s == 0:
            if self.vmem_source:
                self.core_copy(slot, self.source(slot, None)).start()
            else:
                self.source(j, self)
        elif s == 1:
            dummy = self.source(slot, None) if self.vmem_source else self.own
            self.core_copy(slot, dummy).wait()
            if not self.vmem_source:
                pltpu.make_async_copy(self.own, self.own, self.ssem.at[2 * k + 2]).wait()
            for p in range(2):
                self.split_core(j, p)
                self.part_copy(p, 0, slot).start()
        elif s <= k:
            for p in range(2):
                self.part_copy(p, s - 2, slot).wait()
                self.split(j, p, s - 1)
                self.part_copy(p, s - 1, slot).start()
        elif s == k + 1:
            for p in range(2):
                self.part_copy(p, k - 1, slot).wait()
                v = self.keep[p, k - 1][...].astype(F32) + self.got[p, k - 1][slot].astype(F32)
                self.fin[p] = v.astype(BF16)
            self.fin_copy(slot).start()
        elif s == k + 2:
            self.fin_copy(slot).wait()
            for p in range(2):
                mine = pl.ds(pl.multiple_of((2 * p + self.band) * 128, 128), 128)
                other = pl.ds(pl.multiple_of((2 * p + 1 - self.band) * 128, 128), 128)
                self.ostage[:, mine] = self.fin[p].astype(F32)
                self.ostage[:, other] = self.got_fin[slot, p].astype(F32)
            self.write(j, self)
        else:
            pltpu.make_async_copy(self.ostage, self.ostage, self.ssem.at[2 * k + 3]).wait()

    def tick(self, t, jobs):
        for s in reversed(range(self.depth)):
            j = t - s

            @pl.when((j >= 0) & (j < jobs))
            def _():
                self.stage(s, j)


def comm_kernel(sizes, red, *refs):
    n = len(sizes)
    srcs, outs, scratch = refs[:n], refs[n : 2 * n], refs[2 * n :]
    core = lax.rem(lax.axis_index("dp"), 2)

    def dispatch(j, body):
        base = 0
        for i, (q, wide) in enumerate(sizes):
            count = q * wide

            @pl.when((j >= base) & (j < base + count))
            def _():
                at = j - base
                body(i, at // wide, pl.ds(pl.multiple_of(lax.rem(at, wide) * LANES, LANES), LANES))

            base += count

    def source(j, red):
        def body(i, q, lanes):
            cube = (slice(None),) * red.nz
            pltpu.make_async_copy(srcs[i].at[cube + (core, q, slice(None), lanes)], red.own, red.ssem.at[2 * red.stages + 2]).start()
            red.core_copy(lax.rem(j, 2), srcs[i].at[cube + (1 - core, q, slice(None), lanes)]).start()

        dispatch(j, body)

    def write(j, red):
        def body(i, q, lanes):
            pltpu.make_async_copy(red.ostage, outs[i].at[q, :, lanes], red.ssem.at[2 * red.stages + 3]).start()

        dispatch(j, body)

    red.bind(scratch, source, write)
    red.barrier()
    jobs = sum(q * wide for q, wide in sizes)

    def body(t, _):
        red.tick(t, jobs)
        return 0

    lax.fori_loop(0, jobs + red.depth - 1, body, 0)


def reduce_all(grads):
    dp = lax.axis_size("dp")
    low = dp.bit_length() - 2
    red = Reduce(dp, 1024, ((0, 1, *range(2, low + 1)), (1, 0, *range(2, low + 1))), False)
    sizes, srcs, outs = [], [], []
    for g in grads:
        rows, cols = g.shape
        q = rows // 1024
        sizes.append((q, cols // LANES))
        srcs.append(g.reshape((2,) * (red.nz + 1) + (q, red.r, cols)))
        outs.append(jax.ShapeDtypeStruct((q, red.r, cols), F32))
    sums = pl.pallas_call(
        functools.partial(comm_kernel, sizes, red),
        in_specs=[ANY] * len(srcs),
        out_specs=[ANY] * len(srcs),
        out_shape=outs,
        scratch_shapes=red.scratch(),
        compiler_params=params(collective_id=1, has_side_effects=True),
        name="reduce_all",
    )(*srcs)
    return [s.reshape(-1) for s in sums]


def band_swap(v):
    return lax.ppermute(v, "band", [(0, 1), (1, 0)])


def on_device(
    block_input, modulation, band_live, w_query, w_key, w_value, w_out, w_up, w_down, cotangent
):
    assert lax.axis_size("band") == 2 and block_input.shape[2:4] == (16, 16)
    band = lax.axis_index("band")
    flags = band_live[0]
    live_own = lax.dynamic_index_in_dim(flags, band, keepdims=True)
    live_other = lax.dynamic_index_in_dim(flags, 1 - band, keepdims=True)
    live = (live_own == 1).astype(jnp.int32)
    halo_ok = ((live_other == 1) | (live_own != 1)).astype(jnp.int32)
    mod = modulation[0]

    edge = lax.dynamic_slice_in_dim(block_input[0], 12 - 12 * band, 4, axis=1)
    x_halo = band_swap(edge)
    xw, normed, q, k, v = pre(block_input, mod, (w_query, w_key, w_value), 8, True)
    kh, vh = pre(x_halo, mod, (w_key, w_value), 2, False)
    attended, lse = attn_fwd(halo_ok, q, k, v, kh, vh)
    ao, middle, nm, gw, gm = mid(cotangent, live, attended, w_out, xw, mod)
    mo, h, d_up, d_down = mlp(nm, gm, w_up, w_down)
    block_output, gmid, ga, do, sums_m = post(live, middle, mo, h, gw, ao, mod, w_out, block_input)
    d_out = outer(attended, ga)
    dq2, dk2, dv2, send = attn_bwd_paired(halo_ok, q, k, v, do, lse, kh, vh)
    got = band_swap(send).astype(F32)
    dq1, dk1, dv1 = attn_bwd_main(halo_ok, q, k, v, do, lse)
    dq = jnp.concatenate([dq1, dq2])
    dk = jnp.concatenate([dk1, (dk2 + got[0]).astype(BF16)])
    dv = jnp.concatenate([dv1, (dv2 + got[1]).astype(BF16)])
    d_query, d_key, d_value = (outer(normed, d) for d in (dq, dk, dv))
    grad_input, sums_a = final(dq, dk, dv, w_query, w_key, w_value, xw, gmid, mod, block_input)
    mod_part = jnp.concatenate([sums_a[0:2], sums_m[0:4]])
    mod_total = mod_part + band_swap(mod_part)
    g_up, g_down, g_out, g_query, g_key, g_value = reduce_all((d_up, d_down, d_out, d_query, d_key, d_value))
    return block_output, grad_input, mod_total[None], g_query, g_key, g_value, g_out, g_up, g_down


def solution(mesh):
    return jax.shard_map(
        on_device,
        mesh=mesh,
        in_specs=(
            P("dp", None, "band", None, None),
            P("dp", None, None),
            P("dp", None),
            P(),
            P(),
            P(),
            P(),
            P(),
            P(),
            P("dp", None, "band", None, None),
        ),
        out_specs=(
            P("dp", None, "band", None, None),
            P("dp", None, "band", None, None),
            P("dp", None, None),
            P("dp"),
            P("dp"),
            P("dp"),
            P("dp"),
            P("dp"),
            P("dp"),
        ),
        check_vma=False,
    )
```

```python
import functools

import jax
import jax.numpy as jnp
from jax import lax
from jax.experimental import pallas as pl
from jax.experimental.pallas import tpu as pltpu
from jax.sharding import PartitionSpec as P

HEADS = 16
HEAD_DIM = 64
EPS = 1e-06
MASKED = -1e30
LOG2E = 1.4426950408889634
F32 = jnp.float32
BF16 = jnp.bfloat16
ANY = pl.BlockSpec(memory_space=pl.ANY)
VMEM_LIMIT = 60 * 1024 * 1024

MID_SPOTS = ((1, 0), (2, 0), (1, 1), (2, 1))


def group_spot(band, s):
    lone = 3 * band
    paired = 3 - 3 * band
    if s < 2:
        return lone, s
    if s < 6:
        return MID_SPOTS[s - 2]
    return paired, s - 6


def params(**kw):
    return pltpu.CompilerParams(vmem_limit_bytes=VMEM_LIMIT, **kw)


def dot(a, b, ca=1, cb=0):
    return lax.dot_general(a, b, (((ca,), (cb,)), ((), ())), preferred_element_type=F32)


def whole(shape):
    return pl.BlockSpec(shape, lambda *_: (0,) * len(shape), pipeline_mode=pl.Buffered(1))


def norm_stats(v):
    c = v - jnp.mean(v, axis=-1, keepdims=True)
    r = lax.rsqrt(jnp.mean(c * c, axis=-1, keepdims=True) + EPS)
    return c * r, r


def spot_copy(hbm, vmem, band, s, sem, out=False):
    g, j = group_spot(band, s)
    there = hbm.at[0, :, pl.ds(g * 4, 4), pl.ds(j * 8, 8), :]
    if out:
        return pltpu.make_async_copy(vmem.at[s], there, sem.at[s])
    return pltpu.make_async_copy(there, vmem.at[s], sem.at[s])


def pre_kernel(n_group, from_spots, x_hbm, mod_ref, *refs):
    n_mat = (len(refs) - 5) // 2 if from_spots else (len(refs) - 3) // 2
    w_refs = refs[:n_mat]
    outs = refs[n_mat:]
    if from_spots:
        xw_ref, normed_ref = outs[:2]
        o_refs = outs[2 : 2 + n_mat]
    else:
        o_refs = outs[:n_mat]
    stage, sem, nsc = outs[-3:] if not from_spots else outs[-3:]
    rows = nsc.shape[0] // n_group

    @pl.when(pl.program_id(0) == 0)
    def _():
        band = lax.axis_index("band")
        if from_spots:
            copies = [spot_copy(x_hbm, stage, band, s, sem) for s in range(n_group)]
        else:
            copies = [
                pltpu.make_async_copy(x_hbm.at[:, :, pl.ds(8 * s, 8), :], stage.at[s], sem.at[s])
                for s in range(n_group)
            ]
        for c in copies:
            c.start()
        for s in range(n_group):
            copies[s].wait()
            x = stage[s].astype(F32).reshape(rows, stage.shape[-1])
            n, _ = norm_stats(x)
            part = pl.ds(s * rows, rows)
            nsc[part, :] = (n * (1.0 + mod_ref[1:2, :]) + mod_ref[0:1, :]).astype(BF16)
            if from_spots:
                xw_ref[part, :] = x.astype(BF16)
                normed_ref[part, :] = nsc[part, :]

    for w_ref, o_ref in zip(w_refs, o_refs):
        o_ref[...] = dot(nsc[...], w_ref[...]).astype(BF16)


def pre(x, mod, weights, n_group, from_spots):
    d = x.shape[-1]
    frames = x.shape[1] if from_spots else x.shape[0]
    rows = frames * 32
    t = n_group * rows
    tile = 256
    o_tile = pl.BlockSpec((t, tile), lambda n: (0, n))
    full = pl.BlockSpec((t, d), lambda n: (0, 0))
    act = jax.ShapeDtypeStruct((t, d), BF16)
    k = len(weights)
    head = [act, act] if from_spots else []
    return pl.pallas_call(
        functools.partial(pre_kernel, n_group, from_spots),
        grid=(d // tile,),
        in_specs=[ANY, whole((6, d))] + [pl.BlockSpec((d, tile), lambda n: (0, n))] * k,
        out_specs=[full] * len(head) + [o_tile] * k,
        out_shape=head + [act] * k,
        scratch_shapes=[
            pltpu.VMEM((n_group, frames, 4, 8, d), BF16),
            pltpu.SemaphoreType.DMA((n_group,)),
            pltpu.VMEM((t, d), BF16),
        ],
        compiler_params=params(),
        name="pre" if from_spots else "pre_halo",
        cost_estimate=pl.CostEstimate(
            flops=2 * t * d * d * k, bytes_accessed=2 * (k * d * d + (k + 3) * t * d), transcendentals=0
        ),
    )(x, mod, *weights)


LANES = 512


class Reduce:
    def __init__(self, dp, total_rows, orders, vmem_source):
        self.bits = list(range(dp.bit_length() - 2, 0, -1))
        self.nz = len(self.bits)
        self.stages = self.nz + 1
        self.depth = self.stages + 4
        self.r = total_rows // dp
        self.orders = orders
        self.vmem_source = vmem_source
        self.dp = dp

    def scratch(self):
        r, nz, k = self.r, self.nz, self.stages
        cube = (2,) * nz
        out = [] if self.vmem_source else [pltpu.VMEM(cube + (r, LANES), BF16)]
        out += [pltpu.VMEM((2,) + cube + (r, LANES), BF16)]
        for _ in range(2):
            for i in range(k):
                block = (2,) * (k - 1 - i) + (r, 128)
                out += [pltpu.VMEM(block, BF16), pltpu.VMEM(block, BF16), pltpu.VMEM((2,) + block, BF16)]
        out += [pltpu.VMEM((2, r, 128), BF16), pltpu.VMEM((2, 2, r, 128), BF16), pltpu.VMEM((r, LANES), F32)]
        out += [pltpu.SemaphoreType.DMA((2 * k + 4,)), pltpu.SemaphoreType.DMA((2 * k + 2, 2))]
        return out

    def bind(self, refs, source, write):
        refs = list(refs)
        self.own = None if self.vmem_source else refs.pop(0)
        self.got_core = refs.pop(0)
        self.send, self.keep, self.got = {}, {}, {}
        for p in range(2):
            for i in range(self.stages):
                self.send[p, i], self.keep[p, i], self.got[p, i] = refs.pop(0), refs.pop(0), refs.pop(0)
        self.fin, self.got_fin, self.ostage, self.ssem, self.rsem = refs
        self.source, self.write = source, write
        self.me, self.band = lax.axis_index("dp"), lax.axis_index("band")

    def place(self, axis):
        return self.band if axis == 0 else lax.rem(self.me // (1 << axis), 2)

    def partner(self, axis):
        if axis == 0:
            return (self.me, 1 - self.band)
        bit = 1 if axis == -1 else 1 << axis
        here = lax.rem(self.me // bit, 2)
        return (self.me + bit - 2 * bit * here, self.band)

    def barrier(self):
        sem = pltpu.get_barrier_semaphore()
        everyone = [-1, 0] + self.bits
        for axis in everyone:
            pl.semaphore_signal(sem, inc=1, device_id=self.partner(axis), device_id_type=pl.DeviceIdType.MESH)
        pl.semaphore_wait(sem, len(everyone))

    def remote(self, src, dst, s, slot, axis):
        return pltpu.make_async_remote_copy(
            src_ref=src,
            dst_ref=dst,
            send_sem=self.ssem.at[s],
            recv_sem=self.rsem.at[s, slot],
            device_id=self.partner(axis),
            device_id_type=pl.DeviceIdType.MESH,
        )

    def core_copy(self, slot, src):
        return self.remote(src, self.got_core.at[slot], 2 * self.stages, slot, -1)

    def part_copy(self, p, i, slot):
        return self.remote(self.send[p, i], self.got[p, i].at[slot], 2 * i + p, slot, self.orders[p][i])

    def fin_copy(self, slot):
        return self.remote(self.fin, self.got_fin.at[slot], 2 * self.stages + 1, slot, 0)

    def pick(self, axes, axis, at):
        return tuple(at if a == axis else slice(None) for a in axes)

    def split_core(self, j, p):
        slot = lax.rem(j, 2)
        first = self.orders[p][0]
        mine = self.place(first)
        for dst, at in ((self.send[p, 0], 1 - mine), (self.keep[p, 0], mine)):
            if first == 0:
                lanes = pl.ds(pl.multiple_of((2 * p + at) * 128, 128), 128)
                idx = (slice(None),) * (self.nz + 1) + (lanes,)
                v = self.own_half(slot, idx) + self.got_core[(slot,) + idx].astype(F32)
                dst[...] = v.astype(BF16)
            else:
                for b in range(2):
                    lanes = slice((2 * p + b) * 128, (2 * p + b + 1) * 128)
                    idx = self.pick(self.bits, first, at) + (slice(None), lanes)
                    v = self.own_half(slot, idx) + self.got_core[(slot,) + idx].astype(F32)
                    dst[(slice(None),) * (self.nz - 1) + (b,)] = v.astype(BF16)

    def own_half(self, slot, idx):
        if self.vmem_source:
            return self.source(slot, idx).astype(F32)
        return self.own[idx].astype(F32)

    def split(self, j, p, i):
        slot = lax.rem(j, 2)
        axes = [a for a in self.bits + [0] if a not in self.orders[p][:i]]
        axis = self.orders[p][i]
        mine = self.place(axis)
        for dst, at in ((self.send[p, i], 1 - mine), (self.keep[p, i], mine)):
            idx = self.pick(axes, axis, at)
            v = self.keep[p, i - 1][idx].astype(F32) + self.got[p, i - 1][(slot,) + idx].astype(F32)
            dst[...] = v.astype(BF16)

    def stage(self, s, j):
        k = self.stages
        slot = lax.rem(j, 2)
        if s == 0:
            if self.vmem_source:
                self.core_copy(slot, self.source(slot, None)).start()
            else:
                self.source(j, self)
        elif s == 1:
            dummy = self.source(slot, None) if self.vmem_source else self.own
            self.core_copy(slot, dummy).wait()
            if not self.vmem_source:
                pltpu.make_async_copy(self.own, self.own, self.ssem.at[2 * k + 2]).wait()
            for p in range(2):
                self.split_core(j, p)
                self.part_copy(p, 0, slot).start()
        elif s <= k:
            for p in range(2):
                self.part_copy(p, s - 2, slot).wait()
                self.split(j, p, s - 1)
                self.part_copy(p, s - 1, slot).start()
        elif s == k + 1:
            for p in range(2):
                self.part_copy(p, k - 1, slot).wait()
                v = self.keep[p, k - 1][...].astype(F32) + self.got[p, k - 1][slot].astype(F32)
                self.fin[p] = v.astype(BF16)
            self.fin_copy(slot).start()
        elif s == k + 2:
            self.fin_copy(slot).wait()
            for p in range(2):
                mine = pl.ds(pl.multiple_of((2 * p + self.band) * 128, 128), 128)
                other = pl.ds(pl.multiple_of((2 * p + 1 - self.band) * 128, 128), 128)
                self.ostage[:, mine] = self.fin[p].astype(F32)
                self.ostage[:, other] = self.got_fin[slot, p].astype(F32)
            self.write(j, self)
        else:
            pltpu.make_async_copy(self.ostage, self.ostage, self.ssem.at[2 * k + 3]).wait()

    def tick(self, t, jobs):
        for s in reversed(range(self.depth)):
            j = t - s

            @pl.when((j >= 0) & (j < jobs))
            def _():
                self.stage(s, j)

    def plain(self, src, dst, send_sem, recv_sem, axis):
        return pltpu.make_async_remote_copy(
            src_ref=src,
            dst_ref=dst,
            send_sem=send_sem,
            recv_sem=recv_sem,
            device_id=self.partner(axis),
            device_id_type=pl.DeviceIdType.MESH,
        )

    def finish(self, t, jobs):
        def body(u, _):
            self.tick(u, jobs)
            return 0

        lax.fori_loop(t, jobs + self.depth - 1, body, 0)


def grad_arrays(red, grads):
    sizes, srcs, sums = [], [], []
    for g in grads:
        rows, cols = g.shape
        q = rows // (red.r * red.dp)
        sizes.append((q, cols // LANES))
        srcs.append(g.reshape((2,) * (red.nz + 1) + (q, red.r, cols)))
        sums.append(jax.ShapeDtypeStruct((q, red.r, cols), F32))
    return sizes, srcs, sums


def columns(i):
    return pl.ds(pl.multiple_of(i * LANES, LANES), LANES)


def bind_arrays(red, sizes, srcs, sums, scratch):
    def dispatch(j, body):
        base = 0
        for i, (q, wide) in enumerate(sizes):

            @pl.when((j >= base) & (j < base + q * wide))
            def _():
                at = j - base
                body(i, at // wide, columns(lax.rem(at, wide)))

            base += q * wide

    def source(j, red):
        core = lax.rem(red.me, 2)

        def body(i, q, lanes):
            cube = (slice(None),) * red.nz
            here = srcs[i].at[cube + (core, q, slice(None), lanes)]
            pltpu.make_async_copy(here, red.own, red.ssem.at[2 * red.stages + 2]).start()
            red.core_copy(lax.rem(j, 2), srcs[i].at[cube + (1 - core, q, slice(None), lanes)]).start()

        dispatch(j, body)

    def write(j, red):
        def body(i, q, lanes):
            pltpu.make_async_copy(red.ostage, sums[i].at[q, :, lanes], red.ssem.at[2 * red.stages + 3]).start()

        dispatch(j, body)

    red.bind(scratch, source, write)
    return sum(q * wide for q, wide in sizes)


def bind_tiles(red, tiles, write, scratch):
    core = lax.rem(lax.axis_index("dp"), 2)

    def source(slot, idx):
        if idx is None:
            return tiles.at[(slot,) + (slice(None),) * red.nz + (1 - core,)]
        return tiles[(slot,) + idx[: red.nz] + (core,) + idx[red.nz :]]

    red.bind(scratch, source, write)


def tile_scratch(red):
    return pltpu.VMEM((2,) + (2,) * (red.nz + 1) + (red.r, LANES), BF16)


def put_tile(red, tiles, slot, v):
    tiles[slot] = v.reshape((2,) * (red.nz + 1) + (red.r, LANES)).astype(BF16)


SCALE = HEAD_DIM**-0.5
SCALE2 = SCALE * LOG2E


def windows(r):
    return ((0, r), (r, r), (2 * r, 2 * r), (4 * r, 2 * r), (6 * r, r), (7 * r, r))


def head_masks(rows):
    left = lax.broadcasted_iota(jnp.int32, (rows, 128), 1) < 64
    return left, jnp.logical_not(left)


def only(mask, v):
    return jnp.where(mask, v, jnp.zeros_like(v))


def fill_shared(scratch, own_ref, halo_ref, r):
    for w in range(2):
        scratch[2 * r * w : 2 * r * w + r, :] = own_ref[(6 + w) * r : (7 + w) * r, :]
        scratch[2 * r * w + r : 2 * r * (w + 1), :] = halo_ref[r * w : r * (w + 1), :]


def attn_fwd_kernel(ok_ref, q_ref, k_ref, v_ref, kh_ref, vh_ref, o_ref, lse_ref, kc, vc):
    r = q_ref.shape[0] // 8
    fill_shared(kc, k_ref, kh_ref, r)
    fill_shared(vc, v_ref, vh_ref, r)
    col = lax.broadcasted_iota(jnp.int32, (1, 2 * r), 1)
    bias = jnp.where((col >= r) & (ok_ref[0] != 1), MASKED, 0.0)
    for w, (q0, qn) in enumerate(windows(r)):
        q = q_ref[q0 : q0 + qn, :]
        if w < 4:
            k, v = k_ref[q0 : q0 + qn, :], v_ref[q0 : q0 + qn, :]
        else:
            keys = slice(2 * r * (w - 4), 2 * r * (w - 3))
            k, v = kc[keys, :], vc[keys, :]
        masks = head_masks(qn)
        o, lse = [], []
        for mask in masks:
            s = dot(only(mask, q), k, 1, 1) * SCALE2
            if w >= 4:
                s = s + bias
            top = jnp.max(s, axis=-1, keepdims=True)
            e = jnp.exp2(s - top)
            total = jnp.sum(e, axis=-1, keepdims=True)
            o.append(dot(e.astype(BF16), v) * (1.0 / total))
            lse.append(top + jnp.log2(total))
        o_ref[q0 : q0 + qn, :] = jnp.where(masks[0], o[0], o[1]).astype(BF16)
        lse_ref[q0 : q0 + qn, :] = jnp.where(masks[0], lse[0], lse[1])


def attn_fwd(halo_ok, q, k, v, kh, vh):
    t, d = q.shape
    th = kh.shape[0]
    big = pl.BlockSpec((t, 128), lambda n: (0, n))
    small = pl.BlockSpec((th, 128), lambda n: (0, n))
    return pl.pallas_call(
        attn_fwd_kernel,
        grid=(d // 128,),
        in_specs=[pl.BlockSpec(memory_space=pltpu.SMEM), big, big, big, small, small],
        out_specs=[big, big],
        out_shape=[jax.ShapeDtypeStruct((t, d), BF16), jax.ShapeDtypeStruct((t, d), F32)],
        scratch_shapes=[pltpu.VMEM((2 * th, 128), BF16)] * 2,
        compiler_params=params(),
        name="attn_fwd",
        cost_estimate=pl.CostEstimate(flops=t * t * d, bytes_accessed=12 * t * d, transcendentals=t * t * 3),
    )(halo_ok, q, k, v, kh, vh)


def attn_bwd_kernel(n_red, sizes, red, ok_ref, q_ref, k_ref, v_ref, do_ref, lse_ref, kh_ref, vh_ref, *refs):
    srcs, (dq_ref, dk_ref, dv_ref), sums = refs[:n_red], refs[n_red : n_red + 3], refs[n_red + 3 : 2 * n_red + 3]
    kc, vc, own, hsend, hrecv, hsem, *scratch = refs[2 * n_red + 3 :]
    step, steps = pl.program_id(0), pl.num_programs(0)
    slot = lax.rem(step, 2)
    r = q_ref.shape[0] // 8
    jobs = bind_arrays(red, sizes, srcs, sums, scratch)

    @pl.when(step == 0)
    def _():
        red.barrier()

    fill_shared(kc, k_ref, kh_ref, r)
    fill_shared(vc, v_ref, vh_ref, r)
    row = lax.broadcasted_iota(jnp.int32, (2 * r, 1), 0)
    bias = jnp.where((row >= r) & (ok_ref[0] != 1), MASKED, 0.0)

    def window(w):
        q0, qn = windows(r)[w]
        rows = slice(q0, q0 + qn)
        q, do = q_ref[rows, :], do_ref[rows, :]
        if w < 4:
            k, v = k_ref[rows, :], v_ref[rows, :]
        else:
            keys = slice(2 * r * (w - 4), 2 * r * (w - 3))
            k, v = kc[keys, :], vc[keys, :]
        lse = jnp.transpose(lse_ref[rows, :])
        masks = head_masks(qn)
        dq, dk, dv = [], [], []
        for h, mask in enumerate(masks):
            s = dot(k, only(mask, q), 1, 1) * SCALE2
            if w >= 4:
                s = s + bias
            p = jnp.exp2(s - lse[64 * h : 64 * h + 1, :])
            dp = dot(v, only(mask, do), 1, 1)
            total = jnp.sum(p * dp, axis=0, keepdims=True)
            ds = (p * (dp - total)).astype(BF16)
            dv.append(dot(p.astype(BF16), do))
            dk.append(dot(ds, q))
            dq.append(dot(ds, k, 0, 0))
        dq_ref[rows, :] = (jnp.where(masks[0], dq[0], dq[1]) * SCALE).astype(BF16)
        left = head_masks(k.shape[0])[0]
        return rows, jnp.where(left, dk[0], dk[1]) * SCALE, jnp.where(left, dv[0], dv[1])

    red.tick(2 * step, jobs)
    for w in (4, 5):
        part = slice(r * (w - 4), r * (w - 3))
        for i, v in enumerate(window(w)[1:]):
            own[i, part, :] = v[:r, :]
            hsend[i, part, :] = v[r:, :].astype(BF16)
    swap = red.plain(hsend, hrecv.at[slot], hsem.at[0], hsem.at[1 + slot], 0)
    swap.start()
    red.tick(2 * step + 1, jobs)
    for w in range(4):
        rows, dk, dv = window(w)
        dk_ref[rows, :] = dk.astype(BF16)
        dv_ref[rows, :] = dv.astype(BF16)
    swap.wait()
    for i, ref in enumerate((dk_ref, dv_ref)):
        ref[6 * r :, :] = (own[i] + hrecv[slot, i].astype(F32)).astype(BF16)

    @pl.when(step == steps - 1)
    def _():
        red.finish(2 * steps, jobs)


def attn_bwd(halo_ok, q, k, v, do, lse, kh, vh, grads):
    t, d = q.shape
    th = kh.shape[0]
    big = pl.BlockSpec((t, 128), lambda n: (0, n))
    small = pl.BlockSpec((th, 128), lambda n: (0, n))
    low = lax.axis_size("dp").bit_length() - 2
    rest = tuple(range(3, low + 1))
    red = Reduce(lax.axis_size("dp"), 1024, ((1, 2, *rest, 0), (2, 1, *rest, 0)), False)
    sizes, srcs, sums = grad_arrays(red, grads)
    out = pl.pallas_call(
        functools.partial(attn_bwd_kernel, len(srcs), sizes, red),
        grid=(d // 128,),
        in_specs=[pl.BlockSpec(memory_space=pltpu.SMEM)] + [big] * 5 + [small] * 2 + [ANY] * len(srcs),
        out_specs=[big] * 3 + [ANY] * len(srcs),
        out_shape=[jax.ShapeDtypeStruct((t, d), BF16)] * 3 + sums,
        scratch_shapes=[
            pltpu.VMEM((2 * th, 128), BF16),
            pltpu.VMEM((2 * th, 128), BF16),
            pltpu.VMEM((2, th, 128), F32),
            pltpu.VMEM((2, th, 128), BF16),
            pltpu.VMEM((2, 2, th, 128), BF16),
            pltpu.SemaphoreType.DMA((3,)),
        ]
        + red.scratch(),
        compiler_params=params(collective_id=2, has_side_effects=True),
        name="attn_bwd",
        cost_estimate=pl.CostEstimate(flops=3 * t * t * d, bytes_accessed=18 * t * d, transcendentals=t * t * 3),
    )(halo_ok, q, k, v, do, lse, kh, vh, *srcs)
    return out[:3], [s.reshape(-1) for s in out[3:]]


def mid_kernel(g_hbm, live_ref, att_ref, w_ref, x_ref, mod_ref, ao_ref, mid_ref, nm_ref, gw_ref, gm_ref, stage, sem):
    step = pl.program_id(0)
    band = lax.axis_index("band")
    live = live_ref[0].astype(F32)
    n_group = stage.shape[0]
    per = n_group // 4
    rows = gw_ref.shape[0] // per

    @pl.when(step == 0)
    def _():
        for s in range(n_group):
            spot_copy(g_hbm, stage, band, s, sem).start()

    attn_out = dot(att_ref[...], w_ref[...])
    middle = x_ref[...].astype(F32) + (live * mod_ref[2:3, :]) * attn_out
    ao_ref[...] = attn_out
    mid_ref[...] = middle
    n, _ = norm_stats(middle)
    nm_ref[...] = (n * (1.0 + mod_ref[4:5, :]) + mod_ref[3:4, :]).astype(BF16)
    for i in range(per):
        s = step * per + i
        pltpu.make_async_copy(g_hbm.at[0, :, pl.ds(0, 4), pl.ds(0, 8), :], stage.at[s], sem.at[s]).wait()
        g = stage[s].astype(F32).reshape(rows, stage.shape[-1])
        part = pl.ds(i * rows, rows)
        gw_ref[part, :] = g.astype(BF16)
        gm_ref[part, :] = ((live * mod_ref[5:6, :]) * g).astype(BF16)


def mid(cot, live, attended, w_out, xw, mod):
    t, d = xw.shape
    frames = cot.shape[1]
    blk = pl.BlockSpec((t // 4, d), lambda m: (m, 0))
    bf, f32 = jax.ShapeDtypeStruct((t, d), BF16), jax.ShapeDtypeStruct((t, d), F32)
    return pl.pallas_call(
        mid_kernel,
        grid=(4,),
        in_specs=[ANY, pl.BlockSpec(memory_space=pltpu.SMEM), blk, whole((d, d)), blk, whole((6, d))],
        out_specs=[blk] * 5,
        out_shape=[f32, f32, bf, bf, bf],
        scratch_shapes=[pltpu.VMEM((8, frames, 4, 8, d), BF16), pltpu.SemaphoreType.DMA((8,))],
        compiler_params=params(),
        name="mid",
        cost_estimate=pl.CostEstimate(flops=2 * t * d * d, bytes_accessed=22 * t * d, transcendentals=0),
    )(cot, live, attended, w_out, xw, mod)


GELU_C = 0.7978845608
GELU_A = 0.044715


def col_sum(v):
    return jnp.sum(v, axis=0, keepdims=True)


def norm_back(h, n, r, gain):
    e = h * (1.0 + gain)
    return r * (e - jnp.mean(e, axis=-1, keepdims=True) - n * jnp.mean(e * n, axis=-1, keepdims=True))


def add_sums(ref, first, rows):
    sums = jnp.concatenate(rows + [jnp.zeros((ref.shape[0] - len(rows), ref.shape[1]), F32)], axis=0)

    @pl.when(first)
    def _():
        ref[...] = sums

    @pl.when(jnp.logical_not(first))
    def _():
        ref[...] += sums


def put_groups(out, stage, out_hbm, sem, block, blocks):
    band = lax.axis_index("band")
    n_group = stage.shape[0]
    per = n_group // blocks
    rows = out.shape[0] // per
    for k in range(blocks):

        @pl.when(block == k)
        def _():
            for i in range(per):
                s = k * per + i
                stage[s] = out[i * rows : (i + 1) * rows, :].reshape(stage.shape[1:]).astype(BF16)
                spot_copy(out_hbm, stage, band, s, sem, out=True).start()

    @pl.when(block == blocks - 1)
    def _():
        for s in range(n_group):
            spot_copy(out_hbm, stage, band, s, sem, out=True).wait()


def ff_kernel(
    n_ff, red, live_ref, nm_ref, gm_ref, wu_ref, wd_ref, mid_ref, g_ref, ao_ref, mod_ref, wo_ref,
    out_hbm, gmid_ref, ga_ref, do_ref, sums_ref, dwd_ref, gup_hbm,
    mo, h, hid, gp, nmt, tiles, stage, sem, *scratch,
):
    step, steps = pl.program_id(0), pl.num_programs(0)
    t = nm_ref.shape[0]
    chunk = t // 4

    def write(j, red):
        pltpu.make_async_copy(red.ostage, gup_hbm.at[:, columns(j)], red.ssem.at[2 * red.stages + 3]).start()

    bind_tiles(red, tiles, write, scratch)

    @pl.when(step == 0)
    def _():
        red.barrier()
        mo[...] = jnp.zeros_like(mo)
        h[...] = jnp.zeros_like(h)
        nmt[...] = jnp.transpose(nm_ref[...])

    red.tick(step - 1, n_ff)

    @pl.when(step < n_ff)
    def _():
        def rows(i, _):
            part = pl.ds(pl.multiple_of(i * chunk, chunk), chunk)
            v = dot(nm_ref[part, :], wu_ref[...])
            gh = dot(gm_ref[part, :], wd_ref[...], 1, 1)
            v2 = v * v
            th = jnp.tanh(v * (GELU_C + (GELU_C * GELU_A) * v2))
            half = 0.5 * th + 0.5
            hidden = (v * half).astype(BF16)
            slope = half + (0.5 * v) * (1.0 - th * th) * (GELU_C + (3.0 * GELU_C * GELU_A) * v2)
            gpre = (gh * slope).astype(BF16)
            hid[part, :] = hidden
            gp[part, :] = gpre
            mo[part, :] += dot(hidden, wd_ref[...])
            h[part, :] += dot(gpre, wu_ref[...], 1, 1)
            return 0

        lax.fori_loop(0, 4, rows, 0)
        put_tile(red, tiles, lax.rem(step, 2), dot(nmt[...], gp[...]))
        dwd_ref[...] = dot(hid[...], gm_ref[...], 0, 0).astype(BF16)

    @pl.when(step >= n_ff)
    def _():
        block = step - n_ff
        part = pl.ds(pl.multiple_of(block * chunk, chunk), chunk)
        live = live_ref[0].astype(F32)
        middle, g = mid_ref[...], g_ref[...].astype(F32)
        mlp_out, hh = mo[part, :], h[part, :]
        n, r = norm_stats(middle)
        gmid = g + norm_back(hh, n, r, mod_ref[4:5, :])
        gmid_ref[...] = gmid
        ga = ((live * mod_ref[2:3, :]) * gmid).astype(BF16)
        ga_ref[...] = ga
        do_ref[...] = dot(ga, wo_ref[...], 1, 1).astype(BF16)
        sums = [col_sum(live * ao_ref[...] * gmid), col_sum(hh), col_sum(hh * n), col_sum(live * mlp_out * g)]
        add_sums(sums_ref, block == 0, sums)
        put_groups(middle + (live * mod_ref[5:6, :]) * mlp_out, stage, out_hbm, sem, block, 4)

    @pl.when(step == steps - 1)
    def _():
        red.finish(steps - 1, n_ff)


def feed_forward(live, nm, gm, w_up, w_down, middle, gw, ao, mod, w_out, like):
    t, d = nm.shape
    ff = w_up.shape[1]
    n_ff = ff // LANES
    frames = like.shape[1]
    low = lax.axis_size("dp").bit_length() - 2
    rest = tuple(range(2, low + 1))
    red = Reduce(lax.axis_size("dp"), d, ((0, 1, *rest), (1, 0, *rest)), True)
    blk = pl.BlockSpec((t // 4, d), lambda i: (jnp.maximum(i - n_ff, 0), 0))
    up_tile = pl.BlockSpec((d, LANES), lambda i: (0, jnp.minimum(i, n_ff - 1)))
    down_tile = pl.BlockSpec((LANES, d), lambda i: (jnp.minimum(i, n_ff - 1), 0))
    bf, f32 = jax.ShapeDtypeStruct((t, d), BF16), jax.ShapeDtypeStruct((t, d), F32)
    return pl.pallas_call(
        functools.partial(ff_kernel, n_ff, red),
        grid=(n_ff + 4,),
        in_specs=[pl.BlockSpec(memory_space=pltpu.SMEM), whole((t, d)), whole((t, d)), up_tile, down_tile]
        + [blk, blk, blk, whole((6, d)), whole((d, d))],
        out_specs=[ANY, blk, blk, blk, pl.BlockSpec((8, d), lambda i: (0, 0)), down_tile, ANY],
        out_shape=[jax.ShapeDtypeStruct(like.shape, BF16), f32, bf, bf, jax.ShapeDtypeStruct((8, d), F32)]
        + [jax.ShapeDtypeStruct((ff, d), BF16), jax.ShapeDtypeStruct((red.r, ff), F32)],
        scratch_shapes=[
            pltpu.VMEM((t, d), F32),
            pltpu.VMEM((t, d), F32),
            pltpu.VMEM((t, LANES), BF16),
            pltpu.VMEM((t, LANES), BF16),
            pltpu.VMEM((d, t), BF16),
            tile_scratch(red),
            pltpu.VMEM((8, frames, 4, 8, d), BF16),
            pltpu.SemaphoreType.DMA((8,)),
        ]
        + red.scratch(),
        compiler_params=params(collective_id=1, has_side_effects=True),
        name="feed_forward",
        cost_estimate=pl.CostEstimate(flops=12 * t * d * ff, bytes_accessed=8 * d * ff + 12 * t * d, transcendentals=t * ff),
    )(live, nm, gm, w_up, w_down, middle, gw, ao, mod, w_out)


def outer_kernel(a_ref, b_ref, o_ref):
    o_ref[...] = dot(a_ref[...], b_ref[...], 0, 0).astype(BF16)


def outer(a, b):
    t, d = a.shape
    tile = 512
    return pl.pallas_call(
        outer_kernel,
        grid=(b.shape[1] // tile,),
        in_specs=[whole((t, d)), pl.BlockSpec((t, tile), lambda n: (0, n))],
        out_specs=pl.BlockSpec((d, tile), lambda n: (0, n)),
        out_shape=jax.ShapeDtypeStruct((d, b.shape[1]), BF16),
        compiler_params=params(),
        name="outer",
        cost_estimate=pl.CostEstimate(flops=2 * t * d * b.shape[1], bytes_accessed=6 * t * d, transcendentals=0),
    )(a, b)


def final_kernel(
    n_outer, red, nd_ref, *refs
):
    cols, rows = refs[:3], refs[3:6]
    wq_ref, wk_ref, wv_ref, x_ref, gmid_ref, mod_ref, out_hbm, sums_ref, gq_hbm, gk_hbm, gv_hbm = refs[6:17]
    ndt, tiles, stage, sem, *scratch = refs[17:]
    step, steps = pl.program_id(0), pl.num_programs(0)
    per = n_outer // 3

    def write(j, red):
        for i, ref in enumerate((gq_hbm, gk_hbm, gv_hbm)):

            @pl.when(j // per == i)
            def _():
                pltpu.make_async_copy(red.ostage, ref.at[:, columns(lax.rem(j, per))], red.ssem.at[2 * red.stages + 3]).start()

    bind_tiles(red, tiles, write, scratch)

    @pl.when(step == 0)
    def _():
        red.barrier()
        ndt[...] = jnp.transpose(nd_ref[...])

    red.tick(step - 1, n_outer)
    for i in range(3):

        @pl.when(step // per == i)
        def _():
            put_tile(red, tiles, lax.rem(step, 2), dot(ndt[...], cols[i][...]))

    @pl.when(step >= n_outer)
    def _():
        dq, dk, dv = (ref[...] for ref in rows)
        h = dot(dq, wq_ref[...], 1, 1) + dot(dk, wk_ref[...], 1, 1) + dot(dv, wv_ref[...], 1, 1)
        n, r = norm_stats(x_ref[...].astype(F32))
        add_sums(sums_ref, step == n_outer, [col_sum(h), col_sum(h * n)])
        put_groups(gmid_ref[...] + norm_back(h, n, r, mod_ref[1:2, :]), stage, out_hbm, sem, step - n_outer, 4)

    @pl.when(step == steps - 1)
    def _():
        red.finish(steps - 1, n_outer)


def final(normed, dq, dk, dv, wq, wk, wv, xw, gmid, mod, like):
    t, d = xw.shape
    frames = like.shape[1]
    per = d // LANES
    n_outer = 3 * per
    low = lax.axis_size("dp").bit_length() - 2
    rest = tuple(range(2, low + 1))
    red = Reduce(lax.axis_size("dp"), d, ((0, 1, *rest), (1, 0, *rest)), True)

    def col_spec(i):
        return pl.BlockSpec((t, LANES), lambda n: (0, jnp.clip(n - i * per, 0, per - 1)))

    blk = pl.BlockSpec((t // 4, d), lambda n: (jnp.maximum(n - n_outer, 0), 0))
    out = pl.pallas_call(
        functools.partial(final_kernel, n_outer, red),
        grid=(n_outer + 4,),
        in_specs=[whole((t, d))] + [col_spec(i) for i in range(3)] + [blk] * 3 + [whole((d, d))] * 3 + [blk, blk, whole((6, d))],
        out_specs=[ANY, pl.BlockSpec((8, d), lambda n: (0, 0))] + [ANY] * 3,
        out_shape=[jax.ShapeDtypeStruct(like.shape, BF16), jax.ShapeDtypeStruct((8, d), F32)]
        + [jax.ShapeDtypeStruct((red.r, d), F32)] * 3,
        scratch_shapes=[
            pltpu.VMEM((d, t), BF16),
            tile_scratch(red),
            pltpu.VMEM((8, frames, 4, 8, d), BF16),
            pltpu.SemaphoreType.DMA((8,)),
        ]
        + red.scratch(),
        compiler_params=params(collective_id=3, has_side_effects=True),
        name="final",
        cost_estimate=pl.CostEstimate(flops=12 * t * d * d, bytes_accessed=14 * t * d, transcendentals=0),
    )(normed, dq, dk, dv, dq, dk, dv, wq, wk, wv, xw, gmid, mod)
    return out[0], out[1], [g.reshape(-1) for g in out[2:]]


def band_swap(v):
    return lax.ppermute(v, "band", [(0, 1), (1, 0)])


def on_device(
    block_input, modulation, band_live, w_query, w_key, w_value, w_out, w_up, w_down, cotangent
):
    assert lax.axis_size("band") == 2 and block_input.shape[2:4] == (16, 16)
    band = lax.axis_index("band")
    flags = band_live[0]
    live_own = lax.dynamic_index_in_dim(flags, band, keepdims=True)
    live_other = lax.dynamic_index_in_dim(flags, 1 - band, keepdims=True)
    live = (live_own == 1).astype(jnp.int32)
    halo_ok = ((live_other == 1) | (live_own != 1)).astype(jnp.int32)
    mod = modulation[0]

    edge = lax.dynamic_slice_in_dim(block_input[0], 12 - 12 * band, 4, axis=1)
    x_halo = band_swap(edge)
    xw, normed, q, k, v = pre(block_input, mod, (w_query, w_key, w_value), 8, True)
    kh, vh = pre(x_halo, mod, (w_key, w_value), 2, False)
    attended, lse = attn_fwd(halo_ok, q, k, v, kh, vh)
    ao, middle, nm, gw, gm = mid(cotangent, live, attended, w_out, xw, mod)
    block_output, gmid, ga, do, sums_m, d_down, g_up = feed_forward(
        live, nm, gm, w_up, w_down, middle, gw, ao, mod, w_out, block_input
    )
    d_out = outer(attended, ga)
    (dq, dk, dv), (g_down, g_out) = attn_bwd(halo_ok, q, k, v, do, lse, kh, vh, (d_down, d_out))
    grad_input, sums_a, (g_query, g_key, g_value) = final(
        normed, dq, dk, dv, w_query, w_key, w_value, xw, gmid, mod, block_input
    )
    mod_part = jnp.concatenate([sums_a[0:2], sums_m[0:4]])
    mod_total = mod_part + band_swap(mod_part)
    return block_output, grad_input, mod_total[None], g_query, g_key, g_value, g_out, g_up.reshape(-1), g_down


def solution(mesh):
    return jax.shard_map(
        on_device,
        mesh=mesh,
        in_specs=(
            P("dp", None, "band", None, None),
            P("dp", None, None),
            P("dp", None),
            P(),
            P(),
            P(),
            P(),
            P(),
            P(),
            P("dp", None, "band", None, None),
        ),
        out_specs=(
            P("dp", None, "band", None, None),
            P("dp", None, "band", None, None),
            P("dp", None, None),
            P("dp"),
            P("dp"),
            P("dp"),
            P("dp"),
            P("dp"),
            P("dp"),
        ),
        check_vma=False,
    )
```

```python
import functools

import jax
import jax.numpy as jnp
from jax import lax
from jax.experimental import pallas as pl
from jax.experimental.pallas import tpu as pltpu
from jax.sharding import PartitionSpec as P

HEADS = 16
HEAD_DIM = 64
EPS = 1e-06
MASKED = -1e30
LOG2E = 1.4426950408889634
F32 = jnp.float32
BF16 = jnp.bfloat16
ANY = pl.BlockSpec(memory_space=pl.ANY)
VMEM_LIMIT = 60 * 1024 * 1024

MID_SPOTS = ((1, 0), (2, 0), (1, 1), (2, 1))


def group_spot(band, s):
    lone = 3 * band
    paired = 3 - 3 * band
    if s < 2:
        return lone, s
    if s < 6:
        return MID_SPOTS[s - 2]
    return paired, s - 6


def params(limit=VMEM_LIMIT, **kw):
    return pltpu.CompilerParams(vmem_limit_bytes=limit, **kw)


def dot(a, b, ca=1, cb=0):
    return lax.dot_general(a, b, (((ca,), (cb,)), ((), ())), preferred_element_type=F32)


def whole(shape):
    return pl.BlockSpec(shape, lambda *_: (0,) * len(shape), pipeline_mode=pl.Buffered(1))


def norm_stats(v):
    c = v - jnp.mean(v, axis=-1, keepdims=True)
    r = lax.rsqrt(jnp.mean(c * c, axis=-1, keepdims=True) + EPS)
    return c * r, r


def spot_copy(hbm, vmem, band, s, sem, out=False):
    g, j = group_spot(band, s)
    there = hbm.at[0, :, pl.ds(g * 4, 4), pl.ds(j * 8, 8), :]
    if out:
        slot = s % vmem.shape[0]
        return pltpu.make_async_copy(vmem.at[slot], there, sem.at[slot])
    return pltpu.make_async_copy(there, vmem.at[s], sem.at[s])


def pre_kernel(n_group, from_spots, x_hbm, mod_ref, *refs):
    n_mat = (len(refs) - 5) // 2 if from_spots else (len(refs) - 3) // 2
    w_refs = refs[:n_mat]
    outs = refs[n_mat:]
    if from_spots:
        xw_ref, normed_ref = outs[:2]
        o_refs = outs[2 : 2 + n_mat]
    else:
        o_refs = outs[:n_mat]
    stage, sem, nsc = outs[-3:] if not from_spots else outs[-3:]
    rows = nsc.shape[0] // n_group

    @pl.when(pl.program_id(0) == 0)
    def _():
        band = lax.axis_index("band")
        if from_spots:
            copies = [spot_copy(x_hbm, stage, band, s, sem) for s in range(n_group)]
        else:
            copies = [
                pltpu.make_async_copy(x_hbm.at[:, :, pl.ds(8 * s, 8), :], stage.at[s], sem.at[s])
                for s in range(n_group)
            ]
        for c in copies:
            c.start()
        for s in range(n_group):
            copies[s].wait()
            x = stage[s].astype(F32).reshape(rows, stage.shape[-1])
            n, _ = norm_stats(x)
            part = pl.ds(s * rows, rows)
            nsc[part, :] = (n * (1.0 + mod_ref[1:2, :]) + mod_ref[0:1, :]).astype(BF16)
            if from_spots:
                xw_ref[part, :] = x.astype(BF16)
        if from_spots:
            normed_ref[...] = jnp.transpose(nsc[...])

    for w_ref, o_ref in zip(w_refs, o_refs):
        o_ref[...] = dot(nsc[...], w_ref[...]).astype(BF16)


def pre(x, mod, weights, n_group, from_spots):
    d = x.shape[-1]
    frames = x.shape[1] if from_spots else x.shape[0]
    rows = frames * 32
    t = n_group * rows
    tile = 256
    o_tile = pl.BlockSpec((t, tile), lambda n: (0, n))
    full = pl.BlockSpec((t, d), lambda n: (0, 0))
    act = jax.ShapeDtypeStruct((t, d), BF16)
    k = len(weights)
    head = [act, jax.ShapeDtypeStruct((d, t), BF16)] if from_spots else []
    return pl.pallas_call(
        functools.partial(pre_kernel, n_group, from_spots),
        grid=(d // tile,),
        in_specs=[ANY, whole((6, d))] + [pl.BlockSpec((d, tile), lambda n: (0, n))] * k,
        out_specs=[full, whole((d, t))][: len(head)] + [o_tile] * k,
        out_shape=head + [act] * k,
        scratch_shapes=[
            pltpu.VMEM((n_group, frames, 4, 8, d), BF16),
            pltpu.SemaphoreType.DMA((n_group,)),
            pltpu.VMEM((t, d), BF16),
        ],
        compiler_params=params(),
        name="pre" if from_spots else "pre_halo",
        cost_estimate=pl.CostEstimate(
            flops=2 * t * d * d * k, bytes_accessed=2 * (k * d * d + (k + 3) * t * d), transcendentals=0
        ),
    )(x, mod, *weights)


LANES = 512


class Reduce:
    def __init__(self, dp, total_rows, orders, tiles_only):
        self.bits = list(range(dp.bit_length() - 2, 0, -1))
        self.nz = len(self.bits)
        self.stages = self.nz + 1
        self.depth = self.stages + 4
        self.r = total_rows // dp
        self.orders = orders
        self.tiles_only = tiles_only
        self.dp = dp

    def scratch(self):
        r, nz, k = self.r, self.nz, self.stages
        out = [] if self.tiles_only else [pltpu.VMEM((1 << nz, r, LANES), BF16)]
        out += [pltpu.VMEM((2, 1 << nz, r, LANES), BF16)]
        for _ in range(2):
            for i in range(k):
                block = (2,) * (k - 1 - i) + (r, 128)
                out += [pltpu.VMEM(block, BF16), pltpu.VMEM(block, BF16), pltpu.VMEM((2,) + block, BF16)]
        out += [pltpu.VMEM((2, r, 128), BF16), pltpu.VMEM((2, 2, r, 128), BF16), pltpu.VMEM((r, LANES), F32)]
        out += [pltpu.SemaphoreType.DMA((2 * k + 4,)), pltpu.SemaphoreType.DMA((2 * k + 2, 2))]
        return out

    def bind(self, refs, jobs, tiles):
        refs = list(refs)
        cube = (2,) * self.nz
        self.own = tiles.at[0, :, 0] if self.tiles_only else refs.pop(0)
        self.got_core = refs.pop(0)
        self.got_cube = self.got_core.reshape((2,) + cube + (self.r, LANES))
        if self.tiles_only:
            self.tile_cube = tiles.reshape((2,) + cube + (2, self.r, LANES))
        else:
            self.own_cube = self.own.reshape(cube + (self.r, LANES))
        self.send, self.keep, self.got = {}, {}, {}
        for p in range(2):
            for i in range(self.stages):
                self.send[p, i], self.keep[p, i], self.got[p, i] = refs.pop(0), refs.pop(0), refs.pop(0)
        self.fin, self.got_fin, self.ostage, self.ssem, self.rsem = refs
        self.jobs = jobs
        self.starts = [job[0] for job in jobs]
        self.me, self.band = lax.axis_index("dp"), lax.axis_index("band")

    def place(self, axis):
        return self.band if axis == 0 else lax.rem(self.me // (1 << axis), 2)

    def partner(self, axis):
        if axis == 0:
            return (self.me, 1 - self.band)
        bit = 1 if axis == -1 else 1 << axis
        here = lax.rem(self.me // bit, 2)
        return (self.me + bit - 2 * bit * here, self.band)

    def barrier(self):
        sem = pltpu.get_barrier_semaphore()
        everyone = [-1, 0] + self.bits
        for axis in everyone:
            pl.semaphore_signal(sem, inc=1, device_id=self.partner(axis), device_id_type=pl.DeviceIdType.MESH)
        pl.semaphore_wait(sem, len(everyone))

    def remote(self, src, dst, s, slot, axis):
        return pltpu.make_async_remote_copy(
            src_ref=src,
            dst_ref=dst,
            send_sem=self.ssem.at[s],
            recv_sem=self.rsem.at[s, slot],
            device_id=self.partner(axis),
            device_id_type=pl.DeviceIdType.MESH,
        )

    def core_copy(self, slot, src):
        return self.remote(src, self.got_core.at[slot], 2 * self.stages, slot, -1)

    def part_copy(self, p, i, slot):
        return self.remote(self.send[p, i], self.got[p, i].at[slot], 2 * i + p, slot, self.orders[p][i])

    def fin_copy(self, slot):
        return self.remote(self.fin, self.got_fin.at[slot], 2 * self.stages + 1, slot, 0)

    def pick(self, axes, axis, at):
        return tuple(at if a == axis else slice(None) for a in axes)

    def split_core(self, j, p):
        slot = lax.rem(j, 2)
        first = self.orders[p][0]
        mine = self.place(first)
        for dst, at in ((self.send[p, 0], 1 - mine), (self.keep[p, 0], mine)):
            if first == 0:
                lanes = pl.ds(pl.multiple_of((2 * p + at) * 128, 128), 128)
                idx = (slice(None),) * (self.nz + 1) + (lanes,)
                dst[...] = self.mine(slot, idx) + self.got_cube[(slot,) + idx]
            else:
                for b in range(2):
                    lanes = slice((2 * p + b) * 128, (2 * p + b + 1) * 128)
                    idx = self.pick(self.bits, first, at) + (slice(None), lanes)
                    dst[(slice(None),) * (self.nz - 1) + (b,)] = self.mine(slot, idx) + self.got_cube[(slot,) + idx]

    def split(self, j, p, i):
        slot = lax.rem(j, 2)
        axes = [a for a in self.bits + [0] if a not in self.orders[p][:i]]
        axis = self.orders[p][i]
        mine = self.place(axis)
        for dst, at in ((self.send[p, i], 1 - mine), (self.keep[p, i], mine)):
            idx = self.pick(axes, axis, at)
            dst[...] = self.keep[p, i - 1][idx] + self.got[p, i - 1][(slot,) + idx]

    def stage(self, s, j):
        k = self.stages
        slot = lax.rem(j, 2)
        if s == 0:
            self.each(j, 1)
        elif s == 1:
            self.core_copy(slot, self.own).wait()
            if not self.tiles_only:
                self.own_copy(self.own).wait()
            for p in range(2):
                self.split_core(j, p)
                self.part_copy(p, 0, slot).start()
        elif s <= k:
            for p in range(2):
                self.part_copy(p, s - 2, slot).wait()
                self.split(j, p, s - 1)
                self.part_copy(p, s - 1, slot).start()
        elif s == k + 1:
            for p in range(2):
                self.part_copy(p, k - 1, slot).wait()
                self.fin[p] = self.keep[p, k - 1][...] + self.got[p, k - 1][slot]
            self.fin_copy(slot).start()
        elif s == k + 2:
            self.fin_copy(slot).wait()
            for p in range(2):
                mine = pl.ds(pl.multiple_of((2 * p + self.band) * 128, 128), 128)
                other = pl.ds(pl.multiple_of((2 * p + 1 - self.band) * 128, 128), 128)
                self.ostage[:, mine] = self.fin[p].astype(F32)
                self.ostage[:, other] = self.got_fin[slot, p].astype(F32)
            self.each(j, 2)
        else:
            self.out_copy(self.ostage).wait()

    def each(self, j, part):
        for i, job in enumerate(self.jobs):
            pl.when(j == i)(functools.partial(job[part], self, i % 2))

    def own_copy(self, src):
        return pltpu.make_async_copy(src, self.own, self.ssem.at[2 * self.stages + 2])

    def out_copy(self, dst, src=None):
        return pltpu.make_async_copy(self.ostage if src is None else src, dst, self.ssem.at[2 * self.stages + 3])

    def mine(self, slot, idx):
        if self.tiles_only:
            return self.tile_cube[(slot,) + idx[: self.nz] + (lax.rem(self.me, 2),) + idx[self.nz :]]
        return self.own_cube[idx]

    def start_pair(self, slot, ref, at):
        core = lax.rem(self.me, 2)
        if not self.tiles_only:
            self.own_copy(ref.at[(slice(None), core) + at]).start()
        self.core_copy(slot, ref.at[(slice(None), 1 - core) + at]).start()

    def tick(self, t):
        for s in reversed(range(self.depth)):
            u = t - s
            before = sum(jnp.where(u > at, 1, 0) for at in self.starts)
            upto = sum(jnp.where(u >= at, 1, 0) for at in self.starts)

            @pl.when(upto > before)
            def _():
                self.stage(s, before)

    def plain(self, src, dst, send_sem, recv_sem, axis):
        return pltpu.make_async_remote_copy(
            src_ref=src,
            dst_ref=dst,
            send_sem=send_sem,
            recv_sem=recv_sem,
            device_id=self.partner(axis),
            device_id_type=pl.DeviceIdType.MESH,
        )


def cube_shape(red, rows, cols):
    return (red.dp // 2, 2, rows // (red.r * red.dp), red.r, cols)


def lanes_at(i, width=LANES):
    return slice(i * width, (i + 1) * width)


def array_job(start, src, dst, q, i, q_out=None):
    def begin(red, slot):
        red.start_pair(slot, src, (q, slice(None), lanes_at(i)))

    def end(red, slot):
        red.out_copy(dst.at[q if q_out is None else q_out, :, lanes_at(i)]).start()

    return start, begin, end


def tile_job(start, tiles, at, parts):
    width = LANES // len(parts)

    def begin(red, slot):
        red.start_pair(slot, tiles.at[at], ())

    def end(red, slot):
        for n, dst in enumerate(parts):
            red.out_copy(dst, red.ostage.at[:, lanes_at(n, width)]).start()

    return start, begin, end


def tile_scratch(red):
    return pltpu.VMEM((2, red.dp // 2, 2, red.r, LANES), BF16)


def put_tile(red, tiles, slot, v):
    tiles[slot] = v.reshape(tiles.shape[1:]).astype(BF16)


SCALE = HEAD_DIM**-0.5
SCALE2 = SCALE * LOG2E


def windows(r):
    return ((0, r), (r, r), (2 * r, 2 * r), (4 * r, 2 * r), (6 * r, r), (7 * r, r))


def head_masks(rows):
    left = lax.broadcasted_iota(jnp.int32, (rows, 128), 1) < 64
    return left, jnp.logical_not(left)


def only(mask, v):
    return jnp.where(mask, v, jnp.zeros_like(v))


def fill_shared(scratch, own_ref, halo_ref, r):
    for w in range(2):
        scratch[2 * r * w : 2 * r * w + r, :] = own_ref[(6 + w) * r : (7 + w) * r, :]
        scratch[2 * r * w + r : 2 * r * (w + 1), :] = halo_ref[r * w : r * (w + 1), :]


def attn_fwd_kernel(ok_ref, q_ref, k_ref, v_ref, kh_ref, vh_ref, o_ref, lse_ref, kc, vc):
    r = q_ref.shape[0] // 8
    fill_shared(kc, k_ref, kh_ref, r)
    fill_shared(vc, v_ref, vh_ref, r)
    col = lax.broadcasted_iota(jnp.int32, (1, 2 * r), 1)
    bias = jnp.where((col >= r) & (ok_ref[0] != 1), MASKED, 0.0)
    for w, (q0, qn) in enumerate(windows(r)):
        q = q_ref[q0 : q0 + qn, :]
        if w < 4:
            k, v = k_ref[q0 : q0 + qn, :], v_ref[q0 : q0 + qn, :]
        else:
            keys = slice(2 * r * (w - 4), 2 * r * (w - 3))
            k, v = kc[keys, :], vc[keys, :]
        masks = head_masks(qn)
        o, lse = [], []
        for mask in masks:
            s = dot(only(mask, q), k, 1, 1) * SCALE2
            if w >= 4:
                s = s + bias
            top = jnp.max(s, axis=-1, keepdims=True)
            e = jnp.exp2(s - top)
            total = jnp.sum(e, axis=-1, keepdims=True)
            o.append(dot(e.astype(BF16), v) * (1.0 / total))
            lse.append(top + jnp.log2(total))
        o_ref[q0 : q0 + qn, :] = jnp.where(masks[0], o[0], o[1]).astype(BF16)
        lse_ref[q0 : q0 + qn, :] = jnp.where(masks[0], lse[0], lse[1])


def attn_fwd(halo_ok, q, k, v, kh, vh):
    t, d = q.shape
    th = kh.shape[0]
    big = pl.BlockSpec((t, 128), lambda n: (0, n))
    small = pl.BlockSpec((th, 128), lambda n: (0, n))
    return pl.pallas_call(
        attn_fwd_kernel,
        grid=(d // 128,),
        in_specs=[pl.BlockSpec(memory_space=pltpu.SMEM), big, big, big, small, small],
        out_specs=[big, big],
        out_shape=[jax.ShapeDtypeStruct((t, d), BF16), jax.ShapeDtypeStruct((t, d), F32)],
        scratch_shapes=[pltpu.VMEM((2 * th, 128), BF16)] * 2,
        compiler_params=params(),
        name="attn_fwd",
        cost_estimate=pl.CostEstimate(flops=t * t * d, bytes_accessed=12 * t * d, transcendentals=t * t * 3),
    )(halo_ok, q, k, v, kh, vh)


def mid_kernel(
    g_hbm, live_ref, att_ref, w_ref, x_ref, mod_ref, ao_ref, mid_ref, nm_ref, nmt_ref, attt_ref, gw_ref, gm_ref, stage, sem
):
    step = pl.program_id(0)
    band = lax.axis_index("band")
    live = live_ref[0].astype(F32)
    n_group = stage.shape[0]
    rows = gw_ref.shape[0] // n_group

    @pl.when(step == 0)
    def _():
        for s in range(n_group):
            spot_copy(g_hbm, stage, band, s, sem).start()

    attn_out = dot(att_ref[...], w_ref[...])
    middle = x_ref[...].astype(F32) + (live * mod_ref[2:3, :]) * attn_out
    ao_ref[...] = attn_out.astype(BF16)
    mid_ref[...] = middle
    n, _ = norm_stats(middle)
    nm = (n * (1.0 + mod_ref[4:5, :]) + mod_ref[3:4, :]).astype(BF16)
    nm_ref[...] = nm
    nmt_ref[...] = jnp.transpose(nm)
    attt_ref[...] = jnp.transpose(att_ref[...])
    for k in range(4):

        @pl.when(step == k + 1)
        def _():
            for s in range(2 * k, 2 * k + 2):
                spot_copy(g_hbm, stage, band, s, sem).wait()
                g = stage[s].astype(F32).reshape(rows, stage.shape[-1])
                part = slice(s * rows, (s + 1) * rows)
                gw_ref[part, :] = g.astype(BF16)
                gm_ref[part, :] = ((live * mod_ref[5:6, :]) * g).astype(BF16)


def mid(cot, live, attended, w_out, xw, mod):
    t, d = xw.shape
    frames = cot.shape[1]
    blk = pl.BlockSpec((t // 5, d), lambda m: (m, 0))
    blk_t = pl.BlockSpec((d, t // 5), lambda m: (0, m))
    full = pl.BlockSpec((t, d), lambda m: (0, 0))
    bf, f32 = jax.ShapeDtypeStruct((t, d), BF16), jax.ShapeDtypeStruct((t, d), F32)
    bf_t = jax.ShapeDtypeStruct((d, t), BF16)
    return pl.pallas_call(
        mid_kernel,
        grid=(5,),
        in_specs=[ANY, pl.BlockSpec(memory_space=pltpu.SMEM), blk, whole((d, d)), blk, whole((6, d))],
        out_specs=[blk, blk, blk, blk_t, blk_t, full, full],
        out_shape=[bf, f32, bf, bf_t, bf_t, bf, bf],
        scratch_shapes=[pltpu.VMEM((8, frames, 4, 8, d), BF16), pltpu.SemaphoreType.DMA((8,))],
        compiler_params=params(),
        name="mid",
        cost_estimate=pl.CostEstimate(flops=2 * t * d * d, bytes_accessed=22 * t * d, transcendentals=0),
    )(cot, live, attended, w_out, xw, mod)


GELU_C = 0.7978845608
GELU_A = 0.044715


def col_sum(v):
    return jnp.sum(v, axis=0, keepdims=True)


def norm_back(h, n, r, gain):
    e = h * (1.0 + gain)
    return r * (e - jnp.mean(e, axis=-1, keepdims=True) - n * jnp.mean(e * n, axis=-1, keepdims=True))


def add_sums(ref, first, rows):
    sums = jnp.concatenate(rows + [jnp.zeros((ref.shape[0] - len(rows), ref.shape[1]), F32)], axis=0)

    @pl.when(first)
    def _():
        ref[...] = sums

    @pl.when(jnp.logical_not(first))
    def _():
        ref[...] += sums


def put_groups(out, stage, out_hbm, sem, block, blocks):
    band = lax.axis_index("band")
    slots = stage.shape[0]
    n_group = 8
    per = n_group // blocks
    rows = out.shape[0] // per
    for k in range(blocks):

        @pl.when(block == k)
        def _():
            for i in range(per):
                s = k * per + i
                if s >= slots:
                    spot_copy(out_hbm, stage, band, s - slots, sem, out=True).wait()
                stage[s % slots] = out[i * rows : (i + 1) * rows, :].reshape(stage.shape[1:]).astype(BF16)
                spot_copy(out_hbm, stage, band, s, sem, out=True).start()

    @pl.when(block == blocks - 1)
    def _():
        for s in range(n_group - slots, n_group):
            spot_copy(out_hbm, stage, band, s, sem, out=True).wait()


PIECES = 4


class Tiling:
    def __init__(self, ff, dp):
        self.steps = ff // LANES
        self.width = LANES // PIECES
        self.early = ff // dp == 2 * self.width

    def piece(self, i, k):
        if not self.early:
            return PIECES * i + k
        half = self.steps // 2
        return (i % half * PIECES + k) * 2 + i // half


def window_back(w, r, bias, q_ref, k_ref, v_ref, do_of, lse_ref, kc, vc):
    q0, qn = windows(r)[w]
    rows = slice(q0, q0 + qn)
    q, do = q_ref[rows, :], do_of(rows)
    if w < 4:
        k, v = k_ref[rows, :], v_ref[rows, :]
    else:
        keys = slice(2 * r * (w - 4), 2 * r * (w - 3))
        k, v = kc[keys, :], vc[keys, :]
    lse = jnp.transpose(lse_ref[rows, :])
    masks = head_masks(qn)
    dq, dk, dv = [], [], []
    for h, mask in enumerate(masks):
        s = dot(k, only(mask, q), 1, 1) * SCALE2
        if w >= 4:
            s = s + bias
        p = jnp.exp2(s - lse[64 * h : 64 * h + 1, :])
        dp = dot(v, only(mask, do), 1, 1)
        total = jnp.sum(p * dp, axis=0, keepdims=True)
        ds = (p * (dp - total)).astype(BF16)
        dv.append(dot(p.astype(BF16), do))
        dk.append(dot(ds, q))
        dq.append(dot(ds, k, 0, 0))
    left = head_masks(k.shape[0])[0]
    dq = jnp.where(masks[0], dq[0], dq[1]) * SCALE
    return rows, dq, jnp.where(left, dk[0], dk[1]) * SCALE, jnp.where(left, dv[0], dv[1])


TILES = ((("q", 0), ("k", 0)), (("v", 0), ("v", 1)), (("q", 1), ("k", 1)), (("q", 2), ("k", 2)), (("v", 2), ("v", 3)), (("q", 3), ("k", 3)))
TILE_SLOTS = (0, 0, 1, 0, 1, 0)
MADE = {2: (0,), 4: (1, 2), 6: (3,), 8: (4, 5)}


class Plan:
    def __init__(self, n_ff, n_att, early):
        self.n_ff, self.n_att = n_ff, n_att
        self.post = n_ff
        self.out = n_ff + 4
        self.att = self.out + 1
        self.fin = self.att + n_att
        self.steps = self.fin + 4
        self.end = self.fin + 8
        a = self.att
        self.up = [(0, i + 1) for i in range(n_ff)]
        self.o_proj = [(0, a), (1, a)]
        self.tiles = [(1, a + 2), (1, a + 4), (0, a + 5), (1, a + 6), (1, self.fin), (0, self.fin + 1)]
        late = [(1, n_ff + i) for i in range(4)]
        self.down = [(1, n_ff // 2 + i) for i in range(4)] + late if early else late + [(1, n_ff + 4)] + [(1, a + i) for i in (1, 3, 5)]


def finish(reds, first):
    def body(u, _):
        for red in reds:
            red.tick(u)
        return 0

    lax.fori_loop(first, max(red.starts[-1] + red.depth for red in reds), body, 0)


def core_kernel(
    til, plan, reds, live_ref, ok_ref, nm_hbm, gm_hbm, nmt_hbm, attt_hbm, ndt_hbm, wu_hbm, wo_hbm, wq_hbm,
    wd_ref, mid_ref, g_ref, ao_ref, mod_ref, wk_ref, wv_ref, q_ref, k_ref, v_ref, lse_ref, kh_ref, vh_ref, x_ref,
    out_hbm, gin_hbm, sums_ref, sums_a_ref, dwd_hbm, gup_hbm, gdown_hbm, gout_hbm, gq_hbm, gk_hbm, gv_hbm,
    buf_a, buf_b, buf_c, buf_t, mo, h, do_s, w0, wu, dwd, tiles, kc, vc, own, hsend, hrecv,
    hsem, wsem, lsem, stage, sem, *scratch,
):
    step, steps = pl.program_id(0), pl.num_programs(0)
    n_ff, n_att, width = plan.n_ff, plan.n_att, til.width
    t, d = mo.shape
    chunk = t // 4
    r = t // 8
    red = reds[0]

    def up_at(i, k):
        return pl.ds(pl.multiple_of(til.piece(i, k) * width, width), width)

    def load_up(i, k):
        slot = lax.rem(i, 2)
        return pltpu.make_async_copy(wu_hbm.at[:, up_at(i, k)], wu.at[slot, :, lanes_at(k, width)], wsem.at[slot, k])

    def store_down(i, k):
        if til.early:
            d_at = til.piece(i, k) // 2
            dst = dwd_hbm.at[d_at // 2, lax.rem(d_at, 2), pl.ds(2 * lax.rem(til.piece(i, k), 2), 2)]
        else:
            dst = dwd_hbm.at[pl.ds(til.piece(i, k) * width, width), :]
        return pltpu.make_async_copy(dwd.at[k], dst, wsem.at[2, k])

    def load(n):
        pairs = ((nm_hbm, buf_b), (gm_hbm, buf_c), (nmt_hbm, buf_t), (wo_hbm, w0), (attt_hbm, buf_t), (ndt_hbm, buf_t), (wq_hbm, w0))
        return pltpu.make_async_copy(*pairs[n], lsem.at[n])

    grad_of = {"q": (buf_a, gq_hbm), "k": (buf_b, gk_hbm), "v": (buf_c, gv_hbm)}
    cube = dwd_hbm if til.early else dwd_hbm.reshape(cube_shape(red, dwd_hbm.shape[0], d))
    wide = d // LANES
    jobs = ([], [])
    for i, (at, start) in enumerate(plan.up):
        jobs[at].append(tile_job(start, tiles, i % 2, [gup_hbm.at[:, lanes_at(til.piece(i, k), width)] for k in range(PIECES)]))
    for n, (at, start) in enumerate(plan.down):
        jobs[at].append(array_job(start, cube, gdown_hbm, n // wide, n % wide))
    for n, (at, start) in enumerate(plan.o_proj):
        jobs[at].append(tile_job(start, tiles, n, [gout_hbm.at[:, lanes_at(n)]]))
    for m, (at, start) in enumerate(plan.tiles):
        jobs[at].append(tile_job(start, tiles, TILE_SLOTS[m], [grad_of[n][1].at[:, lanes_at(i, 256)] for n, i in TILES[m]]))
    size = len(scratch) // 2
    for i in range(2):
        reds[i].bind(scratch[i * size : (i + 1) * size + i], sorted(jobs[i], key=lambda job: job[0]), tiles)
    red, later = reds

    def swap(i):
        slot = lax.rem(i, 2)
        return red.plain(hsend, hrecv.at[slot], hsem.at[0], hsem.at[1 + slot], 0)

    @pl.when(step == 0)
    def _():
        for k in range(PIECES):
            load_up(0, k).start()
        for n in range(4):
            load(n).start()
        mo[...] = jnp.zeros_like(mo)
        h[...] = jnp.zeros_like(h)
        red.barrier()
        load(0).wait()
        load(1).wait()

    @pl.when(step < n_ff)
    def _():
        slot = lax.rem(step, 2)
        red.tick(step)
        for k in range(PIECES):
            load_up(step, k).wait()

        @pl.when(step + 1 < n_ff)
        def _():
            for k in range(PIECES):
                load_up(step + 1, k).start()

        wd = wd_ref[...].reshape(LANES, d)
        up = wu.at[slot]

        def rows(i, _):
            part = pl.ds(pl.multiple_of(i * chunk, chunk), chunk)
            v = dot(buf_b[part, :], up[...])
            gh = dot(buf_c[part, :], wd, 1, 1)
            v2 = v * v
            th = jnp.tanh(v * (GELU_C + (GELU_C * GELU_A) * v2))
            half = 0.5 * th + 0.5
            hidden = (v * half).astype(BF16)
            slope = half + (0.5 * v) * (1.0 - th * th) * (GELU_C + (3.0 * GELU_C * GELU_A) * v2)
            gpre = (gh * slope).astype(BF16)
            buf_a[part, :LANES] = hidden
            buf_a[part, LANES : 2 * LANES] = gpre
            mo[part, :] += dot(hidden, wd)
            h[part, :] += dot(gpre, up[...], 1, 1)
            return 0

        lax.fori_loop(0, 3, rows, 0)

        @pl.when(step > 0)
        def _():
            for k in range(PIECES):
                store_down(step - 1, k).wait()

        later.tick(step)
        lax.fori_loop(3, 4, rows, 0)
        pl.when(step == 0)(lambda: load(2).wait())
        put_tile(red, tiles, slot, dot(buf_t[...], buf_a[:, LANES : 2 * LANES]))
        dwd[...] = dot(buf_a[:, :LANES], buf_c[...], 0, 0).reshape(dwd.shape).astype(BF16)
        for k in range(PIECES):
            store_down(step, k).start()

    @pl.when((step >= plan.post) & (step < plan.out))
    def _():
        block = step - plan.post

        @pl.when(block == 0)
        def _():
            load(4).start()
            load(3).wait()
            for k in range(PIECES):
                store_down(step - 1, k).wait()

        red.tick(step)
        part = pl.ds(pl.multiple_of(block * chunk, chunk), chunk)
        live = live_ref[0].astype(F32)
        middle, g = mid_ref[...], g_ref[...].astype(F32)
        mlp_out, hh = mo[part, :], h[part, :]
        n, rs = norm_stats(middle)
        gmid = g + norm_back(hh, n, rs, mod_ref[4:5, :])
        h[part, :] = gmid
        later.tick(step)
        ga = ((live * mod_ref[2:3, :]) * gmid).astype(BF16)
        buf_b[part, :] = ga
        do_s[part, :] = dot(ga, w0[...], 1, 1).astype(BF16)
        sums = [col_sum(live * ao_ref[...].astype(F32) * gmid), col_sum(hh), col_sum(hh * n), col_sum(live * mlp_out * g)]
        add_sums(sums_ref, block == 0, sums)
        put_groups(middle + (live * mod_ref[5:6, :]) * mlp_out, stage, out_hbm, sem, block, 4)

    @pl.when(step == plan.out)
    def _():
        red.tick(step)
        load(6).start()
        load(4).wait()
        for n in range(wide):
            put_tile(red, tiles, n, dot(buf_t[...], buf_b[:, lanes_at(n)]))
        load(5).start()
        later.tick(step)

    now = step - plan.att

    @pl.when((now >= 0) & (now < n_att))
    def _():
        red.tick(step)

    @pl.when((now > 0) & (now <= n_att))
    def _():
        swap(now - 1).wait()
        slot = lax.rem(now - 1, 2)
        lanes = pl.ds(pl.multiple_of((now - 1) * 128, 128), 128)
        for i, ref in enumerate((buf_b, buf_c)):
            ref[6 * r :, lanes] = (own[i] + hrecv[slot, i].astype(F32)).astype(BF16)

    for at, made in MADE.items():

        @pl.when(now == at)
        def _():
            if at == min(MADE):
                load(5).wait()
            for m in made:
                cols = [grad_of[n][0][:, lanes_at(i, 256)] for n, i in TILES[m]]
                put_tile(red, tiles, TILE_SLOTS[m], dot(buf_t[...], jnp.concatenate(cols, axis=1)))

    @pl.when((now >= 0) & (now < n_att))
    def _():
        slot = lax.rem(now, 2)
        lanes = pl.ds(pl.multiple_of(now * 128, 128), 128)
        fill_shared(kc, k_ref, kh_ref, r)
        fill_shared(vc, v_ref, vh_ref, r)
        row = lax.broadcasted_iota(jnp.int32, (2 * r, 1), 0)
        bias = jnp.where((row >= r) & (ok_ref[0] != 1), MASKED, 0.0)
        data = (r, bias, q_ref, k_ref, v_ref, lambda rows: do_s[rows, lanes], lse_ref, kc, vc)
        for w in (4, 5):
            part = slice(r * (w - 4), r * (w - 3))
            rows, dq, dk, dv = window_back(w, *data)
            buf_a[rows, lanes] = dq.astype(BF16)
            for i, v in enumerate((dk, dv)):
                own[i, part, :] = v[:r, :]
                hsend[i, part, :] = v[r:, :].astype(BF16)
        swap(now).start()
        later.tick(step)
        for w in range(4):
            rows, dq, dk, dv = window_back(w, *data)
            buf_a[rows, lanes] = dq.astype(BF16)
            buf_b[rows, lanes] = dk.astype(BF16)
            buf_c[rows, lanes] = dv.astype(BF16)

    @pl.when(step >= plan.fin)
    def _():
        i = step - plan.fin
        pl.when(i == 0)(lambda: load(6).wait())
        red.tick(plan.fin + 2 * i)
        part = pl.ds(pl.multiple_of(i * chunk, chunk), chunk)
        hh = dot(buf_a[part, :], w0[...], 1, 1)
        later.tick(plan.fin + 2 * i)
        hh = hh + dot(buf_b[part, :], wk_ref[...], 1, 1)
        red.tick(plan.fin + 2 * i + 1)
        hh = hh + dot(buf_c[part, :], wv_ref[...], 1, 1)
        later.tick(plan.fin + 2 * i + 1)
        n, rs = norm_stats(x_ref[...].astype(F32))
        add_sums(sums_a_ref, i == 0, [col_sum(hh), col_sum(hh * n)])
        put_groups(h[part, :] + norm_back(hh, n, rs, mod_ref[1:2, :]), stage, gin_hbm, sem, i, 4)

    @pl.when(step == steps - 1)
    def _():
        finish(reds, plan.end)


def core(live, halo_ok, nm, gm, nmt, attt, ndt, w_up, w_down, wo, wq, wk, wv, middle, gw, ao, mod, q, k, v, lse, kh, vh, xw, like):
    t, d = nm.shape
    ff = w_up.shape[1]
    th = kh.shape[0]
    frames = like.shape[1]
    dp = lax.axis_size("dp")
    til = Tiling(ff, dp)
    n_ff, n_att = til.steps, d // 128
    plan = Plan(n_ff, n_att, til.early)
    rest = tuple(range(3, dp.bit_length() - 1))
    reds = [Reduce(dp, d, ((0, 1, 2, *rest), (1, 2, 0, *rest)), i == 0) for i in range(2)]
    red = reds[0]

    def block_at(first, count):
        return lambda i: (jnp.clip(i - first, 0, count - 1), 0)

    def lane_at(i):
        return 0, jnp.clip(i - plan.att, 0, n_att - 1)

    post = pl.BlockSpec((t // 4, d), block_at(plan.post, 4))
    last = pl.BlockSpec((t // 4, d), block_at(plan.fin, 4), pipeline_mode=pl.Buffered(1))
    big, small = pl.BlockSpec((t, 128), lane_at), pl.BlockSpec((th, 128), lane_at)
    if til.early:
        half = n_ff // 2
        w_down = w_down.reshape(half, PIECES, 2, til.width, d)

        def down_at(i):
            i = jnp.minimum(i, n_ff - 1)
            return lax.rem(i, half), 0, i // half, 0, 0

        down = pl.BlockSpec((None, PIECES, None, til.width, d), down_at)
        cube, down_tile = cube_shape(red, ff, d), (PIECES, 2, red.r, d)
    else:
        down = pl.BlockSpec((LANES, d), block_at(0, n_ff))
        cube, down_tile = (ff, d), (PIECES, til.width, d)
    smem = pl.BlockSpec(memory_space=pltpu.SMEM)
    full = pl.BlockSpec((8, d), lambda i: (0, 0))
    image, sums = jax.ShapeDtypeStruct(like.shape, BF16), jax.ShapeDtypeStruct((8, d), F32)
    share = jax.ShapeDtypeStruct((red.r, d), F32)
    act, act32 = pltpu.VMEM((t, d), BF16), pltpu.VMEM((t, d), F32)
    return pl.pallas_call(
        functools.partial(core_kernel, til, plan, reds),
        grid=(plan.steps,),
        in_specs=[smem, smem] + [ANY] * 8 + [down, post, post, post, whole((6, d)), whole((d, d)), whole((d, d))]
        + [big] * 4 + [small] * 2 + [last],
        out_specs=[ANY, ANY, full, full] + [ANY] * 7,
        out_shape=[image, image, sums, sums, jax.ShapeDtypeStruct(cube, BF16), jax.ShapeDtypeStruct((red.r, ff), F32)]
        + [jax.ShapeDtypeStruct((ff // d, red.r, d), F32), share, share, share, share],
        scratch_shapes=[
            act,
            act,
            act,
            pltpu.VMEM((d, t), BF16),
            act32,
            act32,
            act,
            pltpu.VMEM((d, d), BF16),
            pltpu.VMEM((2, d, LANES), BF16),
            pltpu.VMEM(down_tile, BF16),
            tile_scratch(red),
            pltpu.VMEM((2 * th, 128), BF16),
            pltpu.VMEM((2 * th, 128), BF16),
            pltpu.VMEM((2, th, 128), F32),
            pltpu.VMEM((2, th, 128), BF16),
            pltpu.VMEM((2, 2, th, 128), BF16),
            pltpu.SemaphoreType.DMA((3,)),
            pltpu.SemaphoreType.DMA((3, PIECES)),
            pltpu.SemaphoreType.DMA((7,)),
            pltpu.VMEM((4, frames, 4, 8, d), BF16),
            pltpu.SemaphoreType.DMA((4,)),
        ]
        + reds[0].scratch()
        + reds[1].scratch(),
        compiler_params=params(limit=63 * 1024 * 1024, collective_id=1, has_side_effects=True),
        name="core",
        cost_estimate=pl.CostEstimate(
            flops=12 * t * d * (ff + d) + 3 * t * t * d, bytes_accessed=8 * d * ff + 60 * t * d, transcendentals=t * (ff + 3 * t)
        ),
    )(live, halo_ok, nm, gm, nmt, attt, ndt, w_up, wo, wq, w_down, middle, gw, ao, mod, wk, wv, q, k, v, lse, kh, vh, xw)


def band_swap(v):
    return lax.ppermute(v, "band", [(0, 1), (1, 0)])


def on_device(
    block_input, modulation, band_live, w_query, w_key, w_value, w_out, w_up, w_down, cotangent
):
    assert lax.axis_size("band") == 2 and block_input.shape[2:4] == (16, 16)
    band = lax.axis_index("band")
    flags = band_live[0]
    live_own = lax.dynamic_index_in_dim(flags, band, keepdims=True)
    live_other = lax.dynamic_index_in_dim(flags, 1 - band, keepdims=True)
    live = (live_own == 1).astype(jnp.int32)
    halo_ok = ((live_other == 1) | (live_own != 1)).astype(jnp.int32)
    mod = modulation[0]

    edge = lax.dynamic_slice_in_dim(block_input[0], 12 - 12 * band, 4, axis=1)
    x_halo = band_swap(edge)
    xw, ndt, q, k, v = pre(block_input, mod, (w_query, w_key, w_value), 8, True)
    kh, vh = pre(x_halo, mod, (w_key, w_value), 2, False)
    attended, lse = attn_fwd(halo_ok, q, k, v, kh, vh)
    ao, middle, nm, nmt, attt, gw, gm = mid(cotangent, live, attended, w_out, xw, mod)
    block_output, grad_input, sums_m, sums_a, _, g_up, g_down, g_out, g_query, g_key, g_value = core(
        live, halo_ok, nm, gm, nmt, attt, ndt, w_up, w_down, w_out, w_query, w_key, w_value,
        middle, gw, ao, mod, q, k, v, lse, kh, vh, xw, block_input,
    )
    mod_part = jnp.concatenate([sums_a[0:2], sums_m[0:4]])
    mod_total = mod_part + band_swap(mod_part)
    grads = (g_query, g_key, g_value, g_out, g_up, g_down)
    return block_output, grad_input, mod_total[None], *(g.reshape(-1) for g in grads)


def solution(mesh):
    return jax.shard_map(
        on_device,
        mesh=mesh,
        in_specs=(
            P("dp", None, "band", None, None),
            P("dp", None, None),
            P("dp", None),
            P(),
            P(),
            P(),
            P(),
            P(),
            P(),
            P("dp", None, "band", None, None),
        ),
        out_specs=(
            P("dp", None, "band", None, None),
            P("dp", None, "band", None, None),
            P("dp", None, None),
            P("dp"),
            P("dp"),
            P("dp"),
            P("dp"),
            P("dp"),
            P("dp"),
        ),
        check_vma=False,
    )
```

```python
import functools

import jax
import jax.numpy as jnp
from jax import lax
from jax.experimental import pallas as pl
from jax.experimental.pallas import tpu as pltpu
from jax.sharding import PartitionSpec as P

HEADS = 16
HEAD_DIM = 64
EPS = 1e-06
MASKED = -1e30
LOG2E = 1.4426950408889634
F32 = jnp.float32
BF16 = jnp.bfloat16
ANY = pl.BlockSpec(memory_space=pl.ANY)
VMEM_LIMIT = 60 * 1024 * 1024

MID_SPOTS = ((1, 0), (2, 0), (1, 1), (2, 1))


def group_spot(band, s):
    lone = 3 * band
    paired = 3 - 3 * band
    if s < 2:
        return lone, s
    if s < 6:
        return MID_SPOTS[s - 2]
    return paired, s - 6


def params(limit=VMEM_LIMIT, **kw):
    return pltpu.CompilerParams(vmem_limit_bytes=limit, **kw)


def dot(a, b, ca=1, cb=0):
    return lax.dot_general(a, b, (((ca,), (cb,)), ((), ())), preferred_element_type=F32)


def whole(shape):
    return pl.BlockSpec(shape, lambda *_: (0,) * len(shape), pipeline_mode=pl.Buffered(1))


def norm_stats(v):
    c = v - jnp.mean(v, axis=-1, keepdims=True)
    r = lax.rsqrt(jnp.mean(c * c, axis=-1, keepdims=True) + EPS)
    return c * r, r


def spot_copy(hbm, vmem, band, s, sem, out=False):
    g, j = group_spot(band, s)
    there = hbm.at[0, :, pl.ds(g * 4, 4), pl.ds(j * 8, 8), :]
    if out:
        slot = s % vmem.shape[0]
        return pltpu.make_async_copy(vmem.at[slot], there, sem.at[slot])
    return pltpu.make_async_copy(there, vmem.at[s], sem.at[s])


def pre_kernel(n_group, from_spots, x_hbm, mod_ref, *refs):
    n_mat = (len(refs) - 5) // 2 if from_spots else (len(refs) - 3) // 2
    w_refs = refs[:n_mat]
    outs = refs[n_mat:]
    if from_spots:
        xw_ref, normed_ref = outs[:2]
        o_refs = outs[2 : 2 + n_mat]
    else:
        o_refs = outs[:n_mat]
    stage, sem, nsc = outs[-3:] if not from_spots else outs[-3:]
    rows = nsc.shape[0] // n_group

    @pl.when(pl.program_id(0) == 0)
    def _():
        band = lax.axis_index("band")
        if from_spots:
            copies = [spot_copy(x_hbm, stage, band, s, sem) for s in range(n_group)]
        else:
            copies = [
                pltpu.make_async_copy(x_hbm.at[:, :, pl.ds(8 * s, 8), :], stage.at[s], sem.at[s])
                for s in range(n_group)
            ]
        for c in copies:
            c.start()
        for s in range(n_group):
            copies[s].wait()
            x = stage[s].astype(F32).reshape(rows, stage.shape[-1])
            n, _ = norm_stats(x)
            part = pl.ds(s * rows, rows)
            nsc[part, :] = (n * (1.0 + mod_ref[1:2, :]) + mod_ref[0:1, :]).astype(BF16)
            if from_spots:
                xw_ref[part, :] = x.astype(BF16)
        if from_spots:
            normed_ref[...] = jnp.transpose(nsc[...])

    for w_ref, o_ref in zip(w_refs, o_refs):
        o_ref[...] = dot(nsc[...], w_ref[...]).astype(BF16)


def pre(x, mod, weights, n_group, from_spots):
    d = x.shape[-1]
    frames = x.shape[1] if from_spots else x.shape[0]
    rows = frames * 32
    t = n_group * rows
    tile = 256
    o_tile = pl.BlockSpec((t, tile), lambda n: (0, n))
    full = pl.BlockSpec((t, d), lambda n: (0, 0))
    act = jax.ShapeDtypeStruct((t, d), BF16)
    k = len(weights)
    head = [act, jax.ShapeDtypeStruct((d, t), BF16)] if from_spots else []
    return pl.pallas_call(
        functools.partial(pre_kernel, n_group, from_spots),
        grid=(d // tile,),
        in_specs=[ANY, whole((6, d))] + [pl.BlockSpec((d, tile), lambda n: (0, n))] * k,
        out_specs=[full, whole((d, t))][: len(head)] + [o_tile] * k,
        out_shape=head + [act] * k,
        scratch_shapes=[
            pltpu.VMEM((n_group, frames, 4, 8, d), BF16),
            pltpu.SemaphoreType.DMA((n_group,)),
            pltpu.VMEM((t, d), BF16),
        ],
        compiler_params=params(),
        name="pre" if from_spots else "pre_halo",
        cost_estimate=pl.CostEstimate(
            flops=2 * t * d * d * k, bytes_accessed=2 * (k * d * d + (k + 3) * t * d), transcendentals=0
        ),
    )(x, mod, *weights)


LANES = 512


class Reduce:
    def __init__(self, dp, total_rows, orders, tiles_only):
        self.bits = list(range(dp.bit_length() - 2, 0, -1))
        self.nz = len(self.bits)
        self.stages = self.nz + 1
        self.depth = self.stages + 4
        self.r = total_rows // dp
        self.orders = orders
        self.tiles_only = tiles_only
        self.dp = dp

    def scratch(self):
        r, nz, k = self.r, self.nz, self.stages
        out = [] if self.tiles_only else [pltpu.VMEM((1 << nz, r, LANES), BF16)]
        out += [pltpu.VMEM((2, 1 << nz, r, LANES), BF16)]
        for _ in range(2):
            for i in range(k):
                block = (2,) * (k - 1 - i) + (r, 128)
                out += [pltpu.VMEM(block, BF16), pltpu.VMEM(block, BF16), pltpu.VMEM((2,) + block, BF16)]
        out += [pltpu.VMEM((2, r, 128), BF16), pltpu.VMEM((2, 2, r, 128), BF16), pltpu.VMEM((r, LANES), F32)]
        out += [pltpu.SemaphoreType.DMA((2 * k + 4,)), pltpu.SemaphoreType.DMA((2 * k + 2, 2))]
        return out

    def bind(self, refs, jobs, tiles):
        refs = list(refs)
        cube = (2,) * self.nz
        self.own = tiles.at[0, :, 0] if self.tiles_only else refs.pop(0)
        self.got_core = refs.pop(0)
        self.got_cube = self.got_core.reshape((2,) + cube + (self.r, LANES))
        if self.tiles_only:
            self.tile_cube = tiles.reshape((2,) + cube + (2, self.r, LANES))
        else:
            self.own_cube = self.own.reshape(cube + (self.r, LANES))
        self.send, self.keep, self.got = {}, {}, {}
        for p in range(2):
            for i in range(self.stages):
                self.send[p, i], self.keep[p, i], self.got[p, i] = refs.pop(0), refs.pop(0), refs.pop(0)
        self.fin, self.got_fin, self.ostage, self.ssem, self.rsem = refs
        self.jobs = jobs
        self.starts = [job[0] for job in jobs]
        self.me, self.band = lax.axis_index("dp"), lax.axis_index("band")

    def place(self, axis):
        return self.band if axis == 0 else lax.rem(self.me // (1 << axis), 2)

    def partner(self, axis):
        if axis == 0:
            return (self.me, 1 - self.band)
        bit = 1 if axis == -1 else 1 << axis
        here = lax.rem(self.me // bit, 2)
        return (self.me + bit - 2 * bit * here, self.band)

    def barrier(self):
        sem = pltpu.get_barrier_semaphore()
        everyone = [-1, 0] + self.bits
        for axis in everyone:
            pl.semaphore_signal(sem, inc=1, device_id=self.partner(axis), device_id_type=pl.DeviceIdType.MESH)
        pl.semaphore_wait(sem, len(everyone))

    def remote(self, src, dst, s, slot, axis):
        return pltpu.make_async_remote_copy(
            src_ref=src,
            dst_ref=dst,
            send_sem=self.ssem.at[s],
            recv_sem=self.rsem.at[s, slot],
            device_id=self.partner(axis),
            device_id_type=pl.DeviceIdType.MESH,
        )

    def core_copy(self, slot, src):
        return self.remote(src, self.got_core.at[slot], 2 * self.stages, slot, -1)

    def part_copy(self, p, i, slot):
        return self.remote(self.send[p, i], self.got[p, i].at[slot], 2 * i + p, slot, self.orders[p][i])

    def fin_copy(self, slot):
        return self.remote(self.fin, self.got_fin.at[slot], 2 * self.stages + 1, slot, 0)

    def pick(self, axes, axis, at):
        return tuple(at if a == axis else slice(None) for a in axes)

    def split_core(self, j, p):
        slot = lax.rem(j, 2)
        first = self.orders[p][0]
        mine = self.place(first)
        for dst, at in ((self.send[p, 0], 1 - mine), (self.keep[p, 0], mine)):
            if first == 0:
                lanes = pl.ds(pl.multiple_of((2 * p + at) * 128, 128), 128)
                idx = (slice(None),) * (self.nz + 1) + (lanes,)
                dst[...] = self.mine(slot, idx) + self.got_cube[(slot,) + idx]
            else:
                for b in range(2):
                    lanes = slice((2 * p + b) * 128, (2 * p + b + 1) * 128)
                    idx = self.pick(self.bits, first, at) + (slice(None), lanes)
                    dst[(slice(None),) * (self.nz - 1) + (b,)] = self.mine(slot, idx) + self.got_cube[(slot,) + idx]

    def split(self, j, p, i):
        slot = lax.rem(j, 2)
        axes = [a for a in self.bits + [0] if a not in self.orders[p][:i]]
        axis = self.orders[p][i]
        mine = self.place(axis)
        for dst, at in ((self.send[p, i], 1 - mine), (self.keep[p, i], mine)):
            idx = self.pick(axes, axis, at)
            dst[...] = self.keep[p, i - 1][idx] + self.got[p, i - 1][(slot,) + idx]

    def stage(self, s, j):
        k = self.stages
        slot = lax.rem(j, 2)
        if s == 0:
            self.each(j, 1)
        elif s == 1:
            self.core_copy(slot, self.own).wait()
            if not self.tiles_only:
                self.own_copy(self.own).wait()
            for p in range(2):
                self.split_core(j, p)
                self.part_copy(p, 0, slot).start()
        elif s <= k:
            for p in range(2):
                self.part_copy(p, s - 2, slot).wait()
                self.split(j, p, s - 1)
                self.part_copy(p, s - 1, slot).start()
        elif s == k + 1:
            for p in range(2):
                self.part_copy(p, k - 1, slot).wait()
                self.fin[p] = self.keep[p, k - 1][...] + self.got[p, k - 1][slot]
            self.fin_copy(slot).start()
        elif s == k + 2:
            self.fin_copy(slot).wait()
            for p in range(2):
                mine = pl.ds(pl.multiple_of((2 * p + self.band) * 128, 128), 128)
                other = pl.ds(pl.multiple_of((2 * p + 1 - self.band) * 128, 128), 128)
                self.ostage[:, mine] = self.fin[p].astype(F32)
                self.ostage[:, other] = self.got_fin[slot, p].astype(F32)
            self.each(j, 2)
        else:
            self.out_copy(self.ostage).wait()

    def each(self, j, part):
        for i, job in enumerate(self.jobs):
            pl.when(j == i)(functools.partial(job[part], self, i % 2))

    def own_copy(self, src):
        return pltpu.make_async_copy(src, self.own, self.ssem.at[2 * self.stages + 2])

    def out_copy(self, dst, src=None):
        return pltpu.make_async_copy(self.ostage if src is None else src, dst, self.ssem.at[2 * self.stages + 3])

    def mine(self, slot, idx):
        if self.tiles_only:
            return self.tile_cube[(slot,) + idx[: self.nz] + (lax.rem(self.me, 2),) + idx[self.nz :]]
        return self.own_cube[idx]

    def start_pair(self, slot, ref, at):
        core = lax.rem(self.me, 2)
        if not self.tiles_only:
            self.own_copy(ref.at[(slice(None), core) + at]).start()
        self.core_copy(slot, ref.at[(slice(None), 1 - core) + at]).start()

    def tick(self, t):
        for s in reversed(range(self.depth)):
            u = t - s
            before = sum(jnp.where(u > at, 1, 0) for at in self.starts)
            upto = sum(jnp.where(u >= at, 1, 0) for at in self.starts)

            @pl.when(upto > before)
            def _():
                self.stage(s, before)

    def plain(self, src, dst, send_sem, recv_sem, axis):
        return pltpu.make_async_remote_copy(
            src_ref=src,
            dst_ref=dst,
            send_sem=send_sem,
            recv_sem=recv_sem,
            device_id=self.partner(axis),
            device_id_type=pl.DeviceIdType.MESH,
        )


def cube_shape(red, rows, cols):
    return (red.dp // 2, 2, rows // (red.r * red.dp), red.r, cols)


def lanes_at(i, width=LANES):
    return slice(i * width, (i + 1) * width)


def array_job(start, src, dst, q, i, q_out=None):
    def begin(red, slot):
        red.start_pair(slot, src, (q, slice(None), lanes_at(i)))

    def end(red, slot):
        red.out_copy(dst.at[q if q_out is None else q_out, :, lanes_at(i)]).start()

    return start, begin, end


def tile_job(start, tiles, at, parts):
    width = LANES // len(parts)

    def begin(red, slot):
        red.start_pair(slot, tiles.at[at], ())

    def end(red, slot):
        for n, dst in enumerate(parts):
            red.out_copy(dst, red.ostage.at[:, lanes_at(n, width)]).start()

    return start, begin, end


def tile_scratch(red):
    return pltpu.VMEM((2, red.dp // 2, 2, red.r, LANES), BF16)


def put_tile(red, tiles, slot, v):
    tiles[slot] = v.reshape(tiles.shape[1:]).astype(BF16)


SCALE = HEAD_DIM**-0.5
SCALE2 = SCALE * LOG2E


def head_masks(rows):
    left = lax.broadcasted_iota(jnp.int32, (rows, 128), 1) < 64
    return left, jnp.logical_not(left)


def only(mask, v):
    return jnp.where(mask, v, jnp.zeros_like(v))


def each_window(r, body):
    for first, rows, at, shared in ((4, r, 6 * r, True), (0, r, 0, False), (2, 2 * r, 2 * r, False)):
        yield functools.partial(window_pair, r, first, rows, at, shared, body)


def window_pair(r, first, rows, at, shared, body):
    def one(i, _):
        q0 = pl.multiple_of(at + i * rows, 32)
        k0 = pl.multiple_of(2 * r * i, 32) if shared else q0
        body(first + i, i, pl.ds(q0, rows), pl.ds(k0, 2 * r if shared else rows), shared)
        return 0

    lax.fori_loop(0, 2, one, 0)


def fill_shared(scratch, own_ref, halo_ref, r):
    for w in range(2):
        scratch[2 * r * w : 2 * r * w + r, :] = own_ref[(6 + w) * r : (7 + w) * r, :]
        scratch[2 * r * w + r : 2 * r * (w + 1), :] = halo_ref[r * w : r * (w + 1), :]


def attn_fwd_kernel(ok_ref, q_ref, k_ref, v_ref, kh_ref, vh_ref, o_ref, lse_ref, kc, vc):
    r = q_ref.shape[0] // 8
    fill_shared(kc, k_ref, kh_ref, r)
    fill_shared(vc, v_ref, vh_ref, r)
    col = lax.broadcasted_iota(jnp.int32, (1, 2 * r), 1)
    bias = jnp.where((col >= r) & (ok_ref[0] != 1), MASKED, 0.0)
    for w, (q0, qn) in enumerate(((0, r), (r, r), (2 * r, 2 * r), (4 * r, 2 * r), (6 * r, r), (7 * r, r))):
        rows = slice(q0, q0 + qn)
        q = q_ref[rows, :]
        if w < 4:
            k, v = k_ref[rows, :], v_ref[rows, :]
        else:
            keys = slice(2 * r * (w - 4), 2 * r * (w - 3))
            k, v = kc[keys, :], vc[keys, :]
        masks = head_masks(qn)
        o, lse = [], []
        for mask in masks:
            s = dot(only(mask, q), k, 1, 1) * SCALE2
            if w >= 4:
                s = s + bias
            top = jnp.max(s, axis=-1, keepdims=True)
            e = jnp.exp2(s - top)
            total = jnp.sum(e, axis=-1, keepdims=True)
            o.append(dot(e.astype(BF16), v) * (1.0 / total))
            lse.append(top + jnp.log2(total))
        o_ref[rows, :] = jnp.where(masks[0], o[0], o[1]).astype(BF16)
        turned = jnp.transpose(jnp.where(masks[0], lse[0], lse[1]))
        for h in range(2):
            lse_ref[w, h : h + 1, :qn] = turned[64 * h : 64 * h + 1, :]


def lse_lanes(t):
    return pl.cdiv(t // 4, 128) * 128


def attn_fwd(halo_ok, q, k, v, kh, vh):
    t, d = q.shape
    th = kh.shape[0]
    big = pl.BlockSpec((t, 128), lambda n: (0, n))
    small = pl.BlockSpec((th, 128), lambda n: (0, n))
    return pl.pallas_call(
        attn_fwd_kernel,
        grid=(d // 128,),
        in_specs=[pl.BlockSpec(memory_space=pltpu.SMEM), big, big, big, small, small],
        out_specs=[big, pl.BlockSpec((None, 6, 8, lse_lanes(t)), lambda n: (n, 0, 0, 0))],
        out_shape=[jax.ShapeDtypeStruct((t, d), BF16), jax.ShapeDtypeStruct((d // 128, 6, 8, lse_lanes(t)), F32)],
        scratch_shapes=[pltpu.VMEM((2 * th, 128), BF16)] * 2,
        compiler_params=params(),
        name="attn_fwd",
        cost_estimate=pl.CostEstimate(flops=t * t * d, bytes_accessed=12 * t * d, transcendentals=t * t * 3),
    )(halo_ok, q, k, v, kh, vh)


def mid_kernel(
    g_hbm, live_ref, att_ref, w_ref, x_ref, mod_ref, ao_ref, mid_ref, nm_ref, nmt_ref, attt_ref, gw_ref, gm_ref, stage, sem
):
    step = pl.program_id(0)
    band = lax.axis_index("band")
    live = live_ref[0].astype(F32)
    n_group = stage.shape[0]
    rows = gw_ref.shape[0] // n_group

    @pl.when(step == 0)
    def _():
        for s in range(n_group):
            spot_copy(g_hbm, stage, band, s, sem).start()

    attn_out = dot(att_ref[...], w_ref[...])
    middle = x_ref[...].astype(F32) + (live * mod_ref[2:3, :]) * attn_out
    ao_ref[...] = attn_out.astype(BF16)
    mid_ref[...] = middle
    n, _ = norm_stats(middle)
    nm = (n * (1.0 + mod_ref[4:5, :]) + mod_ref[3:4, :]).astype(BF16)
    nm_ref[...] = nm
    nmt_ref[...] = jnp.transpose(nm)
    attt_ref[...] = jnp.transpose(att_ref[...])
    for k in range(4):

        @pl.when(step == k + 1)
        def _():
            for s in range(2 * k, 2 * k + 2):
                spot_copy(g_hbm, stage, band, s, sem).wait()
                g = stage[s].astype(F32).reshape(rows, stage.shape[-1])
                part = slice(s * rows, (s + 1) * rows)
                gw_ref[part, :] = g.astype(BF16)
                gm_ref[part, :] = ((live * mod_ref[5:6, :]) * g).astype(BF16)


def mid(cot, live, attended, w_out, xw, mod):
    t, d = xw.shape
    frames = cot.shape[1]
    blk = pl.BlockSpec((t // 5, d), lambda m: (m, 0))
    blk_t = pl.BlockSpec((d, t // 5), lambda m: (0, m))
    full = pl.BlockSpec((t, d), lambda m: (0, 0))
    bf, f32 = jax.ShapeDtypeStruct((t, d), BF16), jax.ShapeDtypeStruct((t, d), F32)
    bf_t = jax.ShapeDtypeStruct((d, t), BF16)
    return pl.pallas_call(
        mid_kernel,
        grid=(5,),
        in_specs=[ANY, pl.BlockSpec(memory_space=pltpu.SMEM), blk, whole((d, d)), blk, whole((6, d))],
        out_specs=[blk, blk, blk, blk_t, blk_t, full, full],
        out_shape=[bf, f32, bf, bf_t, bf_t, bf, bf],
        scratch_shapes=[pltpu.VMEM((8, frames, 4, 8, d), BF16), pltpu.SemaphoreType.DMA((8,))],
        compiler_params=params(),
        name="mid",
        cost_estimate=pl.CostEstimate(flops=2 * t * d * d, bytes_accessed=22 * t * d, transcendentals=0),
    )(cot, live, attended, w_out, xw, mod)


GELU_C = 0.7978845608
GELU_A = 0.044715


def col_sum(v):
    return jnp.sum(v, axis=0, keepdims=True)


def norm_back(h, n, r, gain):
    e = h * (1.0 + gain)
    return r * (e - jnp.mean(e, axis=-1, keepdims=True) - n * jnp.mean(e * n, axis=-1, keepdims=True))


def add_sums(ref, first, rows):
    sums = jnp.concatenate(rows + [jnp.zeros((ref.shape[0] - len(rows), ref.shape[1]), F32)], axis=0)

    @pl.when(first)
    def _():
        ref[...] = sums

    @pl.when(jnp.logical_not(first))
    def _():
        ref[...] += sums


def put_groups(out, stage, out_hbm, sem, block, blocks):
    band = lax.axis_index("band")
    slots = stage.shape[0]
    n_group = 8
    per = n_group // blocks
    rows = out.shape[0] // per
    for k in range(blocks):

        @pl.when(block == k)
        def _():
            for i in range(per):
                s = k * per + i
                if s >= slots:
                    spot_copy(out_hbm, stage, band, s - slots, sem, out=True).wait()
                stage[s % slots] = out[i * rows : (i + 1) * rows, :].reshape(stage.shape[1:]).astype(BF16)
                spot_copy(out_hbm, stage, band, s, sem, out=True).start()

    @pl.when(block == blocks - 1)
    def _():
        for s in range(n_group - slots, n_group):
            spot_copy(out_hbm, stage, band, s, sem, out=True).wait()


PIECES = 4


class Tiling:
    def __init__(self, ff, dp):
        self.steps = ff // LANES
        self.width = LANES // PIECES
        self.early = ff // dp == 2 * self.width

    def piece(self, i, k):
        if not self.early:
            return PIECES * i + k
        half = self.steps // 2
        return (i % half * PIECES + k) * 2 + i // half


def window_back(w, rows, keys, bias, q_ref, k_ref, v_ref, do, lse_ref):
    q, k, v = q_ref[rows, :], k_ref[keys, :], v_ref[keys, :]
    kt = jnp.transpose(k)
    dq, dk, dv = [], [], []
    for h, mask in enumerate(head_masks(rows.size)):
        s = dot(k, only(mask, q), 1, 1) * SCALE2
        if bias is not None:
            s = s + bias
        p = jnp.exp2(s - lse_ref[w, h : h + 1, : rows.size])
        dp = dot(v, only(mask, do), 1, 1)
        total = jnp.sum(p * dp, axis=0, keepdims=True)
        ds = (p * (dp - total)).astype(BF16)
        dv.append(dot(p.astype(BF16), do))
        dk.append(dot(ds, q))
        dq.append(dot(kt[64 * h : 64 * h + 64, :], ds))
    left = head_masks(keys.size)[0]
    dq = jnp.transpose(jnp.concatenate(dq, axis=0)) * SCALE
    return dq, jnp.where(left, dk[0], dk[1]) * SCALE, jnp.where(left, dv[0], dv[1])


TILES = ((("q", 0), ("k", 0)), (("v", 0), ("v", 1)), (("q", 1), ("k", 1)), (("q", 2), ("k", 2)), (("v", 2), ("v", 3)), (("q", 3), ("k", 3)))
TILE_SLOTS = (0, 0, 1, 0, 1, 0)
MADE = {2: (0,), 4: (1, 2), 6: (3,), 8: (4, 5)}


class Plan:
    def __init__(self, n_ff, n_att, early):
        self.n_ff, self.n_att = n_ff, n_att
        self.post = n_ff
        self.out = n_ff + 4
        self.att = self.out + 1
        self.fin = self.att + n_att
        self.steps = self.fin + 4
        self.end = self.fin + 8
        a = self.att
        self.up = [(0, i + 1) for i in range(n_ff)]
        self.o_proj = [(0, a), (1, a)]
        self.tiles = [(1, a + 3), (1, a + 5), (0, a + 5), (1, a + 7), (1, self.fin + 1), (0, self.fin + 1)]
        late = [(1, n_ff + 1 + i) for i in range(4)]
        self.down = [(1, n_ff // 2 + 1 + i) for i in range(4)] + late if early else late + [(1, a + i) for i in (1, 2, 4, 6)]


def finish(reds, first):
    def body(u, _):
        for red in reds:
            red.tick(u)
        return 0

    lax.fori_loop(first, max(red.starts[-1] + red.depth for red in reds), body, 0)


def core_kernel(
    til, plan, reds, live_ref, ok_ref, nm_hbm, gm_hbm, nmt_hbm, attt_hbm, ndt_hbm, wu_hbm, wo_hbm, wq_hbm,
    wd_ref, mid_ref, g_ref, ao_ref, mod_ref, wk_ref, wv_ref, q_ref, k_ref, v_ref, lse_ref, kh_ref, vh_ref, x_ref,
    out_hbm, gin_hbm, sums_ref, sums_a_ref, dwd_hbm, gup_hbm, gdown_hbm, gout_hbm, gq_hbm, gk_hbm, gv_hbm,
    buf_a, buf_b, buf_c, buf_t, mo, h, do_s, w0, wu, dwd, tiles, kc, vc, own, hsend, hrecv,
    hsem, wsem, lsem, stage, sem, *scratch,
):
    step, steps = pl.program_id(0), pl.num_programs(0)
    n_ff, n_att, width = plan.n_ff, plan.n_att, til.width
    t, d = mo.shape
    chunk = t // 4
    r = t // 8
    red = reds[0]

    def up_at(i, k):
        return pl.ds(pl.multiple_of(til.piece(i, k) * width, width), width)

    def load_up(i, k):
        slot = lax.rem(i, 2)
        return pltpu.make_async_copy(wu_hbm.at[:, up_at(i, k)], wu.at[slot, :, lanes_at(k, width)], wsem.at[slot, k])

    def store_down(i, k):
        if til.early:
            d_at = til.piece(i, k) // 2
            dst = dwd_hbm.at[d_at // 2, lax.rem(d_at, 2), pl.ds(2 * lax.rem(til.piece(i, k), 2), 2)]
        else:
            dst = dwd_hbm.at[pl.ds(til.piece(i, k) * width, width), :]
        return pltpu.make_async_copy(dwd.at[k], dst, wsem.at[2, k])

    def load(n):
        pairs = ((nm_hbm, buf_b), (gm_hbm, buf_c), (nmt_hbm, buf_t), (wo_hbm, w0), (attt_hbm, buf_t), (ndt_hbm, buf_t), (wq_hbm, w0))
        return pltpu.make_async_copy(*pairs[n], lsem.at[n])

    grad_of = {"q": (buf_a, gq_hbm), "k": (buf_b, gk_hbm), "v": (buf_c, gv_hbm)}
    cube = dwd_hbm if til.early else dwd_hbm.reshape(cube_shape(red, dwd_hbm.shape[0], d))
    wide = d // LANES
    jobs = ([], [])
    for i, (at, start) in enumerate(plan.up):
        jobs[at].append(tile_job(start, tiles, i % 2, [gup_hbm.at[:, lanes_at(til.piece(i, k), width)] for k in range(PIECES)]))
    for n, (at, start) in enumerate(plan.down):
        jobs[at].append(array_job(start, cube, gdown_hbm, n // wide, n % wide))
    for n, (at, start) in enumerate(plan.o_proj):
        jobs[at].append(tile_job(start, tiles, n, [gout_hbm.at[:, lanes_at(n)]]))
    for m, (at, start) in enumerate(plan.tiles):
        jobs[at].append(tile_job(start, tiles, TILE_SLOTS[m], [grad_of[n][1].at[:, lanes_at(i, 256)] for n, i in TILES[m]]))
    size = len(scratch) // 2
    for i in range(2):
        reds[i].bind(scratch[i * size : (i + 1) * size + i], sorted(jobs[i], key=lambda job: job[0]), tiles)

    def swap(i):
        slot = lax.rem(i, 2)
        return red.plain(hsend, hrecv.at[slot], hsem.at[0], hsem.at[1 + slot], 0)

    @pl.when(step == 0)
    def _():
        for k in range(PIECES):
            load_up(0, k).start()
        for n in range(4):
            load(n).start()
        mo[...] = jnp.zeros_like(mo)
        h[...] = jnp.zeros_like(h)
        red.barrier()
        load(0).wait()
        load(1).wait()

    for one in reds:
        one.tick(step + jnp.maximum(step - plan.fin, 0))

    @pl.when(step < n_ff)
    def _():
        slot = lax.rem(step, 2)
        for k in range(PIECES):
            load_up(step, k).wait()

        @pl.when(step + 1 < n_ff)
        def _():
            for k in range(PIECES):
                load_up(step + 1, k).start()

        wd = wd_ref[...].reshape(LANES, d)
        up = wu.at[slot]

        def rows(i, _):
            part = pl.ds(pl.multiple_of(i * chunk, chunk), chunk)
            v = dot(buf_b[part, :], up[...])
            gh = dot(buf_c[part, :], wd, 1, 1)
            v2 = v * v
            th = jnp.tanh(v * (GELU_C + (GELU_C * GELU_A) * v2))
            half = 0.5 * th + 0.5
            hidden = (v * half).astype(BF16)
            slope = half + (0.5 * v) * (1.0 - th * th) * (GELU_C + (3.0 * GELU_C * GELU_A) * v2)
            gpre = (gh * slope).astype(BF16)
            buf_a[part, :LANES] = hidden
            buf_a[part, LANES : 2 * LANES] = gpre
            mo[part, :] += dot(hidden, wd)
            h[part, :] += dot(gpre, up[...], 1, 1)
            return 0

        lax.fori_loop(0, 4, rows, 0)

        @pl.when(step > 0)
        def _():
            for k in range(PIECES):
                store_down(step - 1, k).wait()

        pl.when(step == 0)(lambda: load(2).wait())
        put_tile(red, tiles, slot, dot(buf_t[...], buf_a[:, LANES : 2 * LANES]))
        dwd[...] = dot(buf_a[:, :LANES], buf_c[...], 0, 0).reshape(dwd.shape).astype(BF16)
        for k in range(PIECES):
            store_down(step, k).start()

    @pl.when((step >= plan.post) & (step < plan.out))
    def _():
        block = step - plan.post

        @pl.when(block == 0)
        def _():
            load(4).start()
            load(3).wait()
            for k in range(PIECES):
                store_down(step - 1, k).wait()

        part = pl.ds(pl.multiple_of(block * chunk, chunk), chunk)
        live = live_ref[0].astype(F32)
        middle, g = mid_ref[...], g_ref[...].astype(F32)
        mlp_out, hh = mo[part, :], h[part, :]
        n, rs = norm_stats(middle)
        gmid = g + norm_back(hh, n, rs, mod_ref[4:5, :])
        h[part, :] = gmid
        ga = ((live * mod_ref[2:3, :]) * gmid).astype(BF16)
        buf_b[part, :] = ga
        do_s[part, :] = dot(ga, w0[...], 1, 1).astype(BF16)
        sums = [col_sum(live * ao_ref[...].astype(F32) * gmid), col_sum(hh), col_sum(hh * n), col_sum(live * mlp_out * g)]
        add_sums(sums_ref, block == 0, sums)
        put_groups(middle + (live * mod_ref[5:6, :]) * mlp_out, stage, out_hbm, sem, block, 4)

    @pl.when(step == plan.out)
    def _():
        load(6).start()
        load(4).wait()
        for n in range(wide):
            put_tile(red, tiles, n, dot(buf_t[...], buf_b[:, lanes_at(n)]))
        load(5).start()

    now = step - plan.att

    @pl.when((now > 0) & (now <= n_att))
    def _():
        swap(now - 1).wait()
        slot = lax.rem(now - 1, 2)
        lanes = pl.ds(pl.multiple_of((now - 1) * 128, 128), 128)
        for i, ref in enumerate((buf_b, buf_c)):
            ref[6 * r :, lanes] = (own[i] + hrecv[slot, i].astype(F32)).astype(BF16)

    for at, made in MADE.items():

        @pl.when(now == at)
        def _():
            if at == min(MADE):
                load(5).wait()
            for m in made:
                cols = [grad_of[n][0][:, lanes_at(i, 256)] for n, i in TILES[m]]
                put_tile(red, tiles, TILE_SLOTS[m], dot(buf_t[...], jnp.concatenate(cols, axis=1)))

    @pl.when((now >= 0) & (now < n_att))
    def _():
        slot = lax.rem(now, 2)
        lanes = pl.ds(pl.multiple_of(now * 128, 128), 128)
        fill_shared(kc, k_ref, kh_ref, r)
        fill_shared(vc, v_ref, vh_ref, r)
        row = lax.broadcasted_iota(jnp.int32, (2 * r, 1), 0)
        bias = jnp.where((row >= r) & (ok_ref[0] != 1), MASKED, 0.0)

        def window(w, i, rows, keys, shared):
            data = (bias, q_ref, kc, vc) if shared else (None, q_ref, k_ref, v_ref)
            dq, dk, dv = window_back(w, rows, keys, *data, do_s[rows, lanes], lse_ref)
            buf_a[rows, lanes] = dq.astype(BF16)
            if shared:
                part = pl.ds(pl.multiple_of(i * r, 32), r)
                for n, v in enumerate((dk, dv)):
                    own[n, part, :] = v[:r, :]
                    hsend[n, part, :] = v[r:, :].astype(BF16)
            else:
                buf_b[rows, lanes] = dk.astype(BF16)
                buf_c[rows, lanes] = dv.astype(BF16)

        pairs = list(each_window(r, window))
        pairs[0]()
        swap(now).start()
        pairs[1]()
        pairs[2]()

    @pl.when(step >= plan.fin)
    def _():
        i = step - plan.fin
        pl.when(i == 0)(lambda: load(6).wait())
        part = pl.ds(pl.multiple_of(i * chunk, chunk), chunk)
        hh = dot(buf_a[part, :], w0[...], 1, 1) + dot(buf_b[part, :], wk_ref[...], 1, 1)
        for one in reds:
            one.tick(plan.fin + 2 * i + 1)
        hh = hh + dot(buf_c[part, :], wv_ref[...], 1, 1)
        n, rs = norm_stats(x_ref[...].astype(F32))
        add_sums(sums_a_ref, i == 0, [col_sum(hh), col_sum(hh * n)])
        put_groups(h[part, :] + norm_back(hh, n, rs, mod_ref[1:2, :]), stage, gin_hbm, sem, i, 4)

    @pl.when(step == steps - 1)
    def _():
        finish(reds, plan.end)


def core(live, halo_ok, nm, gm, nmt, attt, ndt, w_up, w_down, wo, wq, wk, wv, middle, gw, ao, mod, q, k, v, lse, kh, vh, xw, like):
    t, d = nm.shape
    ff = w_up.shape[1]
    th = kh.shape[0]
    frames = like.shape[1]
    dp = lax.axis_size("dp")
    til = Tiling(ff, dp)
    n_ff, n_att = til.steps, d // 128
    plan = Plan(n_ff, n_att, til.early)
    rest = tuple(range(3, dp.bit_length() - 1))
    reds = [Reduce(dp, d, ((0, 1, 2, *rest), (1, 2, 0, *rest)), i == 0) for i in range(2)]
    red = reds[0]

    def block_at(first, count):
        return lambda i: (jnp.clip(i - first, 0, count - 1), 0)

    def lane_at(i):
        return 0, jnp.clip(i - plan.att, 0, n_att - 1)

    post = pl.BlockSpec((t // 4, d), block_at(plan.post, 4))
    last = pl.BlockSpec((t // 4, d), block_at(plan.fin, 4), pipeline_mode=pl.Buffered(1))
    big, small = pl.BlockSpec((t, 128), lane_at), pl.BlockSpec((th, 128), lane_at)
    lse_spec = pl.BlockSpec((None, 6, 8, lse_lanes(t)), lambda i: (lane_at(i)[1], 0, 0, 0))
    if til.early:
        half = n_ff // 2
        w_down = w_down.reshape(half, PIECES, 2, til.width, d)

        def down_at(i):
            i = jnp.minimum(i, n_ff - 1)
            return lax.rem(i, half), 0, i // half, 0, 0

        down = pl.BlockSpec((None, PIECES, None, til.width, d), down_at)
        cube, down_tile = cube_shape(red, ff, d), (PIECES, 2, red.r, d)
    else:
        down = pl.BlockSpec((LANES, d), block_at(0, n_ff))
        cube, down_tile = (ff, d), (PIECES, til.width, d)
    smem = pl.BlockSpec(memory_space=pltpu.SMEM)
    full = pl.BlockSpec((8, d), lambda i: (0, 0))
    image, sums = jax.ShapeDtypeStruct(like.shape, BF16), jax.ShapeDtypeStruct((8, d), F32)
    share = jax.ShapeDtypeStruct((red.r, d), F32)
    act, act32 = pltpu.VMEM((t, d), BF16), pltpu.VMEM((t, d), F32)
    return pl.pallas_call(
        functools.partial(core_kernel, til, plan, reds),
        grid=(plan.steps,),
        in_specs=[smem, smem] + [ANY] * 8 + [down, post, post, post, whole((6, d)), whole((d, d)), whole((d, d))]
        + [big] * 3 + [lse_spec] + [small] * 2 + [last],
        out_specs=[ANY, ANY, full, full] + [ANY] * 7,
        out_shape=[image, image, sums, sums, jax.ShapeDtypeStruct(cube, BF16), jax.ShapeDtypeStruct((red.r, ff), F32)]
        + [jax.ShapeDtypeStruct((ff // d, red.r, d), F32), share, share, share, share],
        scratch_shapes=[
            act,
            act,
            act,
            pltpu.VMEM((d, t), BF16),
            act32,
            act32,
            act,
            pltpu.VMEM((d, d), BF16),
            pltpu.VMEM((2, d, LANES), BF16),
            pltpu.VMEM(down_tile, BF16),
            tile_scratch(red),
            pltpu.VMEM((2 * th, 128), BF16),
            pltpu.VMEM((2 * th, 128), BF16),
            pltpu.VMEM((2, th, 128), F32),
            pltpu.VMEM((2, th, 128), BF16),
            pltpu.VMEM((2, 2, th, 128), BF16),
            pltpu.SemaphoreType.DMA((3,)),
            pltpu.SemaphoreType.DMA((3, PIECES)),
            pltpu.SemaphoreType.DMA((7,)),
            pltpu.VMEM((4, frames, 4, 8, d), BF16),
            pltpu.SemaphoreType.DMA((4,)),
        ]
        + reds[0].scratch()
        + reds[1].scratch(),
        compiler_params=params(limit=63 * 1024 * 1024, collective_id=1, has_side_effects=True),
        name="core",
        cost_estimate=pl.CostEstimate(
            flops=12 * t * d * (ff + d) + 3 * t * t * d, bytes_accessed=8 * d * ff + 60 * t * d, transcendentals=t * (ff + 3 * t)
        ),
    )(live, halo_ok, nm, gm, nmt, attt, ndt, w_up, wo, wq, w_down, middle, gw, ao, mod, wk, wv, q, k, v, lse, kh, vh, xw)


def band_swap(v):
    return lax.ppermute(v, "band", [(0, 1), (1, 0)])


def on_device(
    block_input, modulation, band_live, w_query, w_key, w_value, w_out, w_up, w_down, cotangent
):
    assert lax.axis_size("band") == 2 and block_input.shape[2:4] == (16, 16)
    band = lax.axis_index("band")
    flags = band_live[0]
    live_own = lax.dynamic_index_in_dim(flags, band, keepdims=True)
    live_other = lax.dynamic_index_in_dim(flags, 1 - band, keepdims=True)
    live = (live_own == 1).astype(jnp.int32)
    halo_ok = ((live_other == 1) | (live_own != 1)).astype(jnp.int32)
    mod = modulation[0]

    edge = lax.dynamic_slice_in_dim(block_input[0], 12 - 12 * band, 4, axis=1)
    x_halo = band_swap(edge)
    xw, ndt, q, k, v = pre(block_input, mod, (w_query, w_key, w_value), 8, True)
    kh, vh = pre(x_halo, mod, (w_key, w_value), 2, False)
    attended, lse = attn_fwd(halo_ok, q, k, v, kh, vh)
    ao, middle, nm, nmt, attt, gw, gm = mid(cotangent, live, attended, w_out, xw, mod)
    block_output, grad_input, sums_m, sums_a, _, g_up, g_down, g_out, g_query, g_key, g_value = core(
        live, halo_ok, nm, gm, nmt, attt, ndt, w_up, w_down, w_out, w_query, w_key, w_value,
        middle, gw, ao, mod, q, k, v, lse, kh, vh, xw, block_input,
    )
    mod_part = jnp.concatenate([sums_a[0:2], sums_m[0:4]])
    mod_total = mod_part + band_swap(mod_part)
    grads = (g_query, g_key, g_value, g_out, g_up, g_down)
    return block_output, grad_input, mod_total[None], *(g.reshape(-1) for g in grads)


def solution(mesh):
    return jax.shard_map(
        on_device,
        mesh=mesh,
        in_specs=(
            P("dp", None, "band", None, None),
            P("dp", None, None),
            P("dp", None),
            P(),
            P(),
            P(),
            P(),
            P(),
            P(),
            P("dp", None, "band", None, None),
        ),
        out_specs=(
            P("dp", None, "band", None, None),
            P("dp", None, "band", None, None),
            P("dp", None, None),
            P("dp"),
            P("dp"),
            P("dp"),
            P("dp"),
            P("dp"),
            P("dp"),
        ),
        check_vma=False,
    )
```

```python
import functools

import jax
import jax.numpy as jnp
from jax import lax
from jax.experimental import pallas as pl
from jax.experimental.pallas import tpu as pltpu
from jax.sharding import PartitionSpec as P

HEADS = 16
HEAD_DIM = 64
EPS = 1e-06
MASKED = -1e30
LOG2E = 1.4426950408889634
F32 = jnp.float32
BF16 = jnp.bfloat16
ANY = pl.BlockSpec(memory_space=pl.ANY)
VMEM_LIMIT = 60 * 1024 * 1024

MID_SPOTS = ((1, 0), (2, 0), (1, 1), (2, 1))


def group_spot(band, s):
    lone = 3 * band
    paired = 3 - 3 * band
    if s < 2:
        return lone, s
    if s < 6:
        return MID_SPOTS[s - 2]
    return paired, s - 6


def params(limit=VMEM_LIMIT, **kw):
    return pltpu.CompilerParams(vmem_limit_bytes=limit, **kw)


def dot(a, b, ca=1, cb=0):
    return lax.dot_general(a, b, (((ca,), (cb,)), ((), ())), preferred_element_type=F32)


def whole(shape):
    return pl.BlockSpec(shape, lambda *_: (0,) * len(shape), pipeline_mode=pl.Buffered(1))


def own_live(flags):
    return jnp.where(flags[0, lax.axis_index("band")] == 1, 1.0, 0.0)


def halo_bias(flags, shape, dim, r):
    band = lax.axis_index("band")
    other = jnp.where(flags[0, 1 - band] == 1, 0.0, MASKED)
    off = jnp.where(flags[0, band] == 1, other, 0.0)
    return jnp.where(lax.broadcasted_iota(jnp.int32, shape, dim) >= r, off, 0.0)


def norm_stats(v):
    c = v - jnp.mean(v, axis=-1, keepdims=True)
    r = lax.rsqrt(jnp.mean(c * c, axis=-1, keepdims=True) + EPS)
    return c * r, r


def spot_copy(hbm, vmem, band, s, sem, out=False):
    g, j = group_spot(band, s)
    there = hbm.at[0, :, pl.ds(g * 4, 4), pl.ds(j * 8, 8), :]
    if out:
        slot = s % vmem.shape[0]
        return pltpu.make_async_copy(vmem.at[slot], there, sem.at[slot])
    return pltpu.make_async_copy(there, vmem.at[s], sem.at[s])


def pre_kernel(
    x_hbm, mod_ref, wq_ref, wk_ref, wv_ref, xw_ref, ndt_ref, q_ref, k_ref, v_ref, kh_ref, vh_ref,
    stage, halo, sem, swap_sem, nsc, nhalo,
):
    step, n_tile = pl.program_id(0), pl.num_programs(0) // 2
    band = lax.axis_index("band")
    n_group = stage.shape[0]
    rows = nsc.shape[0] // n_group
    there = (lax.axis_index("dp"), 1 - band)

    def normed(x):
        n, _ = norm_stats(x)
        return (n * (1.0 + mod_ref[1:2, :]) + mod_ref[0:1, :]).astype(BF16)

    swap = pltpu.make_async_remote_copy(
        src_ref=x_hbm.at[0, :, pl.ds(12 - 12 * band, 4)],
        dst_ref=halo,
        send_sem=swap_sem.at[0],
        recv_sem=swap_sem.at[1],
        device_id=there,
        device_id_type=pl.DeviceIdType.MESH,
    )

    @pl.when(step == 0)
    def _():
        for s in range(n_group):
            spot_copy(x_hbm, stage, band, s, sem).start()
        entered = pltpu.get_barrier_semaphore()
        pl.semaphore_signal(entered, inc=1, device_id=there, device_id_type=pl.DeviceIdType.MESH)
        pl.semaphore_wait(entered, 1)
        swap.start()
        for s in range(n_group):
            spot_copy(x_hbm, stage, band, s, sem).wait()
            x = stage[s].astype(F32).reshape(rows, stage.shape[-1])
            part = slice(s * rows, (s + 1) * rows)
            nsc[part, :] = normed(x)
            xw_ref[part, :] = x.astype(BF16)
        ndt_ref[...] = jnp.transpose(nsc[...])

    @pl.when(step < n_tile)
    def _():
        for w_ref, o_ref in ((wq_ref, q_ref), (wk_ref, k_ref), (wv_ref, v_ref)):
            o_ref[...] = dot(nsc[...], w_ref[...]).astype(BF16)

    @pl.when(step == n_tile)
    def _():
        swap.wait()
        for j in range(2):
            x = halo[:, :, 8 * j : 8 * j + 8, :].astype(F32).reshape(rows, halo.shape[-1])
            nhalo[j * rows : (j + 1) * rows, :] = normed(x)

    @pl.when(step >= n_tile)
    def _():
        for w_ref, o_ref in ((wk_ref, kh_ref), (wv_ref, vh_ref)):
            o_ref[...] = dot(nhalo[...], w_ref[...]).astype(BF16)


def pre(x, mod, wq, wk, wv):
    d, frames = x.shape[-1], x.shape[1]
    t = 8 * frames * 32
    th = t // 4
    tile = 256
    n_tile = d // tile
    own = pl.BlockSpec((t, tile), lambda n: (0, jnp.minimum(n, n_tile - 1)))
    other = pl.BlockSpec((th, tile), lambda n: (0, jnp.maximum(n - n_tile, 0)))
    once = pl.BlockSpec((d, tile), lambda n: (0, jnp.minimum(n, n_tile - 1)))
    twice = pl.BlockSpec((d, tile), lambda n: (0, lax.rem(n, n_tile)))
    act, act_h = jax.ShapeDtypeStruct((t, d), BF16), jax.ShapeDtypeStruct((th, d), BF16)
    return pl.pallas_call(
        pre_kernel,
        grid=(2 * n_tile,),
        in_specs=[ANY, whole((6, d)), once, twice, twice],
        out_specs=[whole((t, d)), whole((d, t)), own, own, own, other, other],
        out_shape=[act, jax.ShapeDtypeStruct((d, t), BF16), act, act, act, act_h, act_h],
        scratch_shapes=[
            pltpu.VMEM((8, frames, 4, 8, d), BF16),
            pltpu.VMEM((frames, 4, 16, d), BF16),
            pltpu.SemaphoreType.DMA((8,)),
            pltpu.SemaphoreType.DMA((2,)),
            pltpu.VMEM((t, d), BF16),
            pltpu.VMEM((th, d), BF16),
        ],
        compiler_params=params(collective_id=2, has_side_effects=True),
        name="pre",
        cost_estimate=pl.CostEstimate(flops=7 * t * d * d, bytes_accessed=10 * d * d + 12 * t * d, transcendentals=0),
    )(x, mod, wq, wk, wv)


LANES = 512


class Reduce:
    def __init__(self, dp, total_rows, orders, tiles_only):
        self.bits = list(range(dp.bit_length() - 2, 0, -1))
        self.nz = len(self.bits)
        self.stages = self.nz + 1
        self.depth = self.stages + 4
        self.r = total_rows // dp
        self.orders = orders
        self.tiles_only = tiles_only
        self.dp = dp

    def scratch(self):
        r, nz, k = self.r, self.nz, self.stages
        out = [] if self.tiles_only else [pltpu.VMEM((1 << nz, r, LANES), BF16)]
        out += [pltpu.VMEM((2, 1 << nz, r, LANES), BF16)]
        for _ in range(2):
            for i in range(k):
                block = (2,) * (k - 1 - i) + (r, 128)
                out += [pltpu.VMEM(block, BF16), pltpu.VMEM(block, BF16), pltpu.VMEM((2,) + block, BF16)]
        out += [pltpu.VMEM((2, r, 128), BF16), pltpu.VMEM((2, 2, r, 128), BF16), pltpu.VMEM((r, LANES), F32)]
        out += [pltpu.SemaphoreType.DMA((2 * k + 4,)), pltpu.SemaphoreType.DMA((2 * k + 2, 2))]
        return out

    def bind(self, refs, jobs, tiles):
        refs = list(refs)
        cube = (2,) * self.nz
        self.own = tiles.at[0, :, 0] if self.tiles_only else refs.pop(0)
        self.got_core = refs.pop(0)
        self.got_cube = self.got_core.reshape((2,) + cube + (self.r, LANES))
        if self.tiles_only:
            self.tile_cube = tiles.reshape((2,) + cube + (2, self.r, LANES))
        else:
            self.own_cube = self.own.reshape(cube + (self.r, LANES))
        self.send, self.keep, self.got = {}, {}, {}
        for p in range(2):
            for i in range(self.stages):
                self.send[p, i], self.keep[p, i], self.got[p, i] = refs.pop(0), refs.pop(0), refs.pop(0)
        self.fin, self.got_fin, self.ostage, self.ssem, self.rsem = refs
        self.jobs = jobs
        self.starts = [job[0] for job in jobs]
        self.me, self.band = lax.axis_index("dp"), lax.axis_index("band")

    def place(self, axis):
        return self.band if axis == 0 else lax.rem(self.me // (1 << axis), 2)

    def partner(self, axis):
        if axis == 0:
            return (self.me, 1 - self.band)
        bit = 1 if axis == -1 else 1 << axis
        here = lax.rem(self.me // bit, 2)
        return (self.me + bit - 2 * bit * here, self.band)

    def barrier(self):
        sem = pltpu.get_barrier_semaphore()
        everyone = [-1, 0] + self.bits
        for axis in everyone:
            pl.semaphore_signal(sem, inc=1, device_id=self.partner(axis), device_id_type=pl.DeviceIdType.MESH)
        pl.semaphore_wait(sem, len(everyone))

    def remote(self, src, dst, s, slot, axis):
        return pltpu.make_async_remote_copy(
            src_ref=src,
            dst_ref=dst,
            send_sem=self.ssem.at[s],
            recv_sem=self.rsem.at[s, slot],
            device_id=self.partner(axis),
            device_id_type=pl.DeviceIdType.MESH,
        )

    def core_copy(self, slot, src):
        return self.remote(src, self.got_core.at[slot], 2 * self.stages, slot, -1)

    def part_copy(self, p, i, slot):
        return self.remote(self.send[p, i], self.got[p, i].at[slot], 2 * i + p, slot, self.orders[p][i])

    def fin_copy(self, slot):
        return self.remote(self.fin, self.got_fin.at[slot], 2 * self.stages + 1, slot, 0)

    def pick(self, axes, axis, at):
        return tuple(at if a == axis else slice(None) for a in axes)

    def split_core(self, j, p):
        slot = lax.rem(j, 2)
        first = self.orders[p][0]
        mine = self.place(first)
        for dst, at in ((self.send[p, 0], 1 - mine), (self.keep[p, 0], mine)):
            if first == 0:
                lanes = pl.ds(pl.multiple_of((2 * p + at) * 128, 128), 128)
                idx = (slice(None),) * (self.nz + 1) + (lanes,)
                dst[...] = self.mine(slot, idx) + self.got_cube[(slot,) + idx]
            else:
                for b in range(2):
                    lanes = slice((2 * p + b) * 128, (2 * p + b + 1) * 128)
                    idx = self.pick(self.bits, first, at) + (slice(None), lanes)
                    dst[(slice(None),) * (self.nz - 1) + (b,)] = self.mine(slot, idx) + self.got_cube[(slot,) + idx]

    def split(self, j, p, i):
        slot = lax.rem(j, 2)
        axes = [a for a in self.bits + [0] if a not in self.orders[p][:i]]
        axis = self.orders[p][i]
        mine = self.place(axis)
        for dst, at in ((self.send[p, i], 1 - mine), (self.keep[p, i], mine)):
            idx = self.pick(axes, axis, at)
            dst[...] = self.keep[p, i - 1][idx] + self.got[p, i - 1][(slot,) + idx]

    def stage(self, s, j):
        k = self.stages
        slot = lax.rem(j, 2)
        if s == 0:
            self.each(j, 1)
        elif s == 1:
            self.core_copy(slot, self.own).wait()
            if not self.tiles_only:
                self.own_copy(self.own).wait()
            for p in range(2):
                self.split_core(j, p)
                self.part_copy(p, 0, slot).start()
        elif s <= k:
            for p in range(2):
                self.part_copy(p, s - 2, slot).wait()
                self.split(j, p, s - 1)
                self.part_copy(p, s - 1, slot).start()
        elif s == k + 1:
            for p in range(2):
                self.part_copy(p, k - 1, slot).wait()
                self.fin[p] = self.keep[p, k - 1][...] + self.got[p, k - 1][slot]
            self.fin_copy(slot).start()
        elif s == k + 2:
            self.fin_copy(slot).wait()
            for p in range(2):
                mine = pl.ds(pl.multiple_of((2 * p + self.band) * 128, 128), 128)
                other = pl.ds(pl.multiple_of((2 * p + 1 - self.band) * 128, 128), 128)
                self.ostage[:, mine] = self.fin[p].astype(F32)
                self.ostage[:, other] = self.got_fin[slot, p].astype(F32)
            self.each(j, 2)
        else:
            self.out_copy(self.ostage).wait()

    def each(self, j, part):
        for i, job in enumerate(self.jobs):
            pl.when(j == i)(functools.partial(job[part], self, i % 2))

    def own_copy(self, src):
        return pltpu.make_async_copy(src, self.own, self.ssem.at[2 * self.stages + 2])

    def out_copy(self, dst, src=None):
        return pltpu.make_async_copy(self.ostage if src is None else src, dst, self.ssem.at[2 * self.stages + 3])

    def mine(self, slot, idx):
        if self.tiles_only:
            return self.tile_cube[(slot,) + idx[: self.nz] + (lax.rem(self.me, 2),) + idx[self.nz :]]
        return self.own_cube[idx]

    def start_pair(self, slot, ref, at):
        core = lax.rem(self.me, 2)
        if not self.tiles_only:
            self.own_copy(ref.at[(slice(None), core) + at]).start()
        self.core_copy(slot, ref.at[(slice(None), 1 - core) + at]).start()

    def tick(self, t):
        for s in reversed(range(self.depth)):
            u = t - s
            before = sum(jnp.where(u > at, 1, 0) for at in self.starts)
            upto = sum(jnp.where(u >= at, 1, 0) for at in self.starts)

            @pl.when(upto > before)
            def _():
                self.stage(s, before)

    def plain(self, src, dst, send_sem, recv_sem, axis):
        return pltpu.make_async_remote_copy(
            src_ref=src,
            dst_ref=dst,
            send_sem=send_sem,
            recv_sem=recv_sem,
            device_id=self.partner(axis),
            device_id_type=pl.DeviceIdType.MESH,
        )


def cube_shape(red, rows, cols):
    return (red.dp // 2, 2, rows // (red.r * red.dp), red.r, cols)


def lanes_at(i, width=LANES):
    return slice(i * width, (i + 1) * width)


def array_job(start, src, dst, q, i, q_out=None):
    def begin(red, slot):
        red.start_pair(slot, src, (q, slice(None), lanes_at(i)))

    def end(red, slot):
        red.out_copy(dst.at[q if q_out is None else q_out, :, lanes_at(i)]).start()

    return start, begin, end


def tile_job(start, tiles, at, parts):
    width = LANES // len(parts)

    def begin(red, slot):
        red.start_pair(slot, tiles.at[at], ())

    def end(red, slot):
        for n, dst in enumerate(parts):
            red.out_copy(dst, red.ostage.at[:, lanes_at(n, width)]).start()

    return start, begin, end


def tile_scratch(red):
    return pltpu.VMEM((2, red.dp // 2, 2, red.r, LANES), BF16)


def put_tile(red, tiles, slot, v):
    tiles[slot] = v.reshape(tiles.shape[1:]).astype(BF16)


SCALE = HEAD_DIM**-0.5
SCALE2 = SCALE * LOG2E


def head_masks(rows):
    left = lax.broadcasted_iota(jnp.int32, (rows, 128), 1) < 64
    return left, jnp.logical_not(left)


def only(mask, v):
    return jnp.where(mask, v, jnp.zeros_like(v))


def each_window(r, body):
    for first, rows, at, shared in ((4, r, 6 * r, True), (0, r, 0, False), (2, 2 * r, 2 * r, False)):
        yield functools.partial(window_pair, r, first, rows, at, shared, body)


def window_pair(r, first, rows, at, shared, body):
    def one(i, _):
        q0 = pl.multiple_of(at + i * rows, 32)
        k0 = pl.multiple_of(2 * r * i, 32) if shared else q0
        body(first + i, i, pl.ds(q0, rows), pl.ds(k0, 2 * r if shared else rows), shared)
        return 0

    lax.fori_loop(0, 2, one, 0)


def fill_shared(scratch, own_ref, halo_ref, r):
    for w in range(2):
        scratch[2 * r * w : 2 * r * w + r, :] = own_ref[(6 + w) * r : (7 + w) * r, :]
        scratch[2 * r * w + r : 2 * r * (w + 1), :] = halo_ref[r * w : r * (w + 1), :]


def attn_fwd_kernel(live_ref, q_ref, k_ref, v_ref, kh_ref, vh_ref, o_ref, lse_ref, kc, vc):
    r = q_ref.shape[0] // 8
    fill_shared(kc, k_ref, kh_ref, r)
    fill_shared(vc, v_ref, vh_ref, r)
    bias = halo_bias(live_ref, (1, 2 * r), 1, r)
    for w, (q0, qn) in enumerate(((0, r), (r, r), (2 * r, 2 * r), (4 * r, 2 * r), (6 * r, r), (7 * r, r))):
        rows = slice(q0, q0 + qn)
        q = q_ref[rows, :]
        if w < 4:
            k, v = k_ref[rows, :], v_ref[rows, :]
        else:
            keys = slice(2 * r * (w - 4), 2 * r * (w - 3))
            k, v = kc[keys, :], vc[keys, :]
        masks = head_masks(qn)
        o, lse = [], []
        for mask in masks:
            s = dot(only(mask, q), k, 1, 1) * SCALE2
            if w >= 4:
                s = s + bias
            top = jnp.max(s, axis=-1, keepdims=True)
            e = jnp.exp2(s - top)
            total = jnp.sum(e, axis=-1, keepdims=True)
            o.append(dot(e.astype(BF16), v) * (1.0 / total))
            lse.append(top + jnp.log2(total))
        o_ref[rows, :] = jnp.where(masks[0], o[0], o[1]).astype(BF16)
        turned = jnp.transpose(jnp.where(masks[0], lse[0], lse[1]))
        for h in range(2):
            lse_ref[w, h : h + 1, :qn] = turned[64 * h : 64 * h + 1, :]


def lse_lanes(t):
    return pl.cdiv(t // 4, 128) * 128


def attn_fwd(live, q, k, v, kh, vh):
    t, d = q.shape
    th = kh.shape[0]
    big = pl.BlockSpec((t, 128), lambda n: (0, n))
    small = pl.BlockSpec((th, 128), lambda n: (0, n))
    return pl.pallas_call(
        attn_fwd_kernel,
        grid=(d // 128,),
        in_specs=[pl.BlockSpec(memory_space=pltpu.SMEM), big, big, big, small, small],
        out_specs=[big, pl.BlockSpec((None, 6, 8, lse_lanes(t)), lambda n: (n, 0, 0, 0))],
        out_shape=[jax.ShapeDtypeStruct((t, d), BF16), jax.ShapeDtypeStruct((d // 128, 6, 8, lse_lanes(t)), F32)],
        scratch_shapes=[pltpu.VMEM((2 * th, 128), BF16)] * 2,
        compiler_params=params(),
        name="attn_fwd",
        cost_estimate=pl.CostEstimate(flops=t * t * d, bytes_accessed=12 * t * d, transcendentals=t * t * 3),
    )(live, q, k, v, kh, vh)


def mid_kernel(
    g_hbm, live_ref, att_ref, w_ref, x_ref, mod_ref, ao_ref, mid_ref, nm_ref, nmt_ref, attt_ref, gw_ref, gm_ref, stage, sem
):
    step = pl.program_id(0)
    band = lax.axis_index("band")
    live = own_live(live_ref)
    n_group = stage.shape[0]
    rows = gw_ref.shape[0] // n_group

    @pl.when(step == 0)
    def _():
        for s in range(n_group):
            spot_copy(g_hbm, stage, band, s, sem).start()

    attn_out = dot(att_ref[...], w_ref[...])
    middle = x_ref[...].astype(F32) + (live * mod_ref[2:3, :]) * attn_out
    ao_ref[...] = attn_out.astype(BF16)
    mid_ref[...] = middle
    n, _ = norm_stats(middle)
    nm = (n * (1.0 + mod_ref[4:5, :]) + mod_ref[3:4, :]).astype(BF16)
    nm_ref[...] = nm
    nmt_ref[...] = jnp.transpose(nm)
    attt_ref[...] = jnp.transpose(att_ref[...])
    for k in range(4):

        @pl.when(step == k + 1)
        def _():
            for s in range(2 * k, 2 * k + 2):
                spot_copy(g_hbm, stage, band, s, sem).wait()
                g = stage[s].astype(F32).reshape(rows, stage.shape[-1])
                part = slice(s * rows, (s + 1) * rows)
                gw_ref[part, :] = g.astype(BF16)
                gm_ref[part, :] = ((live * mod_ref[5:6, :]) * g).astype(BF16)


def mid(cot, live, attended, w_out, xw, mod):
    t, d = xw.shape
    frames = cot.shape[1]
    blk = pl.BlockSpec((t // 5, d), lambda m: (m, 0))
    blk_t = pl.BlockSpec((d, t // 5), lambda m: (0, m))
    full = pl.BlockSpec((t, d), lambda m: (0, 0))
    bf, f32 = jax.ShapeDtypeStruct((t, d), BF16), jax.ShapeDtypeStruct((t, d), F32)
    bf_t = jax.ShapeDtypeStruct((d, t), BF16)
    return pl.pallas_call(
        mid_kernel,
        grid=(5,),
        in_specs=[ANY, pl.BlockSpec(memory_space=pltpu.SMEM), blk, whole((d, d)), blk, whole((6, d))],
        out_specs=[blk, blk, blk, blk_t, blk_t, full, full],
        out_shape=[bf, f32, bf, bf_t, bf_t, bf, bf],
        scratch_shapes=[pltpu.VMEM((8, frames, 4, 8, d), BF16), pltpu.SemaphoreType.DMA((8,))],
        compiler_params=params(),
        name="mid",
        cost_estimate=pl.CostEstimate(flops=2 * t * d * d, bytes_accessed=22 * t * d, transcendentals=0),
    )(cot, live, attended, w_out, xw, mod)


GELU_C = 0.7978845608
GELU_A = 0.044715


def col_sum(v):
    return jnp.sum(v, axis=0, keepdims=True)


def norm_back(h, n, r, gain):
    e = h * (1.0 + gain)
    return r * (e - jnp.mean(e, axis=-1, keepdims=True) - n * jnp.mean(e * n, axis=-1, keepdims=True))


def add_sums(ref, first, rows):
    sums = jnp.concatenate(rows + [jnp.zeros((ref.shape[0] - len(rows), ref.shape[1]), F32)], axis=0)

    @pl.when(first)
    def _():
        ref[...] = sums

    @pl.when(jnp.logical_not(first))
    def _():
        ref[...] += sums


def put_groups(out, stage, out_hbm, sem, block, blocks):
    band = lax.axis_index("band")
    slots = stage.shape[0]
    n_group = 8
    per = n_group // blocks
    rows = out.shape[0] // per
    for k in range(blocks):

        @pl.when(block == k)
        def _():
            for i in range(per):
                s = k * per + i
                if s >= slots:
                    spot_copy(out_hbm, stage, band, s - slots, sem, out=True).wait()
                stage[s % slots] = out[i * rows : (i + 1) * rows, :].reshape(stage.shape[1:]).astype(BF16)
                spot_copy(out_hbm, stage, band, s, sem, out=True).start()

    @pl.when(block == blocks - 1)
    def _():
        for s in range(n_group - slots, n_group):
            spot_copy(out_hbm, stage, band, s, sem, out=True).wait()


PIECES = 4


class Tiling:
    def __init__(self, ff, dp):
        self.steps = ff // LANES
        self.width = LANES // PIECES
        self.early = ff // dp == 2 * self.width

    def piece(self, i, k):
        if not self.early:
            return PIECES * i + k
        half = self.steps // 2
        return (i % half * PIECES + k) * 2 + i // half


def window_back(w, rows, keys, bias, q_ref, k_ref, v_ref, do, lse_ref):
    q, k, v = q_ref[rows, :], k_ref[keys, :], v_ref[keys, :]
    kt = jnp.transpose(k)
    dq, dk, dv = [], [], []
    for h, mask in enumerate(head_masks(rows.size)):
        s = dot(k, only(mask, q), 1, 1) * SCALE2
        if bias is not None:
            s = s + bias
        p = jnp.exp2(s - lse_ref[w, h : h + 1, : rows.size])
        dp = dot(v, only(mask, do), 1, 1)
        total = jnp.sum(p * dp, axis=0, keepdims=True)
        ds = (p * (dp - total)).astype(BF16)
        dv.append(dot(p.astype(BF16), do))
        dk.append(dot(ds, q))
        dq.append(dot(kt[64 * h : 64 * h + 64, :], ds))
    left = head_masks(keys.size)[0]
    dq = jnp.transpose(jnp.concatenate(dq, axis=0)) * SCALE
    return dq, jnp.where(left, dk[0], dk[1]) * SCALE, jnp.where(left, dv[0], dv[1])


TILES = ((("q", 0), ("k", 0)), (("v", 0), ("v", 1)), (("q", 1), ("k", 1)), (("q", 2), ("k", 2)), (("v", 2), ("v", 3)), (("q", 3), ("k", 3)))
TILE_SLOTS = (0, 0, 1, 0, 1, 0)
MADE = {2: (0,), 4: (1, 2), 6: (3,), 8: (4, 5)}


class Plan:
    def __init__(self, n_ff, n_att, early):
        self.n_ff, self.n_att = n_ff, n_att
        self.post = n_ff
        self.out = n_ff + 4
        self.att = self.out + 1
        self.fin = self.att + n_att
        self.steps = self.fin + 4
        self.end = self.fin + 8
        a = self.att
        self.up = [(0, i + 1) for i in range(n_ff)]
        self.o_proj = [(0, a), (1, a)]
        self.tiles = [(1, a + 3), (1, a + 5), (0, a + 5), (1, a + 7), (1, self.fin + 1), (0, self.fin + 1)]
        late = [(1, n_ff + 1 + i) for i in range(4)]
        self.down = [(1, n_ff // 2 + 1 + i) for i in range(4)] + late if early else late + [(1, a + i) for i in (1, 2, 4, 6)]


def finish(reds, first):
    def body(u, _):
        for red in reds:
            red.tick(u)
        return 0

    lax.fori_loop(first, max(red.starts[-1] + red.depth for red in reds), body, 0)


def core_kernel(
    til, plan, reds, live_ref, nm_hbm, gm_hbm, nmt_hbm, attt_hbm, ndt_hbm, wu_hbm, wo_hbm, wq_hbm,
    wd_ref, mid_ref, g_ref, ao_ref, mod_ref, wk_ref, wv_ref, q_ref, k_ref, v_ref, lse_ref, kh_ref, vh_ref, x_ref,
    out_hbm, gin_hbm, sums_ref, dwd_hbm, gup_hbm, gdown_hbm, gout_hbm, gq_hbm, gk_hbm, gv_hbm,
    buf_a, buf_b, buf_c, buf_t, mo, h, do_s, w0, wu, dwd, tiles, kc, vc, own, hsend, hrecv,
    hsem, wsem, lsem, stage, sem, sums_m, sums_a, sums_got, *scratch,
):
    step, steps = pl.program_id(0), pl.num_programs(0)
    n_ff, n_att, width = plan.n_ff, plan.n_att, til.width
    t, d = mo.shape
    chunk = t // 4
    r = t // 8
    red = reds[0]

    def up_at(i, k):
        return pl.ds(pl.multiple_of(til.piece(i, k) * width, width), width)

    def load_up(i, k):
        slot = lax.rem(i, 2)
        return pltpu.make_async_copy(wu_hbm.at[:, up_at(i, k)], wu.at[slot, :, lanes_at(k, width)], wsem.at[slot, k])

    def store_down(i, k):
        if til.early:
            d_at = til.piece(i, k) // 2
            dst = dwd_hbm.at[d_at // 2, lax.rem(d_at, 2), pl.ds(2 * lax.rem(til.piece(i, k), 2), 2)]
        else:
            dst = dwd_hbm.at[pl.ds(til.piece(i, k) * width, width), :]
        return pltpu.make_async_copy(dwd.at[k], dst, wsem.at[2, k])

    def load(n):
        pairs = ((nm_hbm, buf_b), (gm_hbm, buf_c), (nmt_hbm, buf_t), (wo_hbm, w0), (attt_hbm, buf_t), (ndt_hbm, buf_t), (wq_hbm, w0))
        return pltpu.make_async_copy(*pairs[n], lsem.at[n])

    grad_of = {"q": (buf_a, gq_hbm), "k": (buf_b, gk_hbm), "v": (buf_c, gv_hbm)}
    cube = dwd_hbm if til.early else dwd_hbm.reshape(cube_shape(red, dwd_hbm.shape[0], d))
    wide = d // LANES
    jobs = ([], [])
    for i, (at, start) in enumerate(plan.up):
        jobs[at].append(tile_job(start, tiles, i % 2, [gup_hbm.at[:, lanes_at(til.piece(i, k), width)] for k in range(PIECES)]))
    for n, (at, start) in enumerate(plan.down):
        jobs[at].append(array_job(start, cube, gdown_hbm, n // wide, n % wide))
    for n, (at, start) in enumerate(plan.o_proj):
        jobs[at].append(tile_job(start, tiles, n, [gout_hbm.at[:, lanes_at(n)]]))
    for m, (at, start) in enumerate(plan.tiles):
        jobs[at].append(tile_job(start, tiles, TILE_SLOTS[m], [grad_of[n][1].at[:, lanes_at(i, 256)] for n, i in TILES[m]]))
    size = len(scratch) // 2
    for i in range(2):
        reds[i].bind(scratch[i * size : (i + 1) * size + i], sorted(jobs[i], key=lambda job: job[0]), tiles)

    def swap(i):
        slot = lax.rem(i, 2)
        return red.plain(hsend, hrecv.at[slot], hsem.at[0], hsem.at[1 + slot], 0)

    @pl.when(step == 0)
    def _():
        for k in range(PIECES):
            load_up(0, k).start()
        for n in range(4):
            load(n).start()
        mo[...] = jnp.zeros_like(mo)
        h[...] = jnp.zeros_like(h)
        red.barrier()
        load(0).wait()
        load(1).wait()

    for one in reds:
        one.tick(step + jnp.maximum(step - plan.fin, 0))

    @pl.when(step < n_ff)
    def _():
        slot = lax.rem(step, 2)
        for k in range(PIECES):
            load_up(step, k).wait()

        @pl.when(step + 1 < n_ff)
        def _():
            for k in range(PIECES):
                load_up(step + 1, k).start()

        wd = wd_ref[...].reshape(LANES, d)
        up = wu.at[slot]

        def rows(i, _):
            part = pl.ds(pl.multiple_of(i * chunk, chunk), chunk)
            v = dot(buf_b[part, :], up[...])
            gh = dot(buf_c[part, :], wd, 1, 1)
            v2 = v * v
            th = jnp.tanh(v * (GELU_C + (GELU_C * GELU_A) * v2))
            half = 0.5 * th + 0.5
            hidden = (v * half).astype(BF16)
            slope = half + (0.5 * v) * (1.0 - th * th) * (GELU_C + (3.0 * GELU_C * GELU_A) * v2)
            gpre = (gh * slope).astype(BF16)
            buf_a[part, :LANES] = hidden
            buf_a[part, LANES : 2 * LANES] = gpre
            mo[part, :] += dot(hidden, wd)
            h[part, :] += dot(gpre, up[...], 1, 1)
            return 0

        lax.fori_loop(0, 4, rows, 0)

        @pl.when(step > 0)
        def _():
            for k in range(PIECES):
                store_down(step - 1, k).wait()

        pl.when(step == 0)(lambda: load(2).wait())
        put_tile(red, tiles, slot, dot(buf_t[...], buf_a[:, LANES : 2 * LANES]))
        dwd[...] = dot(buf_a[:, :LANES], buf_c[...], 0, 0).reshape(dwd.shape).astype(BF16)
        for k in range(PIECES):
            store_down(step, k).start()

    @pl.when((step >= plan.post) & (step < plan.out))
    def _():
        block = step - plan.post

        @pl.when(block == 0)
        def _():
            load(4).start()
            load(3).wait()
            for k in range(PIECES):
                store_down(step - 1, k).wait()

        part = pl.ds(pl.multiple_of(block * chunk, chunk), chunk)
        live = own_live(live_ref)
        middle, g = mid_ref[...], g_ref[...].astype(F32)
        mlp_out, hh = mo[part, :], h[part, :]
        n, rs = norm_stats(middle)
        gmid = g + norm_back(hh, n, rs, mod_ref[4:5, :])
        h[part, :] = gmid
        ga = ((live * mod_ref[2:3, :]) * gmid).astype(BF16)
        buf_b[part, :] = ga
        do_s[part, :] = dot(ga, w0[...], 1, 1).astype(BF16)
        sums = [col_sum(live * ao_ref[...].astype(F32) * gmid), col_sum(hh), col_sum(hh * n), col_sum(live * mlp_out * g)]
        add_sums(sums_m, block == 0, sums)
        put_groups(middle + (live * mod_ref[5:6, :]) * mlp_out, stage, out_hbm, sem, block, 4)

    @pl.when(step == plan.out)
    def _():
        load(6).start()
        load(4).wait()
        for n in range(wide):
            put_tile(red, tiles, n, dot(buf_t[...], buf_b[:, lanes_at(n)]))
        load(5).start()

    now = step - plan.att

    @pl.when((now > 0) & (now <= n_att))
    def _():
        swap(now - 1).wait()
        slot = lax.rem(now - 1, 2)
        lanes = pl.ds(pl.multiple_of((now - 1) * 128, 128), 128)
        for i, ref in enumerate((buf_b, buf_c)):
            ref[6 * r :, lanes] = (own[i] + hrecv[slot, i].astype(F32)).astype(BF16)

    for at, made in MADE.items():

        @pl.when(now == at)
        def _():
            if at == min(MADE):
                load(5).wait()
            for m in made:
                cols = [grad_of[n][0][:, lanes_at(i, 256)] for n, i in TILES[m]]
                put_tile(red, tiles, TILE_SLOTS[m], dot(buf_t[...], jnp.concatenate(cols, axis=1)))

    @pl.when((now >= 0) & (now < n_att))
    def _():
        slot = lax.rem(now, 2)
        lanes = pl.ds(pl.multiple_of(now * 128, 128), 128)
        fill_shared(kc, k_ref, kh_ref, r)
        fill_shared(vc, v_ref, vh_ref, r)
        bias = halo_bias(live_ref, (2 * r, 1), 0, r)

        def window(w, i, rows, keys, shared):
            data = (bias, q_ref, kc, vc) if shared else (None, q_ref, k_ref, v_ref)
            dq, dk, dv = window_back(w, rows, keys, *data, do_s[rows, lanes], lse_ref)
            buf_a[rows, lanes] = dq.astype(BF16)
            if shared:
                part = pl.ds(pl.multiple_of(i * r, 32), r)
                for n, v in enumerate((dk, dv)):
                    own[n, part, :] = v[:r, :]
                    hsend[n, part, :] = v[r:, :].astype(BF16)
            else:
                buf_b[rows, lanes] = dk.astype(BF16)
                buf_c[rows, lanes] = dv.astype(BF16)

        pairs = list(each_window(r, window))
        pairs[0]()
        swap(now).start()
        pairs[1]()
        pairs[2]()

    @pl.when(step >= plan.fin)
    def _():
        i = step - plan.fin
        pl.when(i == 0)(lambda: load(6).wait())
        part = pl.ds(pl.multiple_of(i * chunk, chunk), chunk)
        hh = dot(buf_a[part, :], w0[...], 1, 1) + dot(buf_b[part, :], wk_ref[...], 1, 1)
        for one in reds:
            one.tick(plan.fin + 2 * i + 1)
        hh = hh + dot(buf_c[part, :], wv_ref[...], 1, 1)
        n, rs = norm_stats(x_ref[...].astype(F32))
        add_sums(sums_a, i == 0, [col_sum(hh), col_sum(hh * n)])
        put_groups(h[part, :] + norm_back(hh, n, rs, mod_ref[1:2, :]), stage, gin_hbm, sem, i, 4)

    @pl.when(step == steps - 1)
    def _():
        rows = [sums_a[0:2, :], sums_m[0:4, :], jnp.zeros((2, d), F32)]
        sums_a[...] = jnp.concatenate(rows, axis=0)
        other = red.plain(sums_a, sums_got, hsem.at[3], hsem.at[4], 0)
        other.start()
        finish(reds, plan.end)
        other.wait()
        sums_ref[...] = sums_a[...] + sums_got[...]


def core(live, nm, gm, nmt, attt, ndt, w_up, w_down, wo, wq, wk, wv, middle, gw, ao, mod, q, k, v, lse, kh, vh, xw, like):
    t, d = nm.shape
    ff = w_up.shape[1]
    th = kh.shape[0]
    frames = like.shape[1]
    dp = lax.axis_size("dp")
    til = Tiling(ff, dp)
    n_ff, n_att = til.steps, d // 128
    plan = Plan(n_ff, n_att, til.early)
    rest = tuple(range(3, dp.bit_length() - 1))
    reds = [Reduce(dp, d, ((0, 1, 2, *rest), (1, 2, 0, *rest)), i == 0) for i in range(2)]
    red = reds[0]

    def block_at(first, count):
        return lambda i: (jnp.clip(i - first, 0, count - 1), 0)

    def lane_at(i):
        return 0, jnp.clip(i - plan.att, 0, n_att - 1)

    post = pl.BlockSpec((t // 4, d), block_at(plan.post, 4))
    last = pl.BlockSpec((t // 4, d), block_at(plan.fin, 4), pipeline_mode=pl.Buffered(1))
    big, small = pl.BlockSpec((t, 128), lane_at), pl.BlockSpec((th, 128), lane_at)
    lse_spec = pl.BlockSpec((None, 6, 8, lse_lanes(t)), lambda i: (lane_at(i)[1], 0, 0, 0))
    if til.early:
        half = n_ff // 2
        w_down = w_down.reshape(half, PIECES, 2, til.width, d)

        def down_at(i):
            i = jnp.minimum(i, n_ff - 1)
            return lax.rem(i, half), 0, i // half, 0, 0

        down = pl.BlockSpec((None, PIECES, None, til.width, d), down_at)
        cube, down_tile = cube_shape(red, ff, d), (PIECES, 2, red.r, d)
    else:
        down = pl.BlockSpec((LANES, d), block_at(0, n_ff))
        cube, down_tile = (ff, d), (PIECES, til.width, d)
    smem = pl.BlockSpec(memory_space=pltpu.SMEM)
    full = pl.BlockSpec((8, d), lambda i: (0, 0))
    image, sums = jax.ShapeDtypeStruct(like.shape, BF16), jax.ShapeDtypeStruct((8, d), F32)
    share = jax.ShapeDtypeStruct((red.r, d), F32)
    act, act32 = pltpu.VMEM((t, d), BF16), pltpu.VMEM((t, d), F32)
    return pl.pallas_call(
        functools.partial(core_kernel, til, plan, reds),
        grid=(plan.steps,),
        in_specs=[smem] + [ANY] * 8 + [down, post, post, post, whole((6, d)), whole((d, d)), whole((d, d))]
        + [big] * 3 + [lse_spec] + [small] * 2 + [last],
        out_specs=[ANY, ANY, full] + [ANY] * 7,
        out_shape=[image, image, sums, jax.ShapeDtypeStruct(cube, BF16), jax.ShapeDtypeStruct((red.r, ff), F32)]
        + [jax.ShapeDtypeStruct((ff // d, red.r, d), F32), share, share, share, share],
        scratch_shapes=[
            act,
            act,
            act,
            pltpu.VMEM((d, t), BF16),
            act32,
            act32,
            act,
            pltpu.VMEM((d, d), BF16),
            pltpu.VMEM((2, d, LANES), BF16),
            pltpu.VMEM(down_tile, BF16),
            tile_scratch(red),
            pltpu.VMEM((2 * th, 128), BF16),
            pltpu.VMEM((2 * th, 128), BF16),
            pltpu.VMEM((2, th, 128), F32),
            pltpu.VMEM((2, th, 128), BF16),
            pltpu.VMEM((2, 2, th, 128), BF16),
            pltpu.SemaphoreType.DMA((5,)),
            pltpu.SemaphoreType.DMA((3, PIECES)),
            pltpu.SemaphoreType.DMA((7,)),
            pltpu.VMEM((4, frames, 4, 8, d), BF16),
            pltpu.SemaphoreType.DMA((4,)),
        ]
        + [pltpu.VMEM((8, d), F32)] * 3
        + reds[0].scratch()
        + reds[1].scratch(),
        compiler_params=params(limit=63 * 1024 * 1024, collective_id=1, has_side_effects=True),
        name="core",
        cost_estimate=pl.CostEstimate(
            flops=12 * t * d * (ff + d) + 3 * t * t * d, bytes_accessed=8 * d * ff + 60 * t * d, transcendentals=t * (ff + 3 * t)
        ),
    )(live, nm, gm, nmt, attt, ndt, w_up, wo, wq, w_down, middle, gw, ao, mod, wk, wv, q, k, v, lse, kh, vh, xw)


def results_kernel(n_grad, a_hbm, b_hbm, mod_ref, *refs):
    grads, (a_out, b_out, mod_out), flats = refs[:n_grad], refs[n_grad : n_grad + 3], refs[n_grad + 3 : 2 * n_grad + 3]
    held, sem = refs[-2:]
    loads, stores = [], []
    for n, (src, dst) in enumerate(((a_hbm, a_out), (b_hbm, b_out))):
        for f in range(src.shape[1]):
            loads.append(pltpu.make_async_copy(src.at[0, f], held.at[n, f], sem.at[0, n, f]))
            stores.append(pltpu.make_async_copy(held.at[n, f], dst.at[0, f], sem.at[1, n, f]))
    for c in loads:
        c.start()
    mod_out[0] = mod_ref[0:6, :]
    for src, dst in zip(grads, flats):
        rows, cols = src.shape
        wide = cols // 128
        for g in range(wide):
            dst[pl.ds(g, rows, stride=wide), :] = src[:, lanes_at(g, 128)]
    for load, store in zip(loads, stores):
        load.wait()
        store.start()
    for c in stores:
        c.wait()


def results(image_a, image_b, mod_sums, grads):
    grads = [g.reshape(-1, g.shape[-1]) for g in grads]
    vmem = pl.BlockSpec(memory_space=pltpu.VMEM)
    n = len(grads)
    out = pl.pallas_call(
        functools.partial(results_kernel, n),
        in_specs=[ANY, ANY] + [vmem] * (n + 1),
        out_specs=[ANY, ANY] + [vmem] * (n + 1),
        out_shape=[jax.ShapeDtypeStruct(image_a.shape, BF16)] * 2
        + [jax.ShapeDtypeStruct((1, 6, mod_sums.shape[1]), F32)]
        + [jax.ShapeDtypeStruct((g.size // 128, 128), F32) for g in grads],
        scratch_shapes=[
            pltpu.VMEM((2,) + image_a.shape[1:], BF16),
            pltpu.SemaphoreType.DMA((2, 2, image_a.shape[1])),
        ],
        compiler_params=params(),
        name="results",
        cost_estimate=pl.CostEstimate(flops=0, bytes_accessed=8 * image_a.size, transcendentals=0),
    )(image_a, image_b, mod_sums, *grads)
    return out[0], out[1], out[2], *(g.reshape(-1) for g in out[3:])


def on_device(
    block_input, modulation, band_live, w_query, w_key, w_value, w_out, w_up, w_down, cotangent
):
    assert lax.axis_size("band") == 2 and block_input.shape[2:4] == (16, 16)
    mod = modulation[0]
    xw, ndt, q, k, v, kh, vh = pre(block_input, mod, w_query, w_key, w_value)
    attended, lse = attn_fwd(band_live, q, k, v, kh, vh)
    ao, middle, nm, nmt, attt, gw, gm = mid(cotangent, band_live, attended, w_out, xw, mod)
    block_output, grad_input, mod_sums, _, g_up, g_down, g_out, g_query, g_key, g_value = core(
        band_live, nm, gm, nmt, attt, ndt, w_up, w_down, w_out, w_query, w_key, w_value,
        middle, gw, ao, mod, q, k, v, lse, kh, vh, xw, block_input,
    )
    return results(block_output, grad_input, mod_sums, (g_query, g_key, g_value, g_out, g_up, g_down))


def solution(mesh):
    return jax.shard_map(
        on_device,
        mesh=mesh,
        in_specs=(
            P("dp", None, "band", None, None),
            P("dp", None, None),
            P("dp", None),
            P(),
            P(),
            P(),
            P(),
            P(),
            P(),
            P("dp", None, "band", None, None),
        ),
        out_specs=(
            P("dp", None, "band", None, None),
            P("dp", None, "band", None, None),
            P("dp", None, None),
            P("dp"),
            P("dp"),
            P("dp"),
            P("dp"),
            P("dp"),
            P("dp"),
        ),
        check_vma=False,
    )
```

```python
import functools

import jax
import jax.numpy as jnp
from jax import lax
from jax.experimental import pallas as pl
from jax.experimental.pallas import tpu as pltpu
from jax.sharding import PartitionSpec as P

HEADS = 16
HEAD_DIM = 64
EPS = 1e-06
MASKED = -1e30
LOG2E = 1.4426950408889634
F32 = jnp.float32
BF16 = jnp.bfloat16
ANY = pl.BlockSpec(memory_space=pl.ANY)
VMEM_LIMIT = 60 * 1024 * 1024

MID_SPOTS = ((1, 0), (2, 0), (1, 1), (2, 1))


def group_spot(band, s):
    lone = 3 * band
    paired = 3 - 3 * band
    if s < 2:
        return lone, s
    if s < 6:
        return MID_SPOTS[s - 2]
    return paired, s - 6


def params(limit=VMEM_LIMIT, **kw):
    return pltpu.CompilerParams(vmem_limit_bytes=limit, **kw)


def dot(a, b, ca=1, cb=0):
    return lax.dot_general(a, b, (((ca,), (cb,)), ((), ())), preferred_element_type=F32)


def whole(shape):
    return pl.BlockSpec(shape, lambda *_: (0,) * len(shape), pipeline_mode=pl.Buffered(1))


def own_live(flags):
    return jnp.where(flags[0, lax.axis_index("band")] == 1, 1.0, 0.0)


def halo_bias(flags, shape, dim, r):
    band = lax.axis_index("band")
    other = jnp.where(flags[0, 1 - band] == 1, 0.0, MASKED)
    off = jnp.where(flags[0, band] == 1, other, 0.0)
    return jnp.where(lax.broadcasted_iota(jnp.int32, shape, dim) >= r, off, 0.0)


def norm_stats(v):
    c = v - jnp.mean(v, axis=-1, keepdims=True)
    r = lax.rsqrt(jnp.mean(c * c, axis=-1, keepdims=True) + EPS)
    return c * r, r


def spot_copy(hbm, vmem, band, s, sem, out=False):
    g, j = group_spot(band, s)
    there = hbm.at[0, :, pl.ds(g * 4, 4), pl.ds(j * 8, 8), :]
    if out:
        slot = s % vmem.shape[0]
        return pltpu.make_async_copy(vmem.at[slot], there, sem.at[slot])
    return pltpu.make_async_copy(there, vmem.at[s], sem.at[s])


def pre_kernel(
    x_hbm, g_hbm, live_ref, mod_ref, wq_ref, wk_ref, wv_ref,
    xw_ref, ndt_ref, gw_ref, gm_ref, q_ref, k_ref, v_ref, kh_ref, vh_ref,
    stage, halo, sem, swap_sem, nsc, nhalo,
):
    step, n_tile = pl.program_id(0), pl.num_programs(0) // 2
    band = lax.axis_index("band")
    n_group = stage.shape[0]
    rows = nsc.shape[0] // n_group
    there = (lax.axis_index("dp"), 1 - band)

    def normed(x):
        n, _ = norm_stats(x)
        return (n * (1.0 + mod_ref[1:2, :]) + mod_ref[0:1, :]).astype(BF16)

    swap = pltpu.make_async_remote_copy(
        src_ref=x_hbm.at[0, :, pl.ds(12 - 12 * band, 4)],
        dst_ref=halo,
        send_sem=swap_sem.at[0],
        recv_sem=swap_sem.at[1],
        device_id=there,
        device_id_type=pl.DeviceIdType.MESH,
    )

    @pl.when(step == 0)
    def _():
        for s in range(n_group):
            spot_copy(x_hbm, stage, band, s, sem).start()
        entered = pltpu.get_barrier_semaphore()
        pl.semaphore_signal(entered, inc=1, device_id=there, device_id_type=pl.DeviceIdType.MESH)
        pl.semaphore_wait(entered, 1)
        swap.start()
        for s in range(n_group):
            spot_copy(x_hbm, stage, band, s, sem).wait()
            x = stage[s].astype(F32).reshape(rows, stage.shape[-1])
            part = slice(s * rows, (s + 1) * rows)
            nsc[part, :] = normed(x)
            xw_ref[part, :] = x.astype(BF16)
        for s in range(n_group):
            spot_copy(g_hbm, stage, band, s, sem).start()

    @pl.when(step < n_tile)
    def _():
        for w_ref, o_ref in ((wq_ref, q_ref), (wk_ref, k_ref), (wv_ref, v_ref)):
            o_ref[...] = dot(nsc[...], w_ref[...]).astype(BF16)

    @pl.when(step == n_tile)
    def _():
        ndt_ref[...] = jnp.transpose(nsc[...])
        gate = own_live(live_ref) * mod_ref[5:6, :]
        for s in range(n_group):
            spot_copy(g_hbm, stage, band, s, sem).wait()
            g = stage[s].astype(F32).reshape(rows, stage.shape[-1])
            part = slice(s * rows, (s + 1) * rows)
            gw_ref[part, :] = g.astype(BF16)
            gm_ref[part, :] = (gate * g).astype(BF16)
        swap.wait()
        for j in range(2):
            x = halo[:, :, 8 * j : 8 * j + 8, :].astype(F32).reshape(rows, halo.shape[-1])
            nhalo[j * rows : (j + 1) * rows, :] = normed(x)

    @pl.when(step >= n_tile)
    def _():
        for w_ref, o_ref in ((wk_ref, kh_ref), (wv_ref, vh_ref)):
            o_ref[...] = dot(nhalo[...], w_ref[...]).astype(BF16)


def pre(x, cot, live, mod, wq, wk, wv):
    d, frames = x.shape[-1], x.shape[1]
    t = 8 * frames * 32
    th = t // 4
    tile = 256
    n_tile = d // tile
    own = pl.BlockSpec((t, tile), lambda n: (0, jnp.minimum(n, n_tile - 1)))
    other = pl.BlockSpec((th, tile), lambda n: (0, jnp.maximum(n - n_tile, 0)))
    once = pl.BlockSpec((d, tile), lambda n: (0, jnp.minimum(n, n_tile - 1)))
    twice = pl.BlockSpec((d, tile), lambda n: (0, lax.rem(n, n_tile)))
    act, act_h = jax.ShapeDtypeStruct((t, d), BF16), jax.ShapeDtypeStruct((th, d), BF16)
    return pl.pallas_call(
        pre_kernel,
        grid=(2 * n_tile,),
        in_specs=[ANY, ANY, pl.BlockSpec(memory_space=pltpu.SMEM), whole((6, d)), once, twice, twice],
        out_specs=[whole((t, d)), whole((d, t)), whole((t, d)), whole((t, d)), own, own, own, other, other],
        out_shape=[act, jax.ShapeDtypeStruct((d, t), BF16), act, act, act, act, act, act_h, act_h],
        scratch_shapes=[
            pltpu.VMEM((8, frames, 4, 8, d), BF16),
            pltpu.VMEM((frames, 4, 16, d), BF16),
            pltpu.SemaphoreType.DMA((8,)),
            pltpu.SemaphoreType.DMA((2,)),
            pltpu.VMEM((t, d), BF16),
            pltpu.VMEM((th, d), BF16),
        ],
        compiler_params=params(collective_id=2, has_side_effects=True),
        name="pre",
        cost_estimate=pl.CostEstimate(flops=7 * t * d * d, bytes_accessed=10 * d * d + 12 * t * d, transcendentals=0),
    )(x, cot, live, mod, wq, wk, wv)


LANES = 512


class Reduce:
    def __init__(self, dp, total_rows, orders, tiles_only):
        self.bits = list(range(dp.bit_length() - 2, 0, -1))
        self.nz = len(self.bits)
        self.stages = self.nz + 1
        self.depth = self.stages + 4
        self.r = total_rows // dp
        self.orders = orders
        self.tiles_only = tiles_only
        self.dp = dp

    def scratch(self):
        r, nz, k = self.r, self.nz, self.stages
        out = [] if self.tiles_only else [pltpu.VMEM((1 << nz, r, LANES), BF16)]
        out += [pltpu.VMEM((2, 1 << nz, r, LANES), BF16)]
        for _ in range(2):
            for i in range(k):
                block = (2,) * (k - 1 - i) + (r, 128)
                out += [pltpu.VMEM(block, BF16), pltpu.VMEM(block, BF16), pltpu.VMEM((2,) + block, BF16)]
        out += [pltpu.VMEM((2, r, 128), BF16), pltpu.VMEM((2, 2, r, 128), BF16), pltpu.VMEM((r, LANES), F32)]
        out += [pltpu.SemaphoreType.DMA((2 * k + 4,)), pltpu.SemaphoreType.DMA((2 * k + 2, 2))]
        return out

    def bind(self, refs, jobs, tiles):
        refs = list(refs)
        cube = (2,) * self.nz
        self.own = tiles.at[0, :, 0] if self.tiles_only else refs.pop(0)
        self.got_core = refs.pop(0)
        self.got_cube = self.got_core.reshape((2,) + cube + (self.r, LANES))
        if self.tiles_only:
            self.tile_cube = tiles.reshape((2,) + cube + (2, self.r, LANES))
        else:
            self.own_cube = self.own.reshape(cube + (self.r, LANES))
        self.send, self.keep, self.got = {}, {}, {}
        for p in range(2):
            for i in range(self.stages):
                self.send[p, i], self.keep[p, i], self.got[p, i] = refs.pop(0), refs.pop(0), refs.pop(0)
        self.fin, self.got_fin, self.ostage, self.ssem, self.rsem = refs
        self.jobs = jobs
        self.starts = [job[0] for job in jobs]
        self.me, self.band = lax.axis_index("dp"), lax.axis_index("band")

    def place(self, axis):
        return self.band if axis == 0 else lax.rem(self.me // (1 << axis), 2)

    def partner(self, axis):
        if axis == 0:
            return (self.me, 1 - self.band)
        bit = 1 if axis == -1 else 1 << axis
        here = lax.rem(self.me // bit, 2)
        return (self.me + bit - 2 * bit * here, self.band)

    def barrier(self):
        sem = pltpu.get_barrier_semaphore()
        everyone = [-1, 0] + self.bits
        for axis in everyone:
            pl.semaphore_signal(sem, inc=1, device_id=self.partner(axis), device_id_type=pl.DeviceIdType.MESH)
        pl.semaphore_wait(sem, len(everyone))

    def remote(self, src, dst, s, slot, axis):
        return pltpu.make_async_remote_copy(
            src_ref=src,
            dst_ref=dst,
            send_sem=self.ssem.at[s],
            recv_sem=self.rsem.at[s, slot],
            device_id=self.partner(axis),
            device_id_type=pl.DeviceIdType.MESH,
        )

    def core_copy(self, slot, src):
        return self.remote(src, self.got_core.at[slot], 2 * self.stages, slot, -1)

    def part_copy(self, p, i, slot):
        return self.remote(self.send[p, i], self.got[p, i].at[slot], 2 * i + p, slot, self.orders[p][i])

    def fin_copy(self, slot):
        return self.remote(self.fin, self.got_fin.at[slot], 2 * self.stages + 1, slot, 0)

    def pick(self, axes, axis, at):
        return tuple(at if a == axis else slice(None) for a in axes)

    def split_core(self, j, p):
        slot = lax.rem(j, 2)
        first = self.orders[p][0]
        mine = self.place(first)
        for dst, at in ((self.send[p, 0], 1 - mine), (self.keep[p, 0], mine)):
            if first == 0:
                lanes = pl.ds(pl.multiple_of((2 * p + at) * 128, 128), 128)
                idx = (slice(None),) * (self.nz + 1) + (lanes,)
                dst[...] = self.mine(slot, idx) + self.got_cube[(slot,) + idx]
            else:
                for b in range(2):
                    lanes = slice((2 * p + b) * 128, (2 * p + b + 1) * 128)
                    idx = self.pick(self.bits, first, at) + (slice(None), lanes)
                    dst[(slice(None),) * (self.nz - 1) + (b,)] = self.mine(slot, idx) + self.got_cube[(slot,) + idx]

    def split(self, j, p, i):
        slot = lax.rem(j, 2)
        axes = [a for a in self.bits + [0] if a not in self.orders[p][:i]]
        axis = self.orders[p][i]
        mine = self.place(axis)
        for dst, at in ((self.send[p, i], 1 - mine), (self.keep[p, i], mine)):
            idx = self.pick(axes, axis, at)
            dst[...] = self.keep[p, i - 1][idx] + self.got[p, i - 1][(slot,) + idx]

    def stage(self, s, j):
        k = self.stages
        slot = lax.rem(j, 2)
        if s == 0:
            self.each(j, 1)
        elif s == 1:
            self.core_copy(slot, self.own).wait()
            if not self.tiles_only:
                self.own_copy(self.own).wait()
            for p in range(2):
                self.split_core(j, p)
                self.part_copy(p, 0, slot).start()
        elif s <= k:
            for p in range(2):
                self.part_copy(p, s - 2, slot).wait()
                self.split(j, p, s - 1)
                self.part_copy(p, s - 1, slot).start()
        elif s == k + 1:
            for p in range(2):
                self.part_copy(p, k - 1, slot).wait()
                self.fin[p] = self.keep[p, k - 1][...] + self.got[p, k - 1][slot]
            self.fin_copy(slot).start()
        elif s == k + 2:
            self.fin_copy(slot).wait()
            for p in range(2):
                mine = pl.ds(pl.multiple_of((2 * p + self.band) * 128, 128), 128)
                other = pl.ds(pl.multiple_of((2 * p + 1 - self.band) * 128, 128), 128)
                self.ostage[:, mine] = self.fin[p].astype(F32)
                self.ostage[:, other] = self.got_fin[slot, p].astype(F32)
            self.each(j, 2)
        else:
            self.out_copy(self.ostage).wait()

    def each(self, j, part):
        for i, job in enumerate(self.jobs):
            pl.when(j == i)(functools.partial(job[part], self, i % 2))

    def own_copy(self, src):
        return pltpu.make_async_copy(src, self.own, self.ssem.at[2 * self.stages + 2])

    def out_copy(self, dst, src=None):
        return pltpu.make_async_copy(self.ostage if src is None else src, dst, self.ssem.at[2 * self.stages + 3])

    def mine(self, slot, idx):
        if self.tiles_only:
            return self.tile_cube[(slot,) + idx[: self.nz] + (lax.rem(self.me, 2),) + idx[self.nz :]]
        return self.own_cube[idx]

    def start_pair(self, slot, ref, at):
        core = lax.rem(self.me, 2)
        if not self.tiles_only:
            self.own_copy(ref.at[(slice(None), core) + at]).start()
        self.core_copy(slot, ref.at[(slice(None), 1 - core) + at]).start()

    def tick(self, t):
        for s in reversed(range(self.depth)):
            u = t - s
            before = sum(jnp.where(u > at, 1, 0) for at in self.starts)
            upto = sum(jnp.where(u >= at, 1, 0) for at in self.starts)

            @pl.when(upto > before)
            def _():
                self.stage(s, before)

    def plain(self, src, dst, send_sem, recv_sem, axis):
        return pltpu.make_async_remote_copy(
            src_ref=src,
            dst_ref=dst,
            send_sem=send_sem,
            recv_sem=recv_sem,
            device_id=self.partner(axis),
            device_id_type=pl.DeviceIdType.MESH,
        )


def cube_shape(red, rows, cols):
    return (red.dp // 2, 2, rows // (red.r * red.dp), red.r, cols)


def lanes_at(i, width=LANES):
    return slice(i * width, (i + 1) * width)


def array_job(start, src, dst, q, i, q_out=None):
    def begin(red, slot):
        red.start_pair(slot, src, (q, slice(None), lanes_at(i)))

    def end(red, slot):
        red.out_copy(dst.at[q if q_out is None else q_out, :, lanes_at(i)]).start()

    return start, begin, end


def tile_job(start, tiles, at, parts):
    width = LANES // len(parts)

    def begin(red, slot):
        red.start_pair(slot, tiles.at[at], ())

    def end(red, slot):
        for n, dst in enumerate(parts):
            red.out_copy(dst, red.ostage.at[:, lanes_at(n, width)]).start()

    return start, begin, end


def tile_scratch(red):
    return pltpu.VMEM((2, red.dp // 2, 2, red.r, LANES), BF16)


def put_tile(red, tiles, slot, v):
    tiles[slot] = v.reshape(tiles.shape[1:]).astype(BF16)


SCALE = HEAD_DIM**-0.5
SCALE2 = SCALE * LOG2E


def head_masks(rows):
    left = lax.broadcasted_iota(jnp.int32, (rows, 128), 1) < 64
    return left, jnp.logical_not(left)


def only(mask, v):
    return jnp.where(mask, v, jnp.zeros_like(v))


def each_window(r, body):
    for first, rows, at, shared in ((4, r, 6 * r, True), (0, r, 0, False), (2, 2 * r, 2 * r, False)):
        yield functools.partial(window_pair, r, first, rows, at, shared, body)


def window_pair(r, first, rows, at, shared, body):
    def one(i, _):
        q0 = at + i * rows
        k0 = 2 * r * i if shared else q0
        body(first + i, i, pl.ds(q0, rows), pl.ds(k0, 2 * r if shared else rows), shared)
        return 0

    for i in range(2):
        one(i, 0)


def fill_shared(scratch, own_ref, halo_ref, r):
    for w in range(2):
        scratch[2 * r * w : 2 * r * w + r, :] = own_ref[(6 + w) * r : (7 + w) * r, :]
        scratch[2 * r * w + r : 2 * r * (w + 1), :] = halo_ref[r * w : r * (w + 1), :]


def attn_fwd_kernel(live_ref, q_ref, k_ref, v_ref, kh_ref, vh_ref, o_ref, lse_ref, kc, vc):
    r = q_ref.shape[0] // 8
    fill_shared(kc, k_ref, kh_ref, r)
    fill_shared(vc, v_ref, vh_ref, r)
    bias = halo_bias(live_ref, (1, 2 * r), 1, r)
    for w, (q0, qn) in enumerate(((0, r), (r, r), (2 * r, 2 * r), (4 * r, 2 * r), (6 * r, r), (7 * r, r))):
        rows = slice(q0, q0 + qn)
        q = q_ref[rows, :]
        if w < 4:
            k, v = k_ref[rows, :], v_ref[rows, :]
        else:
            keys = slice(2 * r * (w - 4), 2 * r * (w - 3))
            k, v = kc[keys, :], vc[keys, :]
        masks = head_masks(qn)
        o, lse = [], []
        for mask in masks:
            s = dot(only(mask, q), k, 1, 1) * SCALE2
            if w >= 4:
                s = s + bias
            top = jnp.max(s, axis=-1, keepdims=True)
            e = jnp.exp2(s - top)
            total = jnp.sum(e, axis=-1, keepdims=True)
            o.append(dot(e.astype(BF16), v) * (1.0 / total))
            lse.append(top + jnp.log2(total))
        o_ref[rows, :] = jnp.where(masks[0], o[0], o[1]).astype(BF16)
        turned = jnp.transpose(jnp.where(masks[0], lse[0], lse[1]))
        for h in range(2):
            lse_ref[w, h : h + 1, :qn] = turned[64 * h : 64 * h + 1, :]


def lse_lanes(t):
    return pl.cdiv(t // 4, 128) * 128


def attn_fwd(live, q, k, v, kh, vh):
    t, d = q.shape
    th = kh.shape[0]
    big = pl.BlockSpec((t, 128), lambda n: (0, n))
    small = pl.BlockSpec((th, 128), lambda n: (0, n))
    return pl.pallas_call(
        attn_fwd_kernel,
        grid=(d // 128,),
        in_specs=[pl.BlockSpec(memory_space=pltpu.SMEM), big, big, big, small, small],
        out_specs=[big, pl.BlockSpec((None, 6, 8, lse_lanes(t)), lambda n: (n, 0, 0, 0))],
        out_shape=[jax.ShapeDtypeStruct((t, d), BF16), jax.ShapeDtypeStruct((d // 128, 6, 8, lse_lanes(t)), F32)],
        scratch_shapes=[pltpu.VMEM((2 * th, 128), BF16)] * 2,
        compiler_params=params(),
        name="attn_fwd",
        cost_estimate=pl.CostEstimate(flops=t * t * d, bytes_accessed=12 * t * d, transcendentals=t * t * 3),
    )(live, q, k, v, kh, vh)


def mid_kernel(live_ref, att_ref, w_ref, x_ref, mod_ref, ao_ref, mid_ref, nm_ref, nmt_ref, attt_ref):
    live = own_live(live_ref)
    attn_out = dot(att_ref[...], w_ref[...])
    middle = x_ref[...].astype(F32) + (live * mod_ref[2:3, :]) * attn_out
    ao_ref[...] = attn_out.astype(BF16)
    mid_ref[...] = middle
    n, _ = norm_stats(middle)
    nm = (n * (1.0 + mod_ref[4:5, :]) + mod_ref[3:4, :]).astype(BF16)
    nm_ref[...] = nm
    nmt_ref[...] = jnp.transpose(nm)
    attt_ref[...] = jnp.transpose(att_ref[...])


def mid(live, attended, w_out, xw, mod):
    t, d = xw.shape
    blk = pl.BlockSpec((t // 5, d), lambda m: (m, 0))
    blk_t = pl.BlockSpec((d, t // 5), lambda m: (0, m))
    bf, f32 = jax.ShapeDtypeStruct((t, d), BF16), jax.ShapeDtypeStruct((t, d), F32)
    bf_t = jax.ShapeDtypeStruct((d, t), BF16)
    return pl.pallas_call(
        mid_kernel,
        grid=(5,),
        in_specs=[pl.BlockSpec(memory_space=pltpu.SMEM), blk, whole((d, d)), blk, whole((6, d))],
        out_specs=[blk, blk, blk, blk_t, blk_t],
        out_shape=[bf, f32, bf, bf_t, bf_t],
        compiler_params=params(),
        name="mid",
        cost_estimate=pl.CostEstimate(flops=2 * t * d * d, bytes_accessed=16 * t * d, transcendentals=0),
    )(live, attended, w_out, xw, mod)


GELU_C = 0.7978845608
GELU_A = 0.044715


def col_sum(v):
    return jnp.sum(v, axis=0, keepdims=True)


def norm_back(h, n, r, gain):
    e = h * (1.0 + gain)
    return r * (e - jnp.mean(e, axis=-1, keepdims=True) - n * jnp.mean(e * n, axis=-1, keepdims=True))


def add_sums(ref, first, rows):
    sums = jnp.concatenate(rows + [jnp.zeros((ref.shape[0] - len(rows), ref.shape[1]), F32)], axis=0)

    @pl.when(first)
    def _():
        ref[...] = sums

    @pl.when(jnp.logical_not(first))
    def _():
        ref[...] += sums


def put_groups(out, stage, out_hbm, sem, block, blocks):
    band = lax.axis_index("band")
    slots = stage.shape[0]
    n_group = 8
    per = n_group // blocks
    rows = out.shape[0] // per
    for k in range(blocks):

        @pl.when(block == k)
        def _():
            for i in range(per):
                s = k * per + i
                if s >= slots:
                    spot_copy(out_hbm, stage, band, s - slots, sem, out=True).wait()
                stage[s % slots] = out[i * rows : (i + 1) * rows, :].reshape(stage.shape[1:]).astype(BF16)
                spot_copy(out_hbm, stage, band, s, sem, out=True).start()

    @pl.when(block == blocks - 1)
    def _():
        for s in range(n_group - slots, n_group):
            spot_copy(out_hbm, stage, band, s, sem, out=True).wait()


PIECES = 4


class Tiling:
    def __init__(self, ff, dp):
        self.steps = ff // LANES
        self.width = LANES // PIECES
        self.early = ff // dp == 2 * self.width

    def piece(self, i, k):
        if not self.early:
            return PIECES * i + k
        half = self.steps // 2
        return (i % half * PIECES + k) * 2 + i // half


def window_back(w, rows, keys, bias, q_ref, k_ref, v_ref, do, lse_ref):
    q, k, v = q_ref[rows, :], k_ref[keys, :], v_ref[keys, :]
    kt = jnp.transpose(k)
    dq, dk, dv = [], [], []
    for h, mask in enumerate(head_masks(rows.size)):
        s = dot(k, only(mask, q), 1, 1) * SCALE2
        if bias is not None:
            s = s + bias
        p = jnp.exp2(s - lse_ref[w, h : h + 1, : rows.size])
        dp = dot(v, only(mask, do), 1, 1)
        total = jnp.sum(p * dp, axis=0, keepdims=True)
        ds = (p * (dp - total)).astype(BF16)
        dv.append(dot(p.astype(BF16), do))
        dk.append(dot(ds, q))
        dq.append(dot(kt[64 * h : 64 * h + 64, :], ds))
    left = head_masks(keys.size)[0]
    dq = jnp.transpose(jnp.concatenate(dq, axis=0)) * SCALE
    return dq, jnp.where(left, dk[0], dk[1]) * SCALE, jnp.where(left, dv[0], dv[1])


TILES = ((("q", 0), ("k", 0)), (("v", 0), ("v", 1)), (("q", 1), ("k", 1)), (("q", 2), ("k", 2)), (("v", 2), ("v", 3)), (("q", 3), ("k", 3)))
TILE_SLOTS = (0, 0, 1, 0, 1, 0)
MADE = {2: (0,), 4: (1, 2), 6: (3,), 8: (4, 5)}


class Plan:
    def __init__(self, n_ff, n_att, early):
        self.n_ff, self.n_att = n_ff, n_att
        self.post = n_ff
        self.out = n_ff + 4
        self.att = self.out + 1
        self.fin = self.att + n_att
        self.steps = self.fin + 4
        self.end = self.fin + 8
        a = self.att
        self.up = [(0, i + 1) for i in range(n_ff)]
        self.o_proj = [(0, a), (1, a)]
        self.tiles = [(1, a + 3), (1, a + 5), (0, a + 5), (1, a + 7), (1, self.fin + 1), (0, self.fin + 1)]
        late = [(1, n_ff + 1 + i) for i in range(4)]
        self.down = [(1, n_ff // 2 + 1 + i) for i in range(4)] + late if early else late + [(1, a + i) for i in (1, 2, 4, 6)]


def finish(reds, first):
    def body(u, _):
        for red in reds:
            red.tick(u)
        return 0

    lax.fori_loop(first, max(red.starts[-1] + red.depth for red in reds), body, 0)


def core_kernel(
    til, plan, reds, live_ref, nm_hbm, gm_hbm, nmt_hbm, attt_hbm, ndt_hbm, wu_hbm, wo_hbm, wq_hbm,
    wd_ref, mid_ref, g_ref, ao_ref, mod_ref, wk_ref, wv_ref, q_ref, k_ref, v_ref, lse_ref, kh_ref, vh_ref, x_ref,
    out_hbm, gin_hbm, sums_ref, dwd_hbm, gup_hbm, gdown_hbm, gout_hbm, gq_hbm, gk_hbm, gv_hbm,
    buf_a, buf_b, buf_c, buf_t, mo, h, do_s, w0, wu, dwd, tiles, kc, vc, own, hsend, hrecv,
    hsem, wsem, lsem, stage, sem, sums_m, sums_a, sums_got, *scratch,
):
    step, steps = pl.program_id(0), pl.num_programs(0)
    n_ff, n_att, width = plan.n_ff, plan.n_att, til.width
    t, d = mo.shape
    chunk = t // 4
    r = t // 8
    red = reds[0]

    def up_at(i, k):
        return pl.ds(pl.multiple_of(til.piece(i, k) * width, width), width)

    def load_up(i, k):
        slot = lax.rem(i, 2)
        return pltpu.make_async_copy(wu_hbm.at[:, up_at(i, k)], wu.at[slot, :, lanes_at(k, width)], wsem.at[slot, k])

    def store_down(i, k):
        if til.early:
            d_at = til.piece(i, k) // 2
            dst = dwd_hbm.at[d_at // 2, lax.rem(d_at, 2), pl.ds(2 * lax.rem(til.piece(i, k), 2), 2)]
        else:
            dst = dwd_hbm.at[pl.ds(til.piece(i, k) * width, width), :]
        return pltpu.make_async_copy(dwd.at[k], dst, wsem.at[2, k])

    def load(n):
        pairs = ((nm_hbm, buf_b), (gm_hbm, buf_c), (nmt_hbm, buf_t), (wo_hbm, w0), (attt_hbm, buf_t), (ndt_hbm, buf_t), (wq_hbm, w0))
        return pltpu.make_async_copy(*pairs[n], lsem.at[n])

    grad_of = {"q": (buf_a, gq_hbm), "k": (buf_b, gk_hbm), "v": (buf_c, gv_hbm)}
    cube = dwd_hbm if til.early else dwd_hbm.reshape(cube_shape(red, dwd_hbm.shape[0], d))
    wide = d // LANES
    jobs = ([], [])
    for i, (at, start) in enumerate(plan.up):
        jobs[at].append(tile_job(start, tiles, i % 2, [gup_hbm.at[:, lanes_at(til.piece(i, k), width)] for k in range(PIECES)]))
    for n, (at, start) in enumerate(plan.down):
        jobs[at].append(array_job(start, cube, gdown_hbm, n // wide, n % wide))
    for n, (at, start) in enumerate(plan.o_proj):
        jobs[at].append(tile_job(start, tiles, n, [gout_hbm.at[:, lanes_at(n)]]))
    for m, (at, start) in enumerate(plan.tiles):
        jobs[at].append(tile_job(start, tiles, TILE_SLOTS[m], [grad_of[n][1].at[:, lanes_at(i, 256)] for n, i in TILES[m]]))
    size = len(scratch) // 2
    for i in range(2):
        reds[i].bind(scratch[i * size : (i + 1) * size + i], sorted(jobs[i], key=lambda job: job[0]), tiles)

    def swap(i):
        slot = lax.rem(i, 2)
        return red.plain(hsend, hrecv.at[slot], hsem.at[0], hsem.at[1 + slot], 0)

    @pl.when(step == 0)
    def _():
        for k in range(PIECES):
            load_up(0, k).start()
        for n in range(4):
            load(n).start()
        mo[...] = jnp.zeros_like(mo)
        h[...] = jnp.zeros_like(h)
        red.barrier()
        load(0).wait()
        load(1).wait()

    for one in reds:
        one.tick(step + jnp.maximum(step - plan.fin, 0))

    @pl.when(step < n_ff)
    def _():
        slot = lax.rem(step, 2)
        for k in range(PIECES):
            load_up(step, k).wait()

        @pl.when(step + 1 < n_ff)
        def _():
            for k in range(PIECES):
                load_up(step + 1, k).start()

        wd = wd_ref[...].reshape(LANES, d)
        up = wu.at[slot]

        def rows(i, _):
            part = pl.ds(pl.multiple_of(i * (2 * chunk), 2 * chunk), 2 * chunk)
            v = dot(buf_b[part, :], up[...])
            gh = dot(buf_c[part, :], wd, 1, 1)
            v2 = v * v
            th = jnp.tanh(v * (GELU_C + (GELU_C * GELU_A) * v2))
            half = 0.5 * th + 0.5
            hidden = (v * half).astype(BF16)
            slope = half + (0.5 * v) * (1.0 - th * th) * (GELU_C + (3.0 * GELU_C * GELU_A) * v2)
            gpre = (gh * slope).astype(BF16)
            buf_a[part, :LANES] = hidden
            buf_a[part, LANES : 2 * LANES] = gpre
            mo[part, :] += dot(hidden, wd)
            h[part, :] += dot(gpre, up[...], 1, 1)
            return 0

        lax.fori_loop(0, 2, rows, 0)

        @pl.when(step > 0)
        def _():
            for k in range(PIECES):
                store_down(step - 1, k).wait()

        pl.when(step == 0)(lambda: load(2).wait())
        put_tile(red, tiles, slot, dot(buf_t[...], buf_a[:, LANES : 2 * LANES]))
        dwd[...] = dot(buf_a[:, :LANES], buf_c[...], 0, 0).reshape(dwd.shape).astype(BF16)
        for k in range(PIECES):
            store_down(step, k).start()

    @pl.when((step >= plan.post) & (step < plan.out))
    def _():
        block = step - plan.post

        @pl.when(block == 0)
        def _():
            load(4).start()
            load(3).wait()
            for k in range(PIECES):
                store_down(step - 1, k).wait()

        part = pl.ds(pl.multiple_of(block * chunk, chunk), chunk)
        live = own_live(live_ref)
        middle, g = mid_ref[...], g_ref[...].astype(F32)
        mlp_out, hh = mo[part, :], h[part, :]
        n, rs = norm_stats(middle)
        gmid = g + norm_back(hh, n, rs, mod_ref[4:5, :])
        h[part, :] = gmid
        ga = ((live * mod_ref[2:3, :]) * gmid).astype(BF16)
        buf_b[part, :] = ga
        do_s[part, :] = dot(ga, w0[...], 1, 1).astype(BF16)
        sums = [col_sum(live * ao_ref[...].astype(F32) * gmid), col_sum(hh), col_sum(hh * n), col_sum(live * mlp_out * g)]
        add_sums(sums_m, block == 0, sums)
        put_groups(middle + (live * mod_ref[5:6, :]) * mlp_out, stage, out_hbm, sem, block, 4)

    @pl.when(step == plan.out)
    def _():
        load(6).start()
        load(4).wait()
        for n in range(wide):
            put_tile(red, tiles, n, dot(buf_t[...], buf_b[:, lanes_at(n)]))
        load(5).start()

    now = step - plan.att

    @pl.when((now > 0) & (now <= n_att))
    def _():
        swap(now - 1).wait()
        slot = lax.rem(now - 1, 2)
        lanes = pl.ds(pl.multiple_of((now - 1) * 128, 128), 128)
        for i, ref in enumerate((buf_b, buf_c)):
            ref[6 * r :, lanes] = (own[i] + hrecv[slot, i].astype(F32)).astype(BF16)

    for at, made in MADE.items():

        @pl.when(now == at)
        def _():
            if at == min(MADE):
                load(5).wait()
            for m in made:
                cols = [grad_of[n][0][:, lanes_at(i, 256)] for n, i in TILES[m]]
                put_tile(red, tiles, TILE_SLOTS[m], dot(buf_t[...], jnp.concatenate(cols, axis=1)))

    @pl.when((now >= 0) & (now < n_att))
    def _():
        slot = lax.rem(now, 2)
        lanes = pl.ds(pl.multiple_of(now * 128, 128), 128)
        fill_shared(kc, k_ref, kh_ref, r)
        fill_shared(vc, v_ref, vh_ref, r)
        bias = halo_bias(live_ref, (2 * r, 1), 0, r)

        def window(w, i, rows, keys, shared):
            data = (bias, q_ref, kc, vc) if shared else (None, q_ref, k_ref, v_ref)
            dq, dk, dv = window_back(w, rows, keys, *data, do_s[rows, lanes], lse_ref)
            buf_a[rows, lanes] = dq.astype(BF16)
            if shared:
                part = pl.ds(i * r, r)
                for n, v in enumerate((dk, dv)):
                    own[n, part, :] = v[:r, :]
                    hsend[n, part, :] = v[r:, :].astype(BF16)
            else:
                buf_b[rows, lanes] = dk.astype(BF16)
                buf_c[rows, lanes] = dv.astype(BF16)

        pairs = list(each_window(r, window))
        pairs[0]()
        swap(now).start()
        pairs[1]()
        pairs[2]()

    @pl.when(step >= plan.fin)
    def _():
        i = step - plan.fin
        pl.when(i == 0)(lambda: load(6).wait())
        part = pl.ds(pl.multiple_of(i * chunk, chunk), chunk)
        hh = dot(buf_a[part, :], w0[...], 1, 1) + dot(buf_b[part, :], wk_ref[...], 1, 1)
        for one in reds:
            one.tick(plan.fin + 2 * i + 1)
        hh = hh + dot(buf_c[part, :], wv_ref[...], 1, 1)
        n, rs = norm_stats(x_ref[...].astype(F32))
        add_sums(sums_a, i == 0, [col_sum(hh), col_sum(hh * n)])
        put_groups(h[part, :] + norm_back(hh, n, rs, mod_ref[1:2, :]), stage, gin_hbm, sem, i, 4)

    @pl.when(step == steps - 1)
    def _():
        rows = [sums_a[0:2, :], sums_m[0:4, :], jnp.zeros((2, d), F32)]
        sums_a[...] = jnp.concatenate(rows, axis=0)
        other = red.plain(sums_a, sums_got, hsem.at[3], hsem.at[4], 0)
        other.start()
        finish(reds, plan.end)
        other.wait()
        sums_ref[...] = sums_a[...] + sums_got[...]


def core(live, nm, gm, nmt, attt, ndt, w_up, w_down, wo, wq, wk, wv, middle, gw, ao, mod, q, k, v, lse, kh, vh, xw, like):
    t, d = nm.shape
    ff = w_up.shape[1]
    th = kh.shape[0]
    frames = like.shape[1]
    dp = lax.axis_size("dp")
    til = Tiling(ff, dp)
    n_ff, n_att = til.steps, d // 128
    plan = Plan(n_ff, n_att, til.early)
    rest = tuple(range(3, dp.bit_length() - 1))
    reds = [Reduce(dp, d, ((0, 1, 2, *rest), (1, 2, 0, *rest)), i == 0) for i in range(2)]
    red = reds[0]

    def block_at(first, count):
        return lambda i: (jnp.clip(i - first, 0, count - 1), 0)

    def lane_at(i):
        return 0, jnp.clip(i - plan.att, 0, n_att - 1)

    post = pl.BlockSpec((t // 4, d), block_at(plan.post, 4))
    last = pl.BlockSpec((t // 4, d), block_at(plan.fin, 4), pipeline_mode=pl.Buffered(1))
    big, small = pl.BlockSpec((t, 128), lane_at), pl.BlockSpec((th, 128), lane_at)
    lse_spec = pl.BlockSpec((None, 6, 8, lse_lanes(t)), lambda i: (lane_at(i)[1], 0, 0, 0))
    if til.early:
        half = n_ff // 2
        w_down = w_down.reshape(half, PIECES, 2, til.width, d)

        def down_at(i):
            i = jnp.minimum(i, n_ff - 1)
            return lax.rem(i, half), 0, i // half, 0, 0

        down = pl.BlockSpec((None, PIECES, None, til.width, d), down_at)
        cube, down_tile = cube_shape(red, ff, d), (PIECES, 2, red.r, d)
    else:
        down = pl.BlockSpec((LANES, d), block_at(0, n_ff))
        cube, down_tile = (ff, d), (PIECES, til.width, d)
    smem = pl.BlockSpec(memory_space=pltpu.SMEM)
    full = pl.BlockSpec((8, d), lambda i: (0, 0))
    image, sums = jax.ShapeDtypeStruct(like.shape, BF16), jax.ShapeDtypeStruct((8, d), F32)
    share = jax.ShapeDtypeStruct((red.r, d), F32)
    act, act32 = pltpu.VMEM((t, d), BF16), pltpu.VMEM((t, d), F32)
    return pl.pallas_call(
        functools.partial(core_kernel, til, plan, reds),
        grid=(plan.steps,),
        in_specs=[smem] + [ANY] * 8 + [down, post, post, post, whole((6, d)), whole((d, d)), whole((d, d))]
        + [big] * 3 + [lse_spec] + [small] * 2 + [last],
        out_specs=[ANY, ANY, full] + [ANY] * 7,
        out_shape=[image, image, sums, jax.ShapeDtypeStruct(cube, BF16), jax.ShapeDtypeStruct((red.r, ff), F32)]
        + [jax.ShapeDtypeStruct((ff // d, red.r, d), F32), share, share, share, share],
        scratch_shapes=[
            act,
            act,
            act,
            pltpu.VMEM((d, t), BF16),
            act32,
            act32,
            act,
            pltpu.VMEM((d, d), BF16),
            pltpu.VMEM((2, d, LANES), BF16),
            pltpu.VMEM(down_tile, BF16),
            tile_scratch(red),
            pltpu.VMEM((2 * th, 128), BF16),
            pltpu.VMEM((2 * th, 128), BF16),
            pltpu.VMEM((2, th, 128), F32),
            pltpu.VMEM((2, th, 128), BF16),
            pltpu.VMEM((2, 2, th, 128), BF16),
            pltpu.SemaphoreType.DMA((5,)),
            pltpu.SemaphoreType.DMA((3, PIECES)),
            pltpu.SemaphoreType.DMA((7,)),
            pltpu.VMEM((4, frames, 4, 8, d), BF16),
            pltpu.SemaphoreType.DMA((4,)),
        ]
        + [pltpu.VMEM((8, d), F32)] * 3
        + reds[0].scratch()
        + reds[1].scratch(),
        compiler_params=params(limit=63 * 1024 * 1024, collective_id=1, has_side_effects=True),
        name="core",
        cost_estimate=pl.CostEstimate(
            flops=12 * t * d * (ff + d) + 3 * t * t * d, bytes_accessed=8 * d * ff + 60 * t * d, transcendentals=t * (ff + 3 * t)
        ),
    )(live, nm, gm, nmt, attt, ndt, w_up, wo, wq, w_down, middle, gw, ao, mod, wk, wv, q, k, v, lse, kh, vh, xw)


def results_kernel(n_grad, a_hbm, b_hbm, mod_ref, *refs):
    grads, (a_out, b_out, mod_out), flats = refs[:n_grad], refs[n_grad : n_grad + 3], refs[n_grad + 3 : 2 * n_grad + 3]
    held, sem = refs[-2:]
    loads, stores = [], []
    for n, (src, dst) in enumerate(((a_hbm, a_out), (b_hbm, b_out))):
        for f in range(src.shape[1]):
            loads.append(pltpu.make_async_copy(src.at[0, f], held.at[n, f], sem.at[0, n, f]))
            stores.append(pltpu.make_async_copy(held.at[n, f], dst.at[0, f], sem.at[1, n, f]))
    for c in loads:
        c.start()
    mod_out[0] = mod_ref[0:6, :]
    for src, dst in zip(grads, flats):
        rows, cols = src.shape
        wide = cols // 128
        for g in range(wide):
            dst[pl.ds(g, rows, stride=wide), :] = src[:, lanes_at(g, 128)]
    for load, store in zip(loads, stores):
        load.wait()
        store.start()
    for c in stores:
        c.wait()


def results(image_a, image_b, mod_sums, grads):
    grads = [g.reshape(-1, g.shape[-1]) for g in grads]
    vmem = pl.BlockSpec(memory_space=pltpu.VMEM)
    n = len(grads)
    out = pl.pallas_call(
        functools.partial(results_kernel, n),
        in_specs=[ANY, ANY] + [vmem] * (n + 1),
        out_specs=[ANY, ANY] + [vmem] * (n + 1),
        out_shape=[jax.ShapeDtypeStruct(image_a.shape, BF16)] * 2
        + [jax.ShapeDtypeStruct((1, 6, mod_sums.shape[1]), F32)]
        + [jax.ShapeDtypeStruct((g.size // 128, 128), F32) for g in grads],
        scratch_shapes=[
            pltpu.VMEM((2,) + image_a.shape[1:], BF16),
            pltpu.SemaphoreType.DMA((2, 2, image_a.shape[1])),
        ],
        compiler_params=params(),
        name="results",
        cost_estimate=pl.CostEstimate(flops=0, bytes_accessed=8 * image_a.size, transcendentals=0),
    )(image_a, image_b, mod_sums, *grads)
    return out[0], out[1], out[2], *(g.reshape(-1) for g in out[3:])


def on_device(
    block_input, modulation, band_live, w_query, w_key, w_value, w_out, w_up, w_down, cotangent
):
    assert lax.axis_size("band") == 2 and block_input.shape[2:4] == (16, 16)
    mod = modulation[0]
    xw, ndt, gw, gm, q, k, v, kh, vh = pre(block_input, cotangent, band_live, mod, w_query, w_key, w_value)
    attended, lse = attn_fwd(band_live, q, k, v, kh, vh)
    ao, middle, nm, nmt, attt = mid(band_live, attended, w_out, xw, mod)
    block_output, grad_input, mod_sums, _, g_up, g_down, g_out, g_query, g_key, g_value = core(
        band_live, nm, gm, nmt, attt, ndt, w_up, w_down, w_out, w_query, w_key, w_value,
        middle, gw, ao, mod, q, k, v, lse, kh, vh, xw, block_input,
    )
    return results(block_output, grad_input, mod_sums, (g_query, g_key, g_value, g_out, g_up, g_down))


def solution(mesh):
    return jax.shard_map(
        on_device,
        mesh=mesh,
        in_specs=(
            P("dp", None, "band", None, None),
            P("dp", None, None),
            P("dp", None),
            P(),
            P(),
            P(),
            P(),
            P(),
            P(),
            P("dp", None, "band", None, None),
        ),
        out_specs=(
            P("dp", None, "band", None, None),
            P("dp", None, "band", None, None),
            P("dp", None, None),
            P("dp"),
            P("dp"),
            P("dp"),
            P("dp"),
            P("dp"),
            P("dp"),
        ),
        check_vma=False,
    )
```

```python
import functools

import jax
import jax.numpy as jnp
from jax import lax
from jax.experimental import pallas as pl
from jax.experimental.pallas import tpu as pltpu
from jax.sharding import PartitionSpec as P

HEADS = 16
HEAD_DIM = 64
EPS = 1e-06
MASKED = -1e30
LOG2E = 1.4426950408889634
F32 = jnp.float32
BF16 = jnp.bfloat16
ANY = pl.BlockSpec(memory_space=pl.ANY)
VMEM_LIMIT = 60 * 1024 * 1024

MID_SPOTS = ((1, 0), (2, 0), (1, 1), (2, 1))


def group_spot(band, s):
    lone = 3 * band
    paired = 3 - 3 * band
    if s < 2:
        return lone, s
    if s < 6:
        return MID_SPOTS[s - 2]
    return paired, s - 6


def params(limit=VMEM_LIMIT, **kw):
    return pltpu.CompilerParams(vmem_limit_bytes=limit, **kw)


def dot(a, b, ca=1, cb=0):
    return lax.dot_general(a, b, (((ca,), (cb,)), ((), ())), preferred_element_type=F32)


def whole(shape):
    return pl.BlockSpec(shape, lambda *_: (0,) * len(shape), pipeline_mode=pl.Buffered(1))


def own_live(flags):
    return jnp.where(flags[0, lax.axis_index("band")] == 1, 1.0, 0.0)


def halo_bias(flags, shape, dim, r):
    band = lax.axis_index("band")
    other = jnp.where(flags[0, 1 - band] == 1, 0.0, MASKED)
    off = jnp.where(flags[0, band] == 1, other, 0.0)
    return jnp.where(lax.broadcasted_iota(jnp.int32, shape, dim) >= r, off, 0.0)


def norm_stats(v):
    c = v - jnp.mean(v, axis=-1, keepdims=True)
    r = lax.rsqrt(jnp.mean(c * c, axis=-1, keepdims=True) + EPS)
    return c * r, r


def spot_copy(hbm, vmem, band, s, sem, out=False):
    g, j = group_spot(band, s)
    there = hbm.at[0, :, pl.ds(g * 4, 4), pl.ds(j * 8, 8), :]
    if out:
        slot = s % vmem.shape[0]
        return pltpu.make_async_copy(vmem.at[slot], there, sem.at[slot])
    return pltpu.make_async_copy(there, vmem.at[s], sem.at[s])


def pre_kernel(
    x_hbm, g_hbm, live_ref, mod_ref, wq_ref, wk_ref, wv_ref,
    xw_ref, ndt_ref, gw_ref, gm_ref, q_ref, k_ref, v_ref, kh_ref, vh_ref,
    stage, halo, sem, swap_sem, nsc, nhalo,
):
    step, n_tile = pl.program_id(0), pl.num_programs(0) // 2
    band = lax.axis_index("band")
    n_group = stage.shape[0]
    rows = nsc.shape[0] // n_group
    there = (lax.axis_index("dp"), 1 - band)

    def normed(x):
        n, _ = norm_stats(x)
        return (n * (1.0 + mod_ref[1:2, :]) + mod_ref[0:1, :]).astype(BF16)

    swap = pltpu.make_async_remote_copy(
        src_ref=x_hbm.at[0, :, pl.ds(12 - 12 * band, 4)],
        dst_ref=halo,
        send_sem=swap_sem.at[0],
        recv_sem=swap_sem.at[1],
        device_id=there,
        device_id_type=pl.DeviceIdType.MESH,
    )

    @pl.when(step == 0)
    def _():
        for s in range(n_group):
            spot_copy(x_hbm, stage, band, s, sem).start()
        entered = pltpu.get_barrier_semaphore()
        pl.semaphore_signal(entered, inc=1, device_id=there, device_id_type=pl.DeviceIdType.MESH)
        pl.semaphore_wait(entered, 1)
        swap.start()
        for s in range(n_group):
            spot_copy(x_hbm, stage, band, s, sem).wait()
            x = stage[s].astype(F32).reshape(rows, stage.shape[-1])
            part = slice(s * rows, (s + 1) * rows)
            nsc[part, :] = normed(x)
            xw_ref[part, :] = x.astype(BF16)
        for s in range(n_group):
            spot_copy(g_hbm, stage, band, s, sem).start()

    @pl.when(step < n_tile)
    def _():
        for w_ref, o_ref in ((wq_ref, q_ref), (wk_ref, k_ref), (wv_ref, v_ref)):
            o_ref[...] = dot(nsc[...], w_ref[...]).astype(BF16)

    @pl.when(step == n_tile)
    def _():
        ndt_ref[...] = jnp.transpose(nsc[...])
        gate = own_live(live_ref) * mod_ref[5:6, :]
        for s in range(n_group):
            spot_copy(g_hbm, stage, band, s, sem).wait()
            g = stage[s].astype(F32).reshape(rows, stage.shape[-1])
            part = slice(s * rows, (s + 1) * rows)
            gw_ref[part, :] = g.astype(BF16)
            gm_ref[part, :] = (gate * g).astype(BF16)
        swap.wait()
        for j in range(2):
            x = halo[:, :, 8 * j : 8 * j + 8, :].astype(F32).reshape(rows, halo.shape[-1])
            nhalo[j * rows : (j + 1) * rows, :] = normed(x)

    @pl.when(step >= n_tile)
    def _():
        for w_ref, o_ref in ((wk_ref, kh_ref), (wv_ref, vh_ref)):
            o_ref[...] = dot(nhalo[...], w_ref[...]).astype(BF16)


def pre(x, cot, live, mod, wq, wk, wv):
    d, frames = x.shape[-1], x.shape[1]
    t = 8 * frames * 32
    th = t // 4
    tile = 256
    n_tile = d // tile
    own = pl.BlockSpec((t, tile), lambda n: (0, jnp.minimum(n, n_tile - 1)))
    other = pl.BlockSpec((th, tile), lambda n: (0, jnp.maximum(n - n_tile, 0)))
    once = pl.BlockSpec((d, tile), lambda n: (0, jnp.minimum(n, n_tile - 1)))
    twice = pl.BlockSpec((d, tile), lambda n: (0, lax.rem(n, n_tile)))
    act, act_h = jax.ShapeDtypeStruct((t, d), BF16), jax.ShapeDtypeStruct((th, d), BF16)
    return pl.pallas_call(
        pre_kernel,
        grid=(2 * n_tile,),
        in_specs=[ANY, ANY, pl.BlockSpec(memory_space=pltpu.SMEM), whole((6, d)), once, twice, twice],
        out_specs=[whole((t, d)), whole((d, t)), whole((t, d)), whole((t, d)), own, own, own, other, other],
        out_shape=[act, jax.ShapeDtypeStruct((d, t), BF16), act, act, act, act, act, act_h, act_h],
        scratch_shapes=[
            pltpu.VMEM((8, frames, 4, 8, d), BF16),
            pltpu.VMEM((frames, 4, 16, d), BF16),
            pltpu.SemaphoreType.DMA((8,)),
            pltpu.SemaphoreType.DMA((2,)),
            pltpu.VMEM((t, d), BF16),
            pltpu.VMEM((th, d), BF16),
        ],
        compiler_params=params(collective_id=2, has_side_effects=True),
        name="pre",
        cost_estimate=pl.CostEstimate(flops=7 * t * d * d, bytes_accessed=10 * d * d + 12 * t * d, transcendentals=0),
    )(x, cot, live, mod, wq, wk, wv)


LANES = 512


class Reduce:
    def __init__(self, dp, total_rows, orders, tiles_only):
        self.bits = list(range(dp.bit_length() - 2, 0, -1))
        self.nz = len(self.bits)
        self.stages = self.nz + 1
        self.depth = self.stages + 4
        self.r = total_rows // dp
        self.orders = orders
        self.tiles_only = tiles_only
        self.dp = dp

    def scratch(self):
        r, nz, k = self.r, self.nz, self.stages
        out = [] if self.tiles_only else [pltpu.VMEM((1 << nz, r, LANES), BF16)]
        out += [pltpu.VMEM((2, 1 << nz, r, LANES), BF16)]
        for _ in range(2):
            for i in range(k):
                block = (2,) * (k - 1 - i) + (r, 128)
                out += [pltpu.VMEM(block, BF16), pltpu.VMEM(block, BF16), pltpu.VMEM((2,) + block, BF16)]
        out += [pltpu.VMEM((2, r, 128), BF16), pltpu.VMEM((2, 2, r, 128), BF16), pltpu.VMEM((r, LANES), F32)]
        out += [pltpu.SemaphoreType.DMA((2 * k + 4,)), pltpu.SemaphoreType.DMA((2 * k + 2, 2))]
        return out

    def bind(self, refs, jobs, tiles):
        refs = list(refs)
        cube = (2,) * self.nz
        self.own = tiles.at[0, :, 0] if self.tiles_only else refs.pop(0)
        self.got_core = refs.pop(0)
        self.got_cube = self.got_core.reshape((2,) + cube + (self.r, LANES))
        if self.tiles_only:
            self.tile_cube = tiles.reshape((2,) + cube + (2, self.r, LANES))
        else:
            self.own_cube = self.own.reshape(cube + (self.r, LANES))
        self.send, self.keep, self.got = {}, {}, {}
        for p in range(2):
            for i in range(self.stages):
                self.send[p, i], self.keep[p, i], self.got[p, i] = refs.pop(0), refs.pop(0), refs.pop(0)
        self.fin, self.got_fin, self.ostage, self.ssem, self.rsem = refs
        self.jobs = jobs
        self.starts = [job[0] for job in jobs]
        self.me, self.band = lax.axis_index("dp"), lax.axis_index("band")

    def place(self, axis):
        return self.band if axis == 0 else lax.rem(self.me // (1 << axis), 2)

    def partner(self, axis):
        if axis == 0:
            return (self.me, 1 - self.band)
        bit = 1 if axis == -1 else 1 << axis
        here = lax.rem(self.me // bit, 2)
        return (self.me + bit - 2 * bit * here, self.band)

    def barrier(self):
        sem = pltpu.get_barrier_semaphore()
        everyone = [-1, 0] + self.bits
        for axis in everyone:
            pl.semaphore_signal(sem, inc=1, device_id=self.partner(axis), device_id_type=pl.DeviceIdType.MESH)
        pl.semaphore_wait(sem, len(everyone))

    def remote(self, src, dst, s, slot, axis):
        return pltpu.make_async_remote_copy(
            src_ref=src,
            dst_ref=dst,
            send_sem=self.ssem.at[s],
            recv_sem=self.rsem.at[s, slot],
            device_id=self.partner(axis),
            device_id_type=pl.DeviceIdType.MESH,
        )

    def core_copy(self, slot, src):
        return self.remote(src, self.got_core.at[slot], 2 * self.stages, slot, -1)

    def part_copy(self, p, i, slot):
        return self.remote(self.send[p, i], self.got[p, i].at[slot], 2 * i + p, slot, self.orders[p][i])

    def fin_copy(self, slot):
        return self.remote(self.fin, self.got_fin.at[slot], 2 * self.stages + 1, slot, 0)

    def pick(self, axes, axis, at):
        return tuple(at if a == axis else slice(None) for a in axes)

    def split_core(self, j, p):
        slot = lax.rem(j, 2)
        first = self.orders[p][0]
        mine = self.place(first)
        for dst, at in ((self.send[p, 0], 1 - mine), (self.keep[p, 0], mine)):
            if first == 0:
                lanes = pl.ds(pl.multiple_of((2 * p + at) * 128, 128), 128)
                idx = (slice(None),) * (self.nz + 1) + (lanes,)
                dst[...] = self.mine(slot, idx) + self.got_cube[(slot,) + idx]
            else:
                for b in range(2):
                    lanes = slice((2 * p + b) * 128, (2 * p + b + 1) * 128)
                    idx = self.pick(self.bits, first, at) + (slice(None), lanes)
                    dst[(slice(None),) * (self.nz - 1) + (b,)] = self.mine(slot, idx) + self.got_cube[(slot,) + idx]

    def split(self, j, p, i):
        slot = lax.rem(j, 2)
        axes = [a for a in self.bits + [0] if a not in self.orders[p][:i]]
        axis = self.orders[p][i]
        mine = self.place(axis)
        for dst, at in ((self.send[p, i], 1 - mine), (self.keep[p, i], mine)):
            idx = self.pick(axes, axis, at)
            dst[...] = self.keep[p, i - 1][idx] + self.got[p, i - 1][(slot,) + idx]

    def stage(self, s, j):
        k = self.stages
        slot = lax.rem(j, 2)
        if s == 0:
            self.each(j, 1)
        elif s == 1:
            self.core_copy(slot, self.own).wait()
            if not self.tiles_only:
                self.own_copy(self.own).wait()
            for p in range(2):
                self.split_core(j, p)
                self.part_copy(p, 0, slot).start()
        elif s <= k:
            for p in range(2):
                self.part_copy(p, s - 2, slot).wait()
                self.split(j, p, s - 1)
                self.part_copy(p, s - 1, slot).start()
        elif s == k + 1:
            for p in range(2):
                self.part_copy(p, k - 1, slot).wait()
                self.fin[p] = self.keep[p, k - 1][...] + self.got[p, k - 1][slot]
            self.fin_copy(slot).start()
        elif s == k + 2:
            self.fin_copy(slot).wait()
            for p in range(2):
                mine = pl.ds(pl.multiple_of((2 * p + self.band) * 128, 128), 128)
                other = pl.ds(pl.multiple_of((2 * p + 1 - self.band) * 128, 128), 128)
                self.ostage[:, mine] = self.fin[p].astype(F32)
                self.ostage[:, other] = self.got_fin[slot, p].astype(F32)
            self.each(j, 2)
        else:
            self.out_copy(self.ostage).wait()

    def each(self, j, part):
        for i, job in enumerate(self.jobs):
            pl.when(j == i)(functools.partial(job[part], self, i % 2))

    def own_copy(self, src):
        return pltpu.make_async_copy(src, self.own, self.ssem.at[2 * self.stages + 2])

    def out_copy(self, dst, src=None):
        return pltpu.make_async_copy(self.ostage if src is None else src, dst, self.ssem.at[2 * self.stages + 3])

    def mine(self, slot, idx):
        if self.tiles_only:
            return self.tile_cube[(slot,) + idx[: self.nz] + (lax.rem(self.me, 2),) + idx[self.nz :]]
        return self.own_cube[idx]

    def start_pair(self, slot, ref, at):
        core = lax.rem(self.me, 2)
        if not self.tiles_only:
            self.own_copy(ref.at[(slice(None), core) + at]).start()
        self.core_copy(slot, ref.at[(slice(None), 1 - core) + at]).start()

    def tick(self, t):
        for s in reversed(range(self.depth)):
            u = t - s
            before = sum(jnp.where(u > at, 1, 0) for at in self.starts)
            upto = sum(jnp.where(u >= at, 1, 0) for at in self.starts)

            @pl.when(upto > before)
            def _():
                self.stage(s, before)

    def plain(self, src, dst, send_sem, recv_sem, axis):
        return pltpu.make_async_remote_copy(
            src_ref=src,
            dst_ref=dst,
            send_sem=send_sem,
            recv_sem=recv_sem,
            device_id=self.partner(axis),
            device_id_type=pl.DeviceIdType.MESH,
        )


def cube_shape(red, rows, cols):
    return (red.dp // 2, 2, rows // (red.r * red.dp), red.r, cols)


def lanes_at(i, width=LANES):
    return slice(i * width, (i + 1) * width)


def array_job(start, src, dst, q, i, q_out=None):
    def begin(red, slot):
        red.start_pair(slot, src, (q, slice(None), lanes_at(i)))

    def end(red, slot):
        red.out_copy(dst.at[q if q_out is None else q_out, :, lanes_at(i)]).start()

    return start, begin, end


def tile_job(start, tiles, at, parts):
    width = LANES // len(parts)

    def begin(red, slot):
        red.start_pair(slot, tiles.at[at], ())

    def end(red, slot):
        for n, dst in enumerate(parts):
            red.out_copy(dst, red.ostage.at[:, lanes_at(n, width)]).start()

    return start, begin, end


def tile_scratch(red):
    return pltpu.VMEM((2, red.dp // 2, 2, red.r, LANES), BF16)


def put_tile(red, tiles, slot, v):
    tiles[slot] = v.reshape(tiles.shape[1:]).astype(BF16)


SCALE = HEAD_DIM**-0.5
SCALE2 = SCALE * LOG2E


def head_masks(rows):
    left = lax.broadcasted_iota(jnp.int32, (rows, 128), 1) < 64
    return left, jnp.logical_not(left)


def only(mask, v):
    return jnp.where(mask, v, jnp.zeros_like(v))


def each_window(r, body):
    for first, rows, at, shared in ((4, r, 6 * r, True), (0, r, 0, False), (2, 2 * r, 2 * r, False)):
        yield functools.partial(window_pair, r, first, rows, at, shared, body)


def window_pair(r, first, rows, at, shared, body):
    def one(i, _):
        q0 = at + i * rows
        k0 = 2 * r * i if shared else q0
        body(first + i, i, pl.ds(q0, rows), pl.ds(k0, 2 * r if shared else rows), shared)
        return 0

    for i in range(2):
        one(i, 0)


def fill_shared(scratch, own_ref, halo_ref, r):
    for w in range(2):
        scratch[2 * r * w : 2 * r * w + r, :] = own_ref[(6 + w) * r : (7 + w) * r, :]
        scratch[2 * r * w + r : 2 * r * (w + 1), :] = halo_ref[r * w : r * (w + 1), :]


def attn_fwd_kernel(live_ref, q_ref, k_ref, v_ref, kh_ref, vh_ref, o_ref, lse_ref, kc, vc):
    r = q_ref.shape[0] // 8
    fill_shared(kc, k_ref, kh_ref, r)
    fill_shared(vc, v_ref, vh_ref, r)
    bias = halo_bias(live_ref, (1, 2 * r), 1, r)
    for w, (q0, qn) in enumerate(((0, r), (r, r), (2 * r, 2 * r), (4 * r, 2 * r), (6 * r, r), (7 * r, r))):
        rows = slice(q0, q0 + qn)
        q = q_ref[rows, :]
        if w < 4:
            k, v = k_ref[rows, :], v_ref[rows, :]
        else:
            keys = slice(2 * r * (w - 4), 2 * r * (w - 3))
            k, v = kc[keys, :], vc[keys, :]
        masks = head_masks(qn)
        o, lse = [], []
        for mask in masks:
            s = dot(only(mask, q), k, 1, 1) * SCALE2
            if w >= 4:
                s = s + bias
            top = jnp.max(s, axis=-1, keepdims=True)
            e = jnp.exp2(s - top)
            total = jnp.sum(e, axis=-1, keepdims=True)
            o.append(dot(e.astype(BF16), v) * (1.0 / total))
            lse.append(top + jnp.log2(total))
        o_ref[rows, :] = jnp.where(masks[0], o[0], o[1]).astype(BF16)
        turned = jnp.transpose(jnp.where(masks[0], lse[0], lse[1]))
        for h in range(2):
            lse_ref[w, h : h + 1, :qn] = turned[64 * h : 64 * h + 1, :]


def lse_lanes(t):
    return pl.cdiv(t // 4, 128) * 128


def attn_fwd(live, q, k, v, kh, vh):
    t, d = q.shape
    th = kh.shape[0]
    big = pl.BlockSpec((t, 128), lambda n: (0, n))
    small = pl.BlockSpec((th, 128), lambda n: (0, n))
    return pl.pallas_call(
        attn_fwd_kernel,
        grid=(d // 128,),
        in_specs=[pl.BlockSpec(memory_space=pltpu.SMEM), big, big, big, small, small],
        out_specs=[big, pl.BlockSpec((None, 6, 8, lse_lanes(t)), lambda n: (n, 0, 0, 0))],
        out_shape=[jax.ShapeDtypeStruct((t, d), BF16), jax.ShapeDtypeStruct((d // 128, 6, 8, lse_lanes(t)), F32)],
        scratch_shapes=[pltpu.VMEM((2 * th, 128), BF16)] * 2,
        compiler_params=params(),
        name="attn_fwd",
        cost_estimate=pl.CostEstimate(flops=t * t * d, bytes_accessed=12 * t * d, transcendentals=t * t * 3),
    )(live, q, k, v, kh, vh)


def mid_kernel(live_ref, att_ref, w_ref, x_ref, mod_ref, ao_ref, mid_ref, nm_ref, nmt_ref, attt_ref):
    live = own_live(live_ref)
    attn_out = dot(att_ref[...], w_ref[...])
    middle = x_ref[...].astype(F32) + (live * mod_ref[2:3, :]) * attn_out
    ao_ref[...] = attn_out.astype(BF16)
    mid_ref[...] = middle
    n, _ = norm_stats(middle)
    nm = (n * (1.0 + mod_ref[4:5, :]) + mod_ref[3:4, :]).astype(BF16)
    nm_ref[...] = nm
    nmt_ref[...] = jnp.transpose(nm)
    attt_ref[...] = jnp.transpose(att_ref[...])


def mid(live, attended, w_out, xw, mod):
    t, d = xw.shape
    blk = pl.BlockSpec((t // 5, d), lambda m: (m, 0))
    blk_t = pl.BlockSpec((d, t // 5), lambda m: (0, m))
    bf, f32 = jax.ShapeDtypeStruct((t, d), BF16), jax.ShapeDtypeStruct((t, d), F32)
    bf_t = jax.ShapeDtypeStruct((d, t), BF16)
    return pl.pallas_call(
        mid_kernel,
        grid=(5,),
        in_specs=[pl.BlockSpec(memory_space=pltpu.SMEM), blk, whole((d, d)), blk, whole((6, d))],
        out_specs=[blk, blk, blk, blk_t, blk_t],
        out_shape=[bf, f32, bf, bf_t, bf_t],
        compiler_params=params(),
        name="mid",
        cost_estimate=pl.CostEstimate(flops=2 * t * d * d, bytes_accessed=16 * t * d, transcendentals=0),
    )(live, attended, w_out, xw, mod)


GELU_C = 0.7978845608
GELU_A = 0.044715


def col_sum(v):
    return jnp.sum(v, axis=0, keepdims=True)


def norm_back(h, n, r, gain):
    e = h * (1.0 + gain)
    return r * (e - jnp.mean(e, axis=-1, keepdims=True) - n * jnp.mean(e * n, axis=-1, keepdims=True))


def add_sums(ref, first, rows):
    sums = jnp.concatenate(rows + [jnp.zeros((ref.shape[0] - len(rows), ref.shape[1]), F32)], axis=0)

    @pl.when(first)
    def _():
        ref[...] = sums

    @pl.when(jnp.logical_not(first))
    def _():
        ref[...] += sums


def put_groups(out, stage, out_hbm, sem, block, blocks):
    band = lax.axis_index("band")
    slots = stage.shape[0]
    n_group = 8
    per = n_group // blocks
    rows = out.shape[0] // per
    for k in range(blocks):

        @pl.when(block == k)
        def _():
            for i in range(per):
                s = k * per + i
                if s >= slots:
                    spot_copy(out_hbm, stage, band, s - slots, sem, out=True).wait()
                stage[s % slots] = out[i * rows : (i + 1) * rows, :].reshape(stage.shape[1:]).astype(BF16)
                spot_copy(out_hbm, stage, band, s, sem, out=True).start()

    @pl.when(block == blocks - 1)
    def _():
        for s in range(n_group - slots, n_group):
            spot_copy(out_hbm, stage, band, s, sem, out=True).wait()


PIECES = 4


class Tiling:
    def __init__(self, ff, dp):
        self.steps = ff // LANES
        self.width = LANES // PIECES
        self.early = ff // dp == 2 * self.width

    def piece(self, i, k):
        if not self.early:
            return PIECES * i + k
        half = self.steps // 2
        return (i % half * PIECES + k) * 2 + i // half


def window_back(w, rows, keys, bias, q_ref, k_ref, v_ref, do, lse_ref):
    q, k, v = q_ref[rows, :], k_ref[keys, :], v_ref[keys, :]
    kt = jnp.transpose(k)
    dq, dk, dv = [], [], []
    for h, mask in enumerate(head_masks(rows.size)):
        s = dot(k, only(mask, q), 1, 1) * SCALE2
        if bias is not None:
            s = s + bias
        p = jnp.exp2(s - lse_ref[w, h : h + 1, : rows.size])
        dp = dot(v, only(mask, do), 1, 1)
        total = jnp.sum(p * dp, axis=0, keepdims=True)
        ds = (p * (dp - total)).astype(BF16)
        dv.append(dot(p.astype(BF16), do))
        dk.append(dot(ds, q))
        dq.append(dot(kt[64 * h : 64 * h + 64, :], ds))
    left = head_masks(keys.size)[0]
    dq = jnp.transpose(jnp.concatenate(dq, axis=0)) * SCALE
    return dq, jnp.where(left, dk[0], dk[1]) * SCALE, jnp.where(left, dv[0], dv[1])


TILES = ((("q", 0), ("k", 0)), (("v", 0), ("v", 1)), (("q", 1), ("k", 1)), (("q", 2), ("k", 2)), (("v", 2), ("v", 3)), (("q", 3), ("k", 3)))
TILE_SLOTS = (0, 0, 1, 0, 1, 0)
MADE = {2: (0,), 4: (1, 2), 6: (3,), 8: (4, 5)}


class Plan:
    def __init__(self, n_ff, n_att, early):
        self.n_ff, self.n_att = n_ff, n_att
        self.post = n_ff
        self.out = n_ff + 4
        self.att = self.out + 1
        self.fin = self.att + n_att
        self.steps = self.fin + 4
        self.end = self.fin + 8
        a = self.att
        self.up = [(0, i + 1) for i in range(n_ff)]
        self.o_proj = [(0, a), (1, a)]
        self.tiles = [(1, a + 3), (1, a + 5), (0, a + 5), (1, a + 7), (1, self.fin + 1), (0, self.fin + 1)]
        late = [(1, n_ff + 1 + i) for i in range(4)]
        self.down = [(1, n_ff // 2 + 1 + i) for i in range(4)] + late if early else late + [(1, a + i) for i in (1, 2, 4, 6)]


def finish(reds, first):
    def body(u, _):
        for red in reds:
            red.tick(u)
        return 0

    lax.fori_loop(first, max(red.starts[-1] + red.depth for red in reds), body, 0)


def core_kernel(
    til, plan, reds, live_ref, nm_hbm, gm_hbm, nmt_hbm, attt_hbm, ndt_hbm, wu_hbm, wo_hbm, wq_hbm,
    wd_ref, mid_ref, g_ref, ao_ref, mod_ref, wk_ref, wv_ref, q_ref, k_ref, v_ref, lse_ref, kh_ref, vh_ref, x_ref,
    out_hbm, gin_hbm, sums_ref, dwd_hbm, gup_hbm, gdown_hbm, gout_hbm, gq_hbm, gk_hbm, gv_hbm,
    buf_a, buf_b, buf_c, buf_t, mo, h, do_s, w0, wu, dwd, tiles, kc, vc, own, hsend, hrecv,
    hsem, wsem, lsem, stage, sem, sums_m, sums_a, sums_got, *scratch,
):
    step, steps = pl.program_id(0), pl.num_programs(0)
    n_ff, n_att, width = plan.n_ff, plan.n_att, til.width
    t, d = mo.shape
    chunk = t // 4
    r = t // 8
    red = reds[0]

    def up_at(i, k):
        return pl.ds(pl.multiple_of(til.piece(i, k) * width, width), width)

    def load_up(i, k):
        slot = lax.rem(i, 2)
        return pltpu.make_async_copy(wu_hbm.at[:, up_at(i, k)], wu.at[slot, :, lanes_at(k, width)], wsem.at[slot, k])

    def store_down(i, k):
        if til.early:
            d_at = til.piece(i, k) // 2
            dst = dwd_hbm.at[d_at // 2, lax.rem(d_at, 2), pl.ds(2 * lax.rem(til.piece(i, k), 2), 2)]
        else:
            dst = dwd_hbm.at[pl.ds(til.piece(i, k) * width, width), :]
        return pltpu.make_async_copy(dwd.at[k], dst, wsem.at[2, k])

    def load(n):
        pairs = ((nm_hbm, buf_b), (gm_hbm, buf_c), (nmt_hbm, buf_t), (wo_hbm, w0), (attt_hbm, buf_t), (ndt_hbm, buf_t), (wq_hbm, w0))
        return pltpu.make_async_copy(*pairs[n], lsem.at[n])

    grad_of = {"q": (buf_a, gq_hbm), "k": (buf_b, gk_hbm), "v": (buf_c, gv_hbm)}
    cube = dwd_hbm if til.early else dwd_hbm.reshape(cube_shape(red, dwd_hbm.shape[0], d))
    wide = d // LANES
    jobs = ([], [])
    for i, (at, start) in enumerate(plan.up):
        jobs[at].append(tile_job(start, tiles, i % 2, [gup_hbm.at[:, lanes_at(til.piece(i, k), width)] for k in range(PIECES)]))
    for n, (at, start) in enumerate(plan.down):
        jobs[at].append(array_job(start, cube, gdown_hbm, n // wide, n % wide))
    for n, (at, start) in enumerate(plan.o_proj):
        jobs[at].append(tile_job(start, tiles, n, [gout_hbm.at[:, lanes_at(n)]]))
    for m, (at, start) in enumerate(plan.tiles):
        jobs[at].append(tile_job(start, tiles, TILE_SLOTS[m], [grad_of[n][1].at[:, lanes_at(i, 256)] for n, i in TILES[m]]))
    size = len(scratch) // 2
    for i in range(2):
        reds[i].bind(scratch[i * size : (i + 1) * size + i], sorted(jobs[i], key=lambda job: job[0]), tiles)

    def swap(i):
        slot = lax.rem(i, 2)
        return red.plain(hsend, hrecv.at[slot], hsem.at[0], hsem.at[1 + slot], 0)

    @pl.when(step == 0)
    def _():
        for k in range(PIECES):
            load_up(0, k).start()
        for n in range(4):
            load(n).start()
        mo[...] = jnp.zeros_like(mo)
        h[...] = jnp.zeros_like(h)
        red.barrier()
        load(0).wait()
        load(1).wait()

    for one in reds:
        one.tick(step + jnp.maximum(step - plan.fin, 0))

    @pl.when(step < n_ff)
    def _():
        slot = lax.rem(step, 2)
        for k in range(PIECES):
            load_up(step, k).wait()

        @pl.when(step + 1 < n_ff)
        def _():
            for k in range(PIECES):
                load_up(step + 1, k).start()

        wd = wd_ref[...].reshape(LANES, d)
        up = wu.at[slot]

        def rows(i, _):
            part = pl.ds(pl.multiple_of(i * (2 * chunk), 2 * chunk), 2 * chunk)
            v = dot(buf_b[part, :], up[...])
            gh = dot(buf_c[part, :], wd, 1, 1)
            v2 = v * v
            th = jnp.tanh(v * (GELU_C + (GELU_C * GELU_A) * v2))
            half = 0.5 * th + 0.5
            hidden = (v * half).astype(BF16)
            slope = half + (0.5 * v) * (1.0 - th * th) * (GELU_C + (3.0 * GELU_C * GELU_A) * v2)
            gpre = (gh * slope).astype(BF16)
            buf_a[part, :LANES] = hidden
            buf_a[part, LANES : 2 * LANES] = gpre
            mo[part, :] += dot(hidden, wd)
            h[part, :] += dot(gpre, up[...], 1, 1)
            return 0

        lax.fori_loop(0, 2, rows, 0)

        @pl.when(step > 0)
        def _():
            for k in range(PIECES):
                store_down(step - 1, k).wait()

        pl.when(step == 0)(lambda: load(2).wait())
        put_tile(red, tiles, slot, dot(buf_t[...], buf_a[:, LANES : 2 * LANES]))
        dwd[...] = dot(buf_a[:, :LANES], buf_c[...], 0, 0).reshape(dwd.shape).astype(BF16)
        for k in range(PIECES):
            store_down(step, k).start()

    @pl.when((step >= plan.post) & (step < plan.out))
    def _():
        block = step - plan.post

        @pl.when(block == 0)
        def _():
            load(4).start()
            load(3).wait()
            for k in range(PIECES):
                store_down(step - 1, k).wait()

        part = pl.ds(pl.multiple_of(block * chunk, chunk), chunk)
        live = own_live(live_ref)
        middle, g = mid_ref[...], g_ref[...].astype(F32)
        mlp_out, hh = mo[part, :], h[part, :]
        n, rs = norm_stats(middle)
        gmid = g + norm_back(hh, n, rs, mod_ref[4:5, :])
        h[part, :] = gmid
        ga = ((live * mod_ref[2:3, :]) * gmid).astype(BF16)
        buf_b[part, :] = ga
        do_s[part, :] = dot(ga, w0[...], 1, 1).astype(BF16)
        sums = [col_sum(live * ao_ref[...].astype(F32) * gmid), col_sum(hh), col_sum(hh * n), col_sum(live * mlp_out * g)]
        add_sums(sums_m, block == 0, sums)
        put_groups(middle + (live * mod_ref[5:6, :]) * mlp_out, stage, out_hbm, sem, block, 4)

    @pl.when(step == plan.out)
    def _():
        load(6).start()
        load(4).wait()
        for n in range(wide):
            put_tile(red, tiles, n, dot(buf_t[...], buf_b[:, lanes_at(n)]))
        load(5).start()

    now = step - plan.att

    @pl.when((now > 0) & (now <= n_att))
    def _():
        swap(now - 1).wait()
        slot = lax.rem(now - 1, 2)
        lanes = pl.ds(pl.multiple_of((now - 1) * 128, 128), 128)
        for i, ref in enumerate((buf_b, buf_c)):
            ref[6 * r :, lanes] = (own[i] + hrecv[slot, i].astype(F32)).astype(BF16)

    for at, made in MADE.items():

        @pl.when(now == at)
        def _():
            if at == min(MADE):
                load(5).wait()
            for m in made:
                cols = [grad_of[n][0][:, lanes_at(i, 256)] for n, i in TILES[m]]
                put_tile(red, tiles, TILE_SLOTS[m], dot(buf_t[...], jnp.concatenate(cols, axis=1)))

    @pl.when((now >= 0) & (now < n_att))
    def _():
        slot = lax.rem(now, 2)
        lanes = pl.ds(pl.multiple_of(now * 128, 128), 128)
        fill_shared(kc, k_ref, kh_ref, r)
        fill_shared(vc, v_ref, vh_ref, r)
        bias = halo_bias(live_ref, (2 * r, 1), 0, r)

        def window(w, i, rows, keys, shared):
            data = (bias, q_ref, kc, vc) if shared else (None, q_ref, k_ref, v_ref)
            dq, dk, dv = window_back(w, rows, keys, *data, do_s[rows, lanes], lse_ref)
            buf_a[rows, lanes] = dq.astype(BF16)
            if shared:
                part = pl.ds(i * r, r)
                for n, v in enumerate((dk, dv)):
                    own[n, part, :] = v[:r, :]
                    hsend[n, part, :] = v[r:, :].astype(BF16)
            else:
                buf_b[rows, lanes] = dk.astype(BF16)
                buf_c[rows, lanes] = dv.astype(BF16)

        pairs = list(each_window(r, window))
        pairs[0]()
        swap(now).start()
        pairs[1]()
        pairs[2]()

    @pl.when(step >= plan.fin)
    def _():
        i = step - plan.fin
        pl.when(i == 0)(lambda: load(6).wait())
        part = pl.ds(pl.multiple_of(i * chunk, chunk), chunk)
        hh = dot(buf_a[part, :], w0[...], 1, 1) + dot(buf_b[part, :], wk_ref[...], 1, 1)
        for one in reds:
            one.tick(plan.fin + 2 * i + 1)
        hh = hh + dot(buf_c[part, :], wv_ref[...], 1, 1)
        n, rs = norm_stats(x_ref[...].astype(F32))
        add_sums(sums_a, i == 0, [col_sum(hh), col_sum(hh * n)])
        put_groups(h[part, :] + norm_back(hh, n, rs, mod_ref[1:2, :]), stage, gin_hbm, sem, i, 4)

    @pl.when(step == steps - 1)
    def _():
        rows = [sums_a[0:2, :], sums_m[0:4, :], jnp.zeros((2, d), F32)]
        sums_a[...] = jnp.concatenate(rows, axis=0)
        other = red.plain(sums_a, sums_got, hsem.at[3], hsem.at[4], 0)
        other.start()
        finish(reds, plan.end)
        other.wait()
        sums_ref[...] = sums_a[...] + sums_got[...]


def core(live, nm, gm, nmt, attt, ndt, w_up, w_down, wo, wq, wk, wv, middle, gw, ao, mod, q, k, v, lse, kh, vh, xw, like):
    t, d = nm.shape
    ff = w_up.shape[1]
    th = kh.shape[0]
    frames = like.shape[1]
    dp = lax.axis_size("dp")
    til = Tiling(ff, dp)
    n_ff, n_att = til.steps, d // 128
    plan = Plan(n_ff, n_att, til.early)
    rest = tuple(range(3, dp.bit_length() - 1))
    reds = [
        Reduce(dp, d, ((0, 1, 2, *rest), (1, 2, 0, *rest)), True),
        Reduce(dp, d, ((1, 2, 0, *rest), (2, 1, 0, *rest)), False),
    ]
    red = reds[0]

    def block_at(first, count):
        return lambda i: (jnp.clip(i - first, 0, count - 1), 0)

    def lane_at(i):
        return 0, jnp.clip(i - plan.att, 0, n_att - 1)

    post = pl.BlockSpec((t // 4, d), block_at(plan.post, 4))
    last = pl.BlockSpec((t // 4, d), block_at(plan.fin, 4), pipeline_mode=pl.Buffered(1))
    big, small = pl.BlockSpec((t, 128), lane_at), pl.BlockSpec((th, 128), lane_at)
    lse_spec = pl.BlockSpec((None, 6, 8, lse_lanes(t)), lambda i: (lane_at(i)[1], 0, 0, 0))
    if til.early:
        half = n_ff // 2
        w_down = w_down.reshape(half, PIECES, 2, til.width, d)

        def down_at(i):
            i = jnp.minimum(i, n_ff - 1)
            return lax.rem(i, half), 0, i // half, 0, 0

        down = pl.BlockSpec((None, PIECES, None, til.width, d), down_at)
        cube, down_tile = cube_shape(red, ff, d), (PIECES, 2, red.r, d)
    else:
        down = pl.BlockSpec((LANES, d), block_at(0, n_ff))
        cube, down_tile = (ff, d), (PIECES, til.width, d)
    smem = pl.BlockSpec(memory_space=pltpu.SMEM)
    full = pl.BlockSpec((8, d), lambda i: (0, 0))
    image, sums = jax.ShapeDtypeStruct(like.shape, BF16), jax.ShapeDtypeStruct((8, d), F32)
    share = jax.ShapeDtypeStruct((red.r, d), F32)
    act, act32 = pltpu.VMEM((t, d), BF16), pltpu.VMEM((t, d), F32)
    return pl.pallas_call(
        functools.partial(core_kernel, til, plan, reds),
        grid=(plan.steps,),
        in_specs=[smem] + [ANY] * 8 + [down, post, post, post, whole((6, d)), whole((d, d)), whole((d, d))]
        + [big] * 3 + [lse_spec] + [small] * 2 + [last],
        out_specs=[ANY, ANY, full] + [ANY] * 7,
        out_shape=[image, image, sums, jax.ShapeDtypeStruct(cube, BF16), jax.ShapeDtypeStruct((red.r, ff), F32)]
        + [jax.ShapeDtypeStruct((ff // d, red.r, d), F32), share, share, share, share],
        scratch_shapes=[
            act,
            act,
            act,
            pltpu.VMEM((d, t), BF16),
            act32,
            act32,
            act,
            pltpu.VMEM((d, d), BF16),
            pltpu.VMEM((2, d, LANES), BF16),
            pltpu.VMEM(down_tile, BF16),
            tile_scratch(red),
            pltpu.VMEM((2 * th, 128), BF16),
            pltpu.VMEM((2 * th, 128), BF16),
            pltpu.VMEM((2, th, 128), F32),
            pltpu.VMEM((2, th, 128), BF16),
            pltpu.VMEM((2, 2, th, 128), BF16),
            pltpu.SemaphoreType.DMA((5,)),
            pltpu.SemaphoreType.DMA((3, PIECES)),
            pltpu.SemaphoreType.DMA((7,)),
            pltpu.VMEM((4, frames, 4, 8, d), BF16),
            pltpu.SemaphoreType.DMA((4,)),
        ]
        + [pltpu.VMEM((8, d), F32)] * 3
        + reds[0].scratch()
        + reds[1].scratch(),
        compiler_params=params(limit=63 * 1024 * 1024, collective_id=1, has_side_effects=True),
        name="core",
        cost_estimate=pl.CostEstimate(
            flops=12 * t * d * (ff + d) + 3 * t * t * d, bytes_accessed=8 * d * ff + 60 * t * d, transcendentals=t * (ff + 3 * t)
        ),
    )(live, nm, gm, nmt, attt, ndt, w_up, wo, wq, w_down, middle, gw, ao, mod, wk, wv, q, k, v, lse, kh, vh, xw)


def results_kernel(n_grad, a_hbm, b_hbm, mod_ref, *refs):
    grads, (a_out, b_out, mod_out), flats = refs[:n_grad], refs[n_grad : n_grad + 3], refs[n_grad + 3 : 2 * n_grad + 3]
    held, sem = refs[-2:]
    loads, stores = [], []
    for n, (src, dst) in enumerate(((a_hbm, a_out), (b_hbm, b_out))):
        for f in range(src.shape[1]):
            loads.append(pltpu.make_async_copy(src.at[0, f], held.at[n, f], sem.at[0, n, f]))
            stores.append(pltpu.make_async_copy(held.at[n, f], dst.at[0, f], sem.at[1, n, f]))
    for c in loads:
        c.start()
    mod_out[0] = mod_ref[0:6, :]
    for src, dst in zip(grads, flats):
        rows, cols = src.shape
        wide = cols // 128
        for g in range(wide):
            dst[pl.ds(g, rows, stride=wide), :] = src[:, lanes_at(g, 128)]
    for load, store in zip(loads, stores):
        load.wait()
        store.start()
    for c in stores:
        c.wait()


def results(image_a, image_b, mod_sums, grads):
    grads = [g.reshape(-1, g.shape[-1]) for g in grads]
    vmem = pl.BlockSpec(memory_space=pltpu.VMEM)
    n = len(grads)
    out = pl.pallas_call(
        functools.partial(results_kernel, n),
        in_specs=[ANY, ANY] + [vmem] * (n + 1),
        out_specs=[ANY, ANY] + [vmem] * (n + 1),
        out_shape=[jax.ShapeDtypeStruct(image_a.shape, BF16)] * 2
        + [jax.ShapeDtypeStruct((1, 6, mod_sums.shape[1]), F32)]
        + [jax.ShapeDtypeStruct((g.size // 128, 128), F32) for g in grads],
        scratch_shapes=[
            pltpu.VMEM((2,) + image_a.shape[1:], BF16),
            pltpu.SemaphoreType.DMA((2, 2, image_a.shape[1])),
        ],
        compiler_params=params(),
        name="results",
        cost_estimate=pl.CostEstimate(flops=0, bytes_accessed=8 * image_a.size, transcendentals=0),
    )(image_a, image_b, mod_sums, *grads)
    return out[0], out[1], out[2], *(g.reshape(-1) for g in out[3:])


def on_device(
    block_input, modulation, band_live, w_query, w_key, w_value, w_out, w_up, w_down, cotangent
):
    assert lax.axis_size("band") == 2 and block_input.shape[2:4] == (16, 16)
    mod = modulation[0]
    xw, ndt, gw, gm, q, k, v, kh, vh = pre(block_input, cotangent, band_live, mod, w_query, w_key, w_value)
    attended, lse = attn_fwd(band_live, q, k, v, kh, vh)
    ao, middle, nm, nmt, attt = mid(band_live, attended, w_out, xw, mod)
    block_output, grad_input, mod_sums, _, g_up, g_down, g_out, g_query, g_key, g_value = core(
        band_live, nm, gm, nmt, attt, ndt, w_up, w_down, w_out, w_query, w_key, w_value,
        middle, gw, ao, mod, q, k, v, lse, kh, vh, xw, block_input,
    )
    return results(block_output, grad_input, mod_sums, (g_query, g_key, g_value, g_out, g_up, g_down))


def solution(mesh):
    return jax.shard_map(
        on_device,
        mesh=mesh,
        in_specs=(
            P("dp", None, "band", None, None),
            P("dp", None, None),
            P("dp", None),
            P(),
            P(),
            P(),
            P(),
            P(),
            P(),
            P("dp", None, "band", None, None),
        ),
        out_specs=(
            P("dp", None, "band", None, None),
            P("dp", None, "band", None, None),
            P("dp", None, None),
            P("dp"),
            P("dp"),
            P("dp"),
            P("dp"),
            P("dp"),
            P("dp"),
        ),
        check_vma=False,
    )
```
